32 devices in a mesh: dp: 2 (over x), rows: 4 (over y, core), cols: 4 (over z).
Axes of the slice: x: 2, y: 2, z: 4, core: 2. Of those that a mesh axis runs over, the one named last changes fastest.
Arguments:
- tokens: bfloat16 [768, 4096], P('cols', ('dp', 'rows')), may hold values from -6 to 6
- segment_ids: int32 [4096], P(('dp', 'rows')), may hold values from -1 to 256, as said below
- first_gain: float32 [768], P('cols'), may hold values from 0.5 to 1.5
- first_bias: float32 [768], P('cols'), may hold values from -3 to 3
- qkv_weight: bfloat16 [768, 2304], P('rows', 'cols'), may hold values from -2 to 2
- qv_bias: float32 [1536], P('cols'), may hold values from -3 to 3
- mix_weight: bfloat16 [768, 768], P('cols', 'rows'), may hold values from -0.875 to 0.875
- mix_bias: float32 [768], P('cols'), may hold values from -3 to 3
- second_gain: float32 [768], P('cols'), may hold values from 0.5 to 1.5
- second_bias: float32 [768], P('cols'), may hold values from -3 to 3
- up_weight: bfloat16 [768, 3072], P('rows', 'cols'), may hold values from -0.21875 to 0.21875
- up_bias: float32 [3072], P('cols'), may hold values from -3 to 3
- down_weight: bfloat16 [768, 3072], P('rows', 'cols'), may hold values from -0.109375 to 0.109375
- down_bias: float32 [768], P('cols'), may hold values from -3 to 3
- cotangent: bfloat16 [768, 4096], P('cols', ('dp', 'rows')), may hold values from -6 to 6
Outputs:
- output: bfloat16 [768, 4096], P('cols', ('dp', 'rows'))
- grad_tokens: float32 [768, 4096], P('cols', ('dp', 'rows'))
- grad_first_gain: float32 [768], P('cols')
- grad_first_bias: float32 [768], P('cols')
- grad_qkv_weight: float32 [768, 2304], P('rows', 'cols')
- grad_qv_bias: float32 [1536], P('cols')
- grad_mix_weight: float32 [768, 768], P('cols', 'rows')
- grad_mix_bias: float32 [768], P('cols')
- grad_second_gain: float32 [768], P('cols')
- grad_second_bias: float32 [768], P('cols')
- grad_up_weight: float32 [768, 3072], P('rows', 'cols')
- grad_up_bias: float32 [3072], P('cols')
- grad_down_weight: float32 [768, 3072], P('rows', 'cols')
- grad_down_bias: float32 [768], P('cols')
The draws below stay inside these ranges and needn't reach their ends.
Inputs may be any that keep to these rules, and one draw needn't show every extreme that they name: `segment_ids`: within each aligned block of 512 slots the live slots come first and carry segment numbers 0, 1, 2, ... that never fall; padding slots carry -1; each segment has at most 256 slots and some segment exactly 256; the first 256 slots of a block hold no second segment; between 128 and 512 slots of a block are live, some block is full and some block half full.
All inputs are finite; a program needn't handle non-finite values.
Results may differ from the reference program's by a relative error of at most 0.0085.
Values may be sent and summed in bfloat16 or wider, within the bound.
No kernel may reach another device: no remote copies, remote signals or barrier semaphores. Data moves between devices by JAX's collectives and lax.ppermute only.
A program may use at most 64 MiB of HBM per device.

```python
import math
import jax
import jax.numpy as jnp
from jax import lax

D = 768
H = 12
HD = 64
FF = 3072
TOK_DEV = 512
MAXLEN = 256
HG = 3
TOKENS = 4096
N_COLS = 4


def draw_segment_ids(key, part):
    groups = TOKENS // TOK_DEV
    key_used, key_full, key_half, key_breaks = jax.random.split(key, 4)
    used_count = jax.random.randint(key_used, (groups,), TOK_DEV // 4, TOK_DEV + 1)
    full_group = jax.random.randint(key_full, (), 0, groups)
    half_group = (full_group + 1 + jax.random.randint(key_half, (), 0, groups - 1)) % groups
    group_index = jnp.arange(groups)
    used_count = jnp.where(group_index == full_group, TOK_DEV, jnp.where(group_index == half_group, TOK_DEV // 2, used_count))
    position = jnp.arange(TOK_DEV)
    late = position[None, :] >= MAXLEN
    breaks = (jax.random.randint(key_breaks, (groups, TOK_DEV), 0, MAXLEN // 4 + 1) == 0) & late
    breaks = breaks | (group_index[:, None] == full_group) & late
    breaks = breaks | (position[None, :] % MAXLEN == 0)
    numbers = jnp.cumsum(breaks.astype(jnp.int32), axis=1) - 1
    numbers = jnp.where(position[None, :] < used_count[:, None], numbers, -1)
    return numbers.reshape(TOKENS).astype(jnp.int32)


def draw_qkv_weight(key, part):
    groups = H // HG
    key_base = jax.random.fold_in(key, 0)
    base = jax.random.normal(key_base, (D, groups, 3, HG, HD), jnp.float32) * D ** (-0.5)
    return jnp.clip(base, -2.0, 2.0).reshape(D, 3 * D).astype(jnp.bfloat16)


def block_scale(own_key, dims, cuts, low, high):
    gain, own = 1.0, jax.random.fold_in(own_key, 6)
    for axis_at, blocks in cuts:
        steps = jnp.exp(jax.random.uniform(jax.random.fold_in(own, axis_at), (blocks,), jnp.float32, low / len(cuts), high / len(cuts)))
        gain = gain * jnp.repeat(steps, dims[axis_at] // blocks).reshape([-1 if axis == axis_at else 1 for axis in range(len(dims))])
    return gain


def bell_draw(stream_key, dims, deviation, limit, pieces=(), held_as=jnp.bfloat16):
    loudness = block_scale(stream_key, dims, pieces, -0.22, 0.18) if pieces else 1.0
    entries = jax.random.normal(stream_key, dims, jnp.float32) * deviation * loudness
    return jnp.minimum(jnp.maximum(entries, -limit), limit).astype(held_as)


def setup_inputs(seed: int = 0) -> dict:
    splits = jax.random.split(jax.random.key(seed), 16)
    tokens = bell_draw(splits[0], (D, TOKENS), 1.0, 6.0, ((0, 4), (1, 8)))
    segment_ids = draw_segment_ids(jax.random.fold_in(splits[15], 71), 0)
    first_gain = jnp.clip(1.0 + 0.1 * jax.random.normal(splits[2], (D,), jnp.float32), 0.5, 1.5)
    first_bias = bell_draw(splits[3], (D,), 0.5, 3.0, ((0, 4),), jnp.float32)
    qkv_weight = draw_qkv_weight(jax.random.fold_in(splits[15], 71), 0)
    qv_bias = bell_draw(splits[5], (2 * D,), 0.5, 3.0, ((0, 4),), jnp.float32)
    mix_weight = bell_draw(splits[6], (D, D), (D // 16) ** -0.5, 0.875, ((0, 4), (1, 4)))
    mix_bias = bell_draw(splits[7], (D,), 0.5, 3.0, ((0, 4),), jnp.float32)
    second_gain = jnp.clip(1.0 + 0.1 * jax.random.normal(splits[8], (D,), jnp.float32), 0.5, 1.5)
    second_bias = bell_draw(splits[9], (D,), 0.5, 3.0, ((0, 4),), jnp.float32)
    up_weight = bell_draw(splits[10], (D, FF), D ** -0.5, 0.21875, ((0, 4), (1, 4)))
    up_bias = bell_draw(splits[11], (FF,), 0.5, 3.0, ((0, 4),), jnp.float32)
    down_weight = bell_draw(splits[12], (D, FF), FF ** -0.5, 0.109375, ((0, 4), (1, 4)))
    down_bias = bell_draw(splits[13], (D,), 0.5, 3.0, ((0, 4),), jnp.float32)
    cotangent = bell_draw(splits[14], (D, TOKENS), 1.0, 6.0, ((0, 4), (1, 8)))
    return {"tokens": tokens, "segment_ids": segment_ids, "first_gain": first_gain, "first_bias": first_bias, "qkv_weight": qkv_weight, "qv_bias": qv_bias, "mix_weight": mix_weight, "mix_bias": mix_bias, "second_gain": second_gain, "second_bias": second_bias, "up_weight": up_weight, "up_bias": up_bias, "down_weight": down_weight, "down_bias": down_bias, "cotangent": cotangent}


EPS = 1e-05
NEG = -1e+30
ROOT = 0.7978845608028654
CUBIC = 0.044715

def gelu_value(pre_act):
    inner_arg = ROOT * (pre_act + CUBIC * pre_act * pre_act * pre_act)
    return 0.5 * pre_act * (1.0 + jnp.tanh(inner_arg))

def gelu_slope(pre_act):
    inner_arg = ROOT * (pre_act + CUBIC * pre_act * pre_act * pre_act)
    tanh_val = jnp.tanh(inner_arg)
    return 0.5 * (1.0 + tanh_val) + 0.5 * pre_act * (1.0 - tanh_val * tanh_val) * ROOT * (1.0 + 3.0 * CUBIC * pre_act * pre_act)

def allowed_pairs(seg_rows, seg_keys, block_start):
    query_pos = block_start + jnp.arange(seg_rows.shape[0], dtype=jnp.int32)
    key_pos = jnp.arange(seg_keys.shape[0], dtype=jnp.int32)
    earlier = key_pos[None, :] < query_pos[:, None]
    same_seg = (seg_rows[:, None] == seg_keys[None, :]) & (seg_rows[:, None] >= 0)
    return earlier & same_seg | (key_pos[None, :] == query_pos[:, None])

def product(form, left, right):
    return jnp.einsum(form, left.astype(jnp.float32), right.astype(jnp.float32), precision=lax.Precision.HIGHEST)

def matmul(left, right):
    return jnp.dot(left, right, preferred_element_type=jnp.float32)

def attend(query_vecs, key_vecs, value_vecs, seg_ids):
    row_count, head_count, head_width = query_vecs.shape
    block_rows = min(512, row_count)
    block_count = row_count // block_rows
    score_scale = 1.0 / math.sqrt(head_width)

    def one_block(item):
        query_block, seg_block, block_start = item
        scores = product('qhd,khd->hqk', query_block, key_vecs) * score_scale
        allowed = allowed_pairs(seg_block, seg_ids, block_start)
        scores = jnp.where(allowed[None], scores, NEG)
        row_max = lax.optimization_barrier(jnp.max(scores, axis=-1, keepdims=True))
        log_total = row_max + jnp.log(lax.optimization_barrier(jnp.sum(jnp.exp(scores - row_max), axis=-1, keepdims=True)))
        attn_probs = jnp.exp(scores - log_total).astype(jnp.bfloat16)
        attended = product('hqk,khd->qhd', attn_probs, value_vecs).astype(jnp.bfloat16)
        return (attended, log_total[:, :, 0])
    starts = jnp.arange(block_count, dtype=jnp.int32) * block_rows
    attended, log_totals = lax.map(one_block, (query_vecs.reshape(block_count, block_rows, head_count, head_width), seg_ids.reshape(block_count, block_rows), starts))
    return (attended.reshape(row_count, head_count, head_width), log_totals)

def attend_back(query_vecs, key_vecs, value_vecs, attended, grad_att, seg_ids, log_totals):
    row_count, head_count, head_width = query_vecs.shape
    block_rows = min(512, row_count)
    block_count = row_count // block_rows
    score_scale = 1.0 / math.sqrt(head_width)
    deltas = lax.optimization_barrier(jnp.sum(grad_att.astype(jnp.float32) * attended.astype(jnp.float32), axis=-1))

    def one_block(carry, item):
        grad_keys, grad_values = carry
        query_block, grad_block, delta_block, seg_block, total_block, block_start = item
        scores = product('qhd,khd->hqk', query_block, key_vecs) * score_scale
        allowed = allowed_pairs(seg_block, seg_ids, block_start)
        scores = jnp.where(allowed[None], scores, NEG)
        attn_probs = jnp.exp(scores - total_block[:, :, None])
        rounded = attn_probs.astype(jnp.bfloat16)
        grad_values = grad_values + product('hqk,qhd->khd', rounded, grad_block)
        grad_probs = product('qhd,khd->hqk', grad_block, value_vecs)
        grad_scores = (attn_probs * (grad_probs - delta_block.T[:, :, None]) * score_scale).astype(jnp.bfloat16)
        grad_query = product('hqk,khd->qhd', grad_scores, key_vecs)
        grad_keys = grad_keys + product('hqk,qhd->khd', grad_scores, query_block)
        return ((grad_keys, grad_values), grad_query)
    starts = jnp.arange(block_count, dtype=jnp.int32) * block_rows
    empty = jnp.zeros(key_vecs.shape, jnp.float32)
    shape_blocks = (block_count, block_rows, head_count, head_width)
    (grad_keys, grad_values), grad_query = lax.scan(one_block, (empty, empty), (query_vecs.reshape(shape_blocks), grad_att.reshape(shape_blocks), deltas.reshape(block_count, block_rows, head_count), seg_ids.reshape(block_count, block_rows), log_totals, starts))
    return (grad_query.reshape(row_count, head_count, head_width), grad_keys, grad_values)

def norm_forward(values, norm_gain, norm_bias):
    row_mean = lax.optimization_barrier(jnp.mean(values, axis=-1, keepdims=True))
    row_var = lax.optimization_barrier(jnp.mean(values * values, axis=-1, keepdims=True)) - row_mean * row_mean
    inv_std = lax.rsqrt(row_var + EPS)
    normed = (values - row_mean) * inv_std
    return ((normed * norm_gain + norm_bias).astype(jnp.bfloat16), normed, inv_std)

def norm_back(grad_out, normed, inv_std, norm_gain):
    scaled = grad_out * norm_gain
    return inv_std * (scaled - lax.optimization_barrier(jnp.mean(scaled, axis=-1, keepdims=True)) - normed * lax.optimization_barrier(jnp.mean(scaled * normed, axis=-1, keepdims=True)))

def layer_group(tokens, seg_ids, cotangent, weights):
    first_gain, first_bias, qkv_weight, qv_bias, mix_weight, mix_bias, second_gain, second_bias, up_weight, up_bias, down_weight, down_bias = weights
    row_count = tokens.shape[0]
    inputs = tokens.astype(jnp.float32)
    normed_one, hat_one, inv_one = norm_forward(inputs, first_gain, first_bias)
    projected = matmul(normed_one, qkv_weight).reshape(row_count, N_COLS, 3, HG, HD)
    bias_parts = qv_bias.reshape(N_COLS, 2, HG, HD)
    query_vecs = (projected[:, :, 0] + bias_parts[:, 0]).reshape(row_count, H, HD).astype(jnp.bfloat16)
    key_vecs = projected[:, :, 1].reshape(row_count, H, HD).astype(jnp.bfloat16)
    value_vecs = (projected[:, :, 2] + bias_parts[:, 1]).reshape(row_count, H, HD).astype(jnp.bfloat16)
    attended, log_totals = attend(query_vecs, key_vecs, value_vecs, seg_ids)
    attended_flat = attended.reshape(row_count, D)
    hidden = inputs + matmul(attended_flat, mix_weight) + mix_bias
    normed_two, hat_two, inv_two = norm_forward(hidden, second_gain, second_bias)
    pre_act = matmul(normed_two, up_weight) + up_bias
    active = gelu_value(pre_act).astype(jnp.bfloat16)
    final_sum = hidden + matmul(active, down_weight) + down_bias
    output = final_sum.astype(jnp.bfloat16)
    live_mask = (seg_ids >= 0).astype(jnp.float32)
    grad_final = cotangent.astype(jnp.float32) * live_mask[:, None]
    grad_final_b = grad_final.astype(jnp.bfloat16)
    grad_down = matmul(active.T, grad_final_b)
    grad_down_b = lax.optimization_barrier(jnp.sum(grad_final, axis=0))
    grad_pre = (matmul(grad_final_b, down_weight.T) * gelu_slope(pre_act)).astype(jnp.bfloat16)
    grad_up = matmul(normed_two.T, grad_pre)
    grad_up_b = lax.optimization_barrier(jnp.sum(grad_pre.astype(jnp.float32), axis=0))
    grad_second_in = matmul(grad_pre, up_weight.T)
    grad_second_gain = lax.optimization_barrier(jnp.sum(grad_second_in * hat_two, axis=0))
    grad_second_bias = lax.optimization_barrier(jnp.sum(grad_second_in, axis=0))
    grad_hidden = grad_final + norm_back(grad_second_in, hat_two, inv_two, second_gain)
    grad_hidden_b = grad_hidden.astype(jnp.bfloat16)
    grad_mix = matmul(attended_flat.T, grad_hidden_b)
    grad_mix_b = lax.optimization_barrier(jnp.sum(grad_hidden, axis=0))
    grad_att = matmul(grad_hidden_b, mix_weight.T).astype(jnp.bfloat16).reshape(row_count, H, HD)
    grad_query, grad_keys, grad_values = attend_back(query_vecs, key_vecs, value_vecs, attended, grad_att, seg_ids, log_totals)
    group_shape = (row_count, N_COLS, HG, HD)
    grad_qv = jnp.stack([lax.optimization_barrier(jnp.sum(grad_query, axis=0)).reshape(N_COLS, HG, HD), lax.optimization_barrier(jnp.sum(grad_values, axis=0)).reshape(N_COLS, HG, HD)], axis=1).reshape(2 * D)
    grad_projected = jnp.stack([grad_query.reshape(group_shape), grad_keys.reshape(group_shape), grad_values.reshape(group_shape)], axis=2).reshape(row_count, 3 * D).astype(jnp.bfloat16)
    grad_qkv = matmul(normed_one.T, grad_projected)
    grad_first_in = matmul(grad_projected, qkv_weight.T)
    grad_first_gain = lax.optimization_barrier(jnp.sum(grad_first_in * hat_one, axis=0))
    grad_first_bias = lax.optimization_barrier(jnp.sum(grad_first_in, axis=0))
    grad_tokens = grad_hidden + norm_back(grad_first_in, hat_one, inv_one, first_gain)
    grads = (grad_first_gain, grad_first_bias, grad_qkv, grad_qv, grad_mix, grad_mix_b, grad_second_gain, grad_second_bias, grad_up, grad_up_b, grad_down, grad_down_b)
    return (output, grad_tokens, grads)

def reference(tokens, segment_ids, first_gain, first_bias, qkv_weight, qv_bias, mix_weight, mix_bias, second_gain, second_bias, up_weight, up_bias, down_weight, down_bias, cotangent):
    groups = tokens.shape[1] // TOK_DEV
    weights = (first_gain, first_bias, qkv_weight, qv_bias, mix_weight, mix_bias, second_gain, second_bias, up_weight, up_bias, down_weight.T, down_bias)
    zeros = tuple((jnp.zeros(param.shape, jnp.float32) for param in weights))

    def one_group(carry, item):
        token_block, seg_block, grad_block = item
        output, grad_tokens, grads = layer_group(token_block, seg_block, grad_block, weights)
        return (tuple((acc + part for acc, part in zip(carry, grads))), (output, grad_tokens))
    token_rows = tokens.T.reshape(groups, TOK_DEV, D)
    grad_in = cotangent.T.reshape(groups, TOK_DEV, D)
    totals, (outputs, grad_rows) = lax.scan(one_group, zeros, (token_rows, segment_ids.reshape(groups, TOK_DEV), grad_in))
    return (outputs.reshape(groups * TOK_DEV, D).T, grad_rows.reshape(groups * TOK_DEV, D).T, totals[0], totals[1], totals[2], totals[3], totals[4], totals[5], totals[6], totals[7], totals[8], totals[9], totals[10].T, totals[11])
```

```python
import functools
import math

import jax
import jax.numpy as jnp
from jax import lax
from jax.experimental import pallas as pl
from jax.experimental.pallas import tpu as pltpu
from jax.sharding import PartitionSpec as P

HD = 64
MAXLEN = 256
EPS = 1e-05
NEG = -1e30
ROOT = 0.7978845608028654
CUBIC = 0.044715
F32 = jnp.float32
BF16 = jnp.bfloat16


def dot(left, right, dims):
    return lax.dot_general(left, right, (dims, ((), ())), preferred_element_type=F32)


def mm(left, right):
    return dot(left, right, ((1,), (0,)))


def mm_t(left, right):
    return dot(left, right, ((0,), (0,)))


def mm_nt(left, right):
    return dot(left, right, ((1,), (1,)))


def gelu_both(pre_act):
    inner_arg = ROOT * (pre_act + CUBIC * pre_act * pre_act * pre_act)
    tanh_val = jnp.tanh(inner_arg)
    value = 0.5 * pre_act * (1.0 + tanh_val)
    slope = 0.5 * (1.0 + tanh_val) + 0.5 * pre_act * (1.0 - tanh_val * tanh_val) * ROOT * (
        1.0 + 3.0 * CUBIC * pre_act * pre_act
    )
    return value, slope


def allowed_mask(seg_row, seg_col, width):
    key_pos = lax.broadcasted_iota(jnp.int32, (width, width), 0)
    query_pos = lax.broadcasted_iota(jnp.int32, (width, width), 1)
    same_seg = (seg_col == seg_row) & (seg_row >= 0)
    return (key_pos < query_pos) & same_seg | (key_pos == query_pos)


def attend_kernel(width, heads, qkv_ref, bias_ref, row_ref, col_ref, qkv_out, att_out, total_out):
    head_rows = heads * HD
    biased = qkv_ref[...] + bias_ref[...]
    qkv_out[...] = biased.astype(BF16)
    scale = 1.0 / math.sqrt(HD)
    for half in range(qkv_ref.shape[1] // width):
        cols = pl.ds(half * width, width)
        allowed = allowed_mask(row_ref[:, cols], col_ref[cols, :], width)
        for head in range(heads):
            query = qkv_out[pl.ds(head * HD, HD), cols]
            keys = qkv_out[pl.ds(head_rows + head * HD, HD), cols]
            values = qkv_out[pl.ds(2 * head_rows + head * HD, HD), cols]
            scores = jnp.where(allowed, mm_t(keys, query) * scale, NEG)
            top = jnp.max(scores, axis=0, keepdims=True)
            log_total = top + jnp.log(jnp.sum(jnp.exp(scores - top), axis=0, keepdims=True))
            probs = jnp.exp(scores - log_total).astype(BF16)
            att_out[pl.ds(head * HD, HD), cols] = mm(values, probs).astype(BF16)
            total_out[pl.ds(head, 1), cols] = log_total


def attend(projected, bias_col, seg_row, seg_col, heads):
    rows, tokens = projected.shape
    width = min(MAXLEN, tokens)
    return pl.pallas_call(
        functools.partial(attend_kernel, width, heads),
        out_shape=(
            jax.ShapeDtypeStruct((rows, tokens), BF16),
            jax.ShapeDtypeStruct((heads * HD, tokens), BF16),
            jax.ShapeDtypeStruct((heads, tokens), F32),
        ),
        name="attend",
    )(projected, bias_col, seg_row, seg_col)


def attend_back_kernel(
    width, heads, qkv_ref, att_ref, grad_ref, total_ref, row_ref, col_ref, out_ref, sums_ref
):
    head_rows = heads * HD
    scale = 1.0 / math.sqrt(HD)
    for head in range(heads):
        sum_query = jnp.zeros((HD, 1), F32)
        sum_value = jnp.zeros((HD, 1), F32)
        for half in range(qkv_ref.shape[1] // width):
            cols = pl.ds(half * width, width)
            allowed = allowed_mask(row_ref[:, cols], col_ref[cols, :], width)
            query = qkv_ref[pl.ds(head * HD, HD), cols]
            keys = qkv_ref[pl.ds(head_rows + head * HD, HD), cols]
            values = qkv_ref[pl.ds(2 * head_rows + head * HD, HD), cols]
            grad = grad_ref[pl.ds(head * HD, HD), cols]
            attended = att_ref[pl.ds(head * HD, HD), cols]
            delta = jnp.sum(grad.astype(F32) * attended.astype(F32), axis=0, keepdims=True)
            scores = jnp.where(allowed, mm_t(keys, query) * scale, NEG)
            probs = jnp.exp(scores - total_ref[pl.ds(head, 1), cols])
            grad_values = mm_nt(grad, probs.astype(BF16))
            grad_probs = mm_t(values, grad)
            grad_scores = (probs * (grad_probs - delta) * scale).astype(BF16)
            grad_query = mm(keys, grad_scores)
            grad_keys = mm_nt(query, grad_scores)
            out_ref[pl.ds(head * HD, HD), cols] = grad_query.astype(BF16)
            out_ref[pl.ds(head_rows + head * HD, HD), cols] = grad_keys.astype(BF16)
            out_ref[pl.ds(2 * head_rows + head * HD, HD), cols] = grad_values.astype(BF16)
            sum_query += jnp.sum(grad_query, axis=1, keepdims=True)
            sum_value += jnp.sum(grad_values, axis=1, keepdims=True)
        sums_ref[pl.ds(head * HD, HD), :] = sum_query
        sums_ref[pl.ds(head_rows + head * HD, HD), :] = sum_value


def attend_back(qkv, attended, grad_att, totals, seg_row, seg_col, heads):
    rows, tokens = qkv.shape
    width = min(MAXLEN, tokens)
    return pl.pallas_call(
        functools.partial(attend_back_kernel, width, heads),
        out_shape=(
            jax.ShapeDtypeStruct((rows, tokens), BF16),
            jax.ShapeDtypeStruct((2 * heads * HD, 1), F32),
        ),
        name="attend_back",
    )(qkv, attended, grad_att, totals, seg_row, seg_col)


def bits_of(size):
    bits, bit = [], 1
    while bit < size:
        bits.append(bit)
        bit *= 2
    return bits


def swap(values, axis, size, bit):
    return lax.ppermute(values, axis, [(at, at ^ bit) for at in range(size)])


def shift(values, axis, size, step):
    return lax.ppermute(values, axis, [(at, (at + step) % size) for at in range(size)])


def whole_sum(values, axis_sizes):
    for axis, size in axis_sizes:
        for bit in bits_of(size):
            values = values + swap(values, axis, size, bit)
    return values


def put(target, piece, start, axis):
    return lax.dynamic_update_slice_in_dim(target, piece, start, axis)


def take(source, start, length, axis):
    return lax.dynamic_slice_in_dim(source, start, length, axis)


def make_body(n_dp, n_rows, n_cols):
    row_bits = bits_of(n_rows)[::-1]
    order = [0]
    for bit in row_bits:
        order = order + [value ^ bit for value in order]

    def body(
        tokens,
        segment_ids,
        first_gain,
        first_bias,
        qkv_weight,
        qv_bias,
        mix_weight,
        mix_bias,
        second_gain,
        second_bias,
        up_weight,
        up_bias,
        down_weight,
        down_bias,
        cotangent,
    ):
        feat, count = tokens.shape
        width = feat * n_cols
        part = count // n_cols
        heads = qkv_weight.shape[1] // (3 * HD)
        at_row = lax.axis_index("rows")
        at_col = lax.axis_index("cols")
        places = jnp.array([order.index(value) for value in range(n_rows)], jnp.int32)

        def place(block):
            return places[at_row ^ block]

        def col_of(step):
            return (at_col + step) % n_cols

        def to_rel(values):
            pieces = [take(values, (at_row ^ value) * feat, feat, 0) for value in order]
            return jnp.concatenate(pieces, axis=0)

        def to_nat(values):
            pieces = [take(values, place(block) * feat, feat, 0) for block in range(n_rows)]
            return jnp.concatenate(pieces, axis=0)

        def rows_whole(shard):
            for bit in row_bits:
                shard = jnp.concatenate([shard, swap(shard, "rows", n_rows, bit)], axis=0)
            return shard

        def rows_reduce(grad):
            for bit in row_bits[::-1]:
                half = grad.shape[0] // 2
                sent = swap(grad[half:].astype(BF16), "rows", n_rows, bit)
                grad = grad[:half] + sent.astype(F32)
            for bit in bits_of(n_dp):
                grad = grad + swap(grad.astype(BF16), "dp", n_dp, bit).astype(F32)
            return grad

        def col_blocks(own, start_of):
            whole = jnp.zeros((own.shape[0] * n_cols,) + own.shape[1:], own.dtype)
            whole = put(whole, own, start_of(at_col), 0)
            for step in range(1, n_cols):
                whole = put(whole, shift(own, "cols", n_cols, step), start_of(col_of(-step)), 0)
            return whole

        def col_exchange(piece_for):
            got = [(piece_for(at_col), at_col)]
            for step in range(1, n_cols):
                got.append((shift(piece_for(col_of(step)), "cols", n_cols, step), col_of(-step)))
            return got

        tok_whole = lax.all_gather(tokens, "cols", axis=0, tiled=True)
        qkv_rel = rows_whole(qkv_weight)
        mix_cols = col_blocks(mix_weight, lambda col: col * feat)
        mix_rel = rows_whole(mix_cols.T)
        up_rel = rows_whole(up_weight)
        down_rel = rows_whole(down_weight)
        cot_rel = col_blocks(cotangent, lambda col: place(col) * feat)

        seg_row = segment_ids.reshape(1, count)
        seg_col = segment_ids.reshape(count, 1)
        live = seg_row >= 0

        norms = jnp.stack([first_gain, first_bias, mix_bias, second_gain, second_bias], axis=1)
        norms = to_rel(lax.all_gather(norms, "cols", axis=0, tiled=True))
        gain_one, bias_one, bias_mix, gain_two, bias_two = [norms[:, k : k + 1] for k in range(5)]

        inputs = to_rel(tok_whole).astype(F32)
        mean_one = jnp.mean(inputs, axis=0, keepdims=True)
        inv_one = lax.rsqrt(jnp.mean(inputs * inputs, axis=0, keepdims=True) - mean_one * mean_one + EPS)
        hat_one = (inputs - mean_one) * inv_one
        normed_one = (hat_one * gain_one + bias_one).astype(BF16)
        projected = mm_t(qkv_rel, normed_one)
        head_rows = heads * HD
        bias_col = jnp.concatenate(
            [qv_bias[:head_rows], jnp.zeros((head_rows,), F32), qv_bias[head_rows:]]
        ).reshape(3 * head_rows, 1)
        qkv, attended, totals = attend(projected, bias_col, seg_row, seg_col, heads)

        att_whole = lax.all_gather(attended, "cols", axis=0, tiled=True)
        hidden = inputs + mm(mix_rel, att_whole) + bias_mix
        mean_two = jnp.mean(hidden, axis=0, keepdims=True)
        inv_two = lax.rsqrt(jnp.mean(hidden * hidden, axis=0, keepdims=True) - mean_two * mean_two + EPS)
        hat_two = (hidden - mean_two) * inv_two
        normed_two = (hat_two * gain_two + bias_two).astype(BF16)

        pre_act = mm_t(up_rel, normed_two) + up_bias[:, None]
        value, slope = gelu_both(pre_act)
        active = value.astype(BF16)
        grad_final_b = jnp.where(live, cot_rel, jnp.zeros_like(cot_rel))
        grad_pre = (mm_t(down_rel, grad_final_b) * slope).astype(BF16)
        part_two = mm(up_rel, grad_pre).astype(BF16)
        got = col_exchange(lambda col: take(part_two, col * part, part, 1))
        grad_two = sum(piece.astype(F32) for piece, _ in got)

        grad_down = rows_reduce(mm_nt(grad_final_b, active))
        grad_up = rows_reduce(mm_nt(normed_two, grad_pre))

        part_out = mm(down_rel, active).astype(BF16)
        got = col_exchange(lambda col: take(part_out, place(col) * feat, feat, 0))
        own_hidden = take(hidden, place(at_col) * feat, feat, 0)
        output = own_hidden + down_bias[:, None] + sum(piece.astype(F32) for piece, _ in got)

        own_at = at_col * part
        own_hat = (take(hidden, own_at, part, 1) - take(mean_two, own_at, part, 1)) * take(
            inv_two, own_at, part, 1
        )
        scaled = grad_two * gain_two
        grad_hidden = take(grad_final_b, own_at, part, 1).astype(F32) + take(inv_two, own_at, part, 1) * (
            scaled
            - jnp.mean(scaled, axis=0, keepdims=True)
            - own_hat * jnp.mean(scaled * own_hat, axis=0, keepdims=True)
        )
        grad_hidden_b = grad_hidden.astype(BF16)
        grad_att_all = mm_t(mix_rel, grad_hidden_b).astype(BF16)
        got = col_exchange(lambda col: take(grad_att_all, col * feat, feat, 0))
        grad_att = jnp.zeros((feat, count), BF16)
        for piece, col in got:
            grad_att = put(grad_att, piece, col * part, 1)
        got = col_exchange(lambda col: grad_hidden_b)
        grad_hidden_all = jnp.zeros((width, count), BF16)
        for piece, col in got:
            grad_hidden_all = put(grad_hidden_all, piece, col * part, 1)

        grad_proj, qv_sums = attend_back(qkv, attended, grad_att, totals, seg_row, seg_col, heads)
        grad_one_part = mm(qkv_rel, grad_proj)
        grad_qkv = rows_reduce(mm_nt(normed_one, grad_proj))
        grad_mix = rows_reduce(mm_nt(grad_hidden_all, attended))

        scaled = grad_one_part * gain_one
        stats = jnp.concatenate(
            [
                jnp.sum(scaled, axis=0, keepdims=True),
                jnp.sum(scaled * hat_one, axis=0, keepdims=True),
            ],
            axis=0,
        )
        stats = whole_sum(stats, [("cols", n_cols)]) / width
        grad_one_b = grad_one_part.astype(BF16)
        got = col_exchange(lambda col: take(grad_one_b, place(col) * feat, feat, 0))
        grad_one = sum(piece.astype(F32) for piece, _ in got)
        own_place = place(at_col) * feat
        hat_own = (tokens.astype(F32) - mean_one) * inv_one
        grad_tokens = take(grad_hidden_all, own_place, feat, 0).astype(F32) + inv_one * (
            grad_one * first_gain[:, None] - stats[:1] - hat_own * stats[1:]
        )

        token_sums = jnp.stack(
            [
                jnp.sum(grad_two * own_hat, axis=1),
                jnp.sum(grad_two, axis=1),
                jnp.sum(grad_hidden, axis=1),
            ],
            axis=1,
        )
        token_sums = whole_sum(to_nat(token_sums), [("cols", n_cols)])
        token_sums = take(token_sums, at_col * feat, feat, 0)
        own_final = jnp.where(live, cotangent.astype(F32), 0.0)
        early = jnp.concatenate(
            [
                token_sums.T.reshape(-1),
                jnp.sum(own_final, axis=1),
                jnp.sum(grad_pre.astype(F32), axis=1),
            ]
        )
        late = jnp.concatenate(
            [qv_sums.reshape(-1), jnp.sum(grad_one * hat_own, axis=1), jnp.sum(grad_one, axis=1)]
        )
        axes = [("rows", n_rows), ("dp", n_dp)]
        early = whole_sum(early, axes)
        late = whole_sum(late, axes)
        n_qv = 2 * head_rows
        return (
            output.astype(BF16),
            grad_tokens,
            late[n_qv : n_qv + feat],
            late[n_qv + feat :],
            grad_qkv,
            late[:n_qv],
            grad_mix.T,
            early[2 * feat : 3 * feat],
            early[:feat],
            early[feat : 2 * feat],
            grad_up,
            early[4 * feat :],
            grad_down,
            early[3 * feat : 4 * feat],
        )

    return body


def solution(mesh):
    sizes = mesh.shape
    return jax.shard_map(
        make_body(sizes["dp"], sizes["rows"], sizes["cols"]),
        mesh=mesh,
        in_specs=(
            P("cols", ("dp", "rows")),
            P(("dp", "rows")),
            P("cols"),
            P("cols"),
            P("rows", "cols"),
            P("cols"),
            P("cols", "rows"),
            P("cols"),
            P("cols"),
            P("cols"),
            P("rows", "cols"),
            P("cols"),
            P("rows", "cols"),
            P("cols"),
            P("cols", ("dp", "rows")),
        ),
        out_specs=(
            P("cols", ("dp", "rows")),
            P("cols", ("dp", "rows")),
            P("cols"),
            P("cols"),
            P("rows", "cols"),
            P("cols"),
            P("cols", "rows"),
            P("cols"),
            P("cols"),
            P("cols"),
            P("rows", "cols"),
            P("cols"),
            P("rows", "cols"),
            P("cols"),
        ),
        check_vma=False,
    )
```

```python
import functools
import math

import jax
import jax.numpy as jnp
from jax import lax
from jax.experimental import pallas as pl
from jax.experimental.pallas import tpu as pltpu
from jax.sharding import PartitionSpec as P

HD = 64
MAXLEN = 256
EPS = 1e-05
NEG = -1e30
ROOT = 0.7978845608028654
CUBIC = 0.044715
F32 = jnp.float32
BF16 = jnp.bfloat16


def dot(left, right, dims):
    return lax.dot_general(left, right, (dims, ((), ())), preferred_element_type=F32)


def mm(left, right):
    return dot(left, right, ((1,), (0,)))


def mm_t(left, right):
    return dot(left, right, ((0,), (0,)))


def mm_nt(left, right):
    return dot(left, right, ((1,), (1,)))


def gelu_both(pre_act):
    inner_arg = ROOT * (pre_act + CUBIC * pre_act * pre_act * pre_act)
    tanh_val = jnp.tanh(inner_arg)
    value = 0.5 * pre_act * (1.0 + tanh_val)
    slope = 0.5 * (1.0 + tanh_val) + 0.5 * pre_act * (1.0 - tanh_val * tanh_val) * ROOT * (
        1.0 + 3.0 * CUBIC * pre_act * pre_act
    )
    return value, slope


def allowed_mask(seg_row, seg_col, width):
    key_pos = lax.broadcasted_iota(jnp.int32, (width, width), 0)
    query_pos = lax.broadcasted_iota(jnp.int32, (width, width), 1)
    same_seg = (seg_col == seg_row) & (seg_row >= 0)
    return (key_pos < query_pos) & same_seg | (key_pos == query_pos)


def attend_kernel(width, heads, qkv_ref, bias_ref, row_ref, col_ref, qkv_out, att_out, total_out):
    head_rows = heads * HD
    biased = qkv_ref[...] + bias_ref[...]
    qkv_out[...] = biased.astype(BF16)
    scale = 1.0 / math.sqrt(HD)
    for half in range(qkv_ref.shape[1] // width):
        cols = pl.ds(half * width, width)
        allowed = allowed_mask(row_ref[:, cols], col_ref[cols, :], width)
        for head in range(heads):
            query = qkv_out[pl.ds(head * HD, HD), cols]
            keys = qkv_out[pl.ds(head_rows + head * HD, HD), cols]
            values = qkv_out[pl.ds(2 * head_rows + head * HD, HD), cols]
            scores = jnp.where(allowed, mm_t(keys, query) * scale, NEG)
            top = jnp.max(scores, axis=0, keepdims=True)
            log_total = top + jnp.log(jnp.sum(jnp.exp(scores - top), axis=0, keepdims=True))
            probs = jnp.exp(scores - log_total).astype(BF16)
            att_out[pl.ds(head * HD, HD), cols] = mm(values, probs).astype(BF16)
            total_out[pl.ds(head, 1), cols] = log_total


def attend(projected, bias_col, seg_row, seg_col, heads):
    rows, tokens = projected.shape
    width = min(MAXLEN, tokens)
    return pl.pallas_call(
        functools.partial(attend_kernel, width, heads),
        out_shape=(
            jax.ShapeDtypeStruct((rows, tokens), BF16),
            jax.ShapeDtypeStruct((heads * HD, tokens), BF16),
            jax.ShapeDtypeStruct((heads, tokens), F32),
        ),
        name="attend",
    )(projected, bias_col, seg_row, seg_col)


def attend_back_kernel(
    width, heads, qkv_ref, att_ref, grad_ref, total_ref, row_ref, col_ref, out_ref, sums_ref
):
    head_rows = heads * HD
    scale = 1.0 / math.sqrt(HD)
    for head in range(heads):
        sum_query = jnp.zeros((HD, 1), F32)
        sum_value = jnp.zeros((HD, 1), F32)
        for half in range(qkv_ref.shape[1] // width):
            cols = pl.ds(half * width, width)
            allowed = allowed_mask(row_ref[:, cols], col_ref[cols, :], width)
            query = qkv_ref[pl.ds(head * HD, HD), cols]
            keys = qkv_ref[pl.ds(head_rows + head * HD, HD), cols]
            values = qkv_ref[pl.ds(2 * head_rows + head * HD, HD), cols]
            grad = grad_ref[pl.ds(head * HD, HD), cols]
            attended = att_ref[pl.ds(head * HD, HD), cols]
            delta = jnp.sum(grad.astype(F32) * attended.astype(F32), axis=0, keepdims=True)
            scores = jnp.where(allowed, mm_t(keys, query) * scale, NEG)
            probs = jnp.exp(scores - total_ref[pl.ds(head, 1), cols])
            grad_values = mm_nt(grad, probs.astype(BF16))
            grad_probs = mm_t(values, grad)
            grad_scores = (probs * (grad_probs - delta) * scale).astype(BF16)
            grad_query = mm(keys, grad_scores)
            grad_keys = mm_nt(query, grad_scores)
            out_ref[pl.ds(head * HD, HD), cols] = grad_query.astype(BF16)
            out_ref[pl.ds(head_rows + head * HD, HD), cols] = grad_keys.astype(BF16)
            out_ref[pl.ds(2 * head_rows + head * HD, HD), cols] = grad_values.astype(BF16)
            sum_query += jnp.sum(grad_query, axis=1, keepdims=True)
            sum_value += jnp.sum(grad_values, axis=1, keepdims=True)
        sums_ref[pl.ds(head * HD, HD), :] = sum_query
        sums_ref[pl.ds(head_rows + head * HD, HD), :] = sum_value


def attend_back(qkv, attended, grad_att, totals, seg_row, seg_col, heads):
    rows, tokens = qkv.shape
    width = min(MAXLEN, tokens)
    return pl.pallas_call(
        functools.partial(attend_back_kernel, width, heads),
        out_shape=(
            jax.ShapeDtypeStruct((rows, tokens), BF16),
            jax.ShapeDtypeStruct((2 * heads * HD, 1), F32),
        ),
        name="attend_back",
    )(qkv, attended, grad_att, totals, seg_row, seg_col)


def bits_of(size):
    bits, bit = [], 1
    while bit < size:
        bits.append(bit)
        bit *= 2
    return bits


def swap(values, axis, size, bit):
    return lax.ppermute(values, axis, [(at, at ^ bit) for at in range(size)])


def shift(values, axis, size, step):
    return lax.ppermute(values, axis, [(at, (at + step) % size) for at in range(size)])


def whole_sum(values, axis_sizes):
    for axis, size in axis_sizes:
        for bit in bits_of(size):
            values = values + swap(values, axis, size, bit)
    return values


def put(target, piece, start, axis):
    return lax.dynamic_update_slice_in_dim(target, piece, start, axis)


def take(source, start, length, axis):
    return lax.dynamic_slice_in_dim(source, start, length, axis)


def make_body(n_dp, n_rows, n_cols):
    row_bits = bits_of(n_rows)[::-1]
    order = [0]
    for bit in row_bits:
        order = order + [value ^ bit for value in order]

    def body(
        tokens,
        segment_ids,
        first_gain,
        first_bias,
        qkv_weight,
        qv_bias,
        mix_weight,
        mix_bias,
        second_gain,
        second_bias,
        up_weight,
        up_bias,
        down_weight,
        down_bias,
        cotangent,
    ):
        feat, count = tokens.shape
        width = feat * n_cols
        part = count // n_cols
        heads = qkv_weight.shape[1] // (3 * HD)
        at_row = lax.axis_index("rows")
        at_col = lax.axis_index("cols")
        places = jnp.array([order.index(value) for value in range(n_rows)], jnp.int32)

        def place(block):
            return places[at_row ^ block]

        def col_of(step):
            return (at_col + step) % n_cols

        def to_rel(values):
            pieces = [take(values, (at_row ^ value) * feat, feat, 0) for value in order]
            return jnp.concatenate(pieces, axis=0)

        def to_nat(values):
            pieces = [take(values, place(block) * feat, feat, 0) for block in range(n_rows)]
            return jnp.concatenate(pieces, axis=0)

        def col_blocks(own, start_of):
            whole = jnp.zeros((own.shape[0] * n_cols,) + own.shape[1:], own.dtype)
            whole = put(whole, own, start_of(at_col), 0)
            for step in range(1, n_cols):
                whole = put(whole, shift(own, "cols", n_cols, step), start_of(col_of(-step)), 0)
            return whole

        def col_exchange(piece_for):
            got = [(piece_for(at_col), at_col)]
            for step in range(1, n_cols):
                got.append((shift(piece_for(col_of(step)), "cols", n_cols, step), col_of(-step)))
            return got

        def col_halving(piece_for):
            bits = bits_of(n_cols)
            held = [at_col ^ value for value in range(n_cols)]
            held = [piece_for(col) for col in held]
            for bit in bits:
                keep = [held[at] for at in range(len(held)) if not at & 1]
                give = [held[at] for at in range(len(held)) if at & 1]
                got = swap(jnp.concatenate(give, axis=0).astype(BF16), "cols", n_cols, bit)
                got = jnp.split(got, len(give), axis=0)
                held = [mine.astype(F32) + theirs.astype(F32) for mine, theirs in zip(keep, got)]
            return held[0]

        def after(value, *others):
            return lax.optimization_barrier((value,) + others)[0]

        def split_three(values):
            high = lax.reduce_precision(values, 8, 7)
            middle = lax.reduce_precision(values - high, 8, 7)
            low = values - high - middle
            return [part_of.astype(BF16) for part_of in (high, middle, low)]

        n_qkv = qkv_weight.shape[1]
        n_hid = up_weight.shape[1]
        pair = jnp.concatenate([up_weight, down_weight], axis=1)
        if n_rows > 1:
            qkv_half = jnp.concatenate([qkv_weight, swap(qkv_weight, "rows", n_rows, row_bits[0])], axis=0)
            pair_half = jnp.concatenate([pair, swap(pair, "rows", n_rows, row_bits[0])], axis=0)
        norms = jnp.stack([first_gain, first_bias, mix_bias, second_gain, second_bias], axis=1)
        norms = jnp.concatenate(split_three(norms), axis=1)
        tok_whole = lax.all_gather(tokens, "cols", axis=0, tiled=True)
        packed = after(jnp.concatenate([mix_weight, norms], axis=1), tok_whole)
        packed = lax.all_gather(packed, "cols", axis=0, tiled=True)
        mix_cols = packed[:, :feat].T
        norms = packed[:, feat:].astype(F32)
        n_norm = norms.shape[1] // 3
        norms = to_rel(norms[:, :n_norm] + norms[:, n_norm : 2 * n_norm] + norms[:, 2 * n_norm :])
        gain_one, bias_one, bias_mix, gain_two, bias_two = [norms[:, k : k + 1] for k in range(n_norm)]

        def rest_whole(half, bits):
            for bit in bits:
                half = jnp.concatenate([half, swap(half, "rows", n_rows, bit)], axis=0)
            return half

        qkv_rel = rest_whole(qkv_half, row_bits[1:])
        mix_half = jnp.concatenate([mix_cols, swap(mix_cols, "rows", n_rows, row_bits[0])], axis=0)
        cot_rel = col_blocks(after(cotangent, packed), lambda col: place(col) * feat)

        seg_row = segment_ids.reshape(1, count)
        seg_col = segment_ids.reshape(count, 1)
        live = seg_row >= 0

        inputs = to_rel(tok_whole).astype(F32)
        mean_one = jnp.mean(inputs, axis=0, keepdims=True)
        inv_one = lax.rsqrt(jnp.mean(inputs * inputs, axis=0, keepdims=True) - mean_one * mean_one + EPS)
        hat_one = (inputs - mean_one) * inv_one
        normed_one = (hat_one * gain_one + bias_one).astype(BF16)
        projected = mm_t(qkv_rel, normed_one)
        head_rows = heads * HD
        bias_col = jnp.concatenate(
            [qv_bias[:head_rows], jnp.zeros((head_rows,), F32), qv_bias[head_rows:]]
        ).reshape(3 * head_rows, 1)
        rest = jnp.concatenate([after(pair_half, projected), mix_half], axis=1)
        rest = rest_whole(rest, row_bits[1:])
        up_rel, down_rel, mix_rel = rest[:, :n_hid], rest[:, n_hid : 2 * n_hid], rest[:, 2 * n_hid :]
        qkv, attended, totals = attend(projected, bias_col, seg_row, seg_col, heads)

        att_whole = lax.all_gather(attended, "cols", axis=0, tiled=True)
        hidden = inputs + mm(mix_rel, att_whole) + bias_mix
        mean_two = jnp.mean(hidden, axis=0, keepdims=True)
        inv_two = lax.rsqrt(jnp.mean(hidden * hidden, axis=0, keepdims=True) - mean_two * mean_two + EPS)
        hat_two = (hidden - mean_two) * inv_two
        normed_two = (hat_two * gain_two + bias_two).astype(BF16)

        pre_act = mm_t(up_rel, normed_two) + up_bias[:, None]
        value, slope = gelu_both(pre_act)
        active = value.astype(BF16)
        grad_final_b = jnp.where(live, cot_rel, jnp.zeros_like(cot_rel))
        grad_pre = (mm_t(down_rel, grad_final_b) * slope).astype(BF16)
        part_two = mm(up_rel, grad_pre).astype(BF16)
        got = col_exchange(lambda col: take(part_two, col * part, part, 1))
        grad_two = sum(piece.astype(F32) for piece, _ in got)

        def reduce_core(grad):
            half = grad.shape[0] // 2
            return grad[:half] + swap(grad[half:].astype(BF16), "rows", n_rows, row_bits[-1]).astype(F32)

        def reduce_rest(grad, bits):
            for bit in bits:
                half = grad.shape[0] // 2
                grad = grad[:half] + swap(grad[half:].astype(BF16), "rows", n_rows, bit).astype(F32)
            return grad

        def reduce_dp(grad):
            for bit in bits_of(n_dp):
                grad = grad + swap(grad.astype(BF16), "dp", n_dp, bit).astype(F32)
            return grad

        grads_ff = jnp.concatenate([mm_nt(grad_final_b, active), mm_nt(normed_two, grad_pre)], axis=1)
        grads_ff = reduce_core(grads_ff)
        part_out = mm(down_rel, active)

        own_at = at_col * part
        own_hat = (take(hidden, own_at, part, 1) - take(mean_two, own_at, part, 1)) * take(
            inv_two, own_at, part, 1
        )
        scaled = grad_two * gain_two
        grad_hidden = take(grad_final_b, own_at, part, 1).astype(F32) + take(inv_two, own_at, part, 1) * (
            scaled
            - jnp.mean(scaled, axis=0, keepdims=True)
            - own_hat * jnp.mean(scaled * own_hat, axis=0, keepdims=True)
        )
        grad_hidden_b = grad_hidden.astype(BF16)
        grad_att_all = mm_t(mix_rel, grad_hidden_b).astype(BF16)
        got = col_exchange(lambda col: take(grad_att_all, col * feat, feat, 0))
        grad_att = jnp.zeros((feat, count), BF16)
        for piece, col in got:
            grad_att = put(grad_att, piece, col * part, 1)

        grads_ff = reduce_rest(after(grads_ff, grad_att_all), row_bits[::-1][1:])
        grads_mix = mm_nt(grad_hidden_b, take(att_whole, own_at, part, 1))
        grads_mix = reduce_core(grads_mix)
        part_out = after(part_out, grad_att_all)
        out_sum = col_halving(lambda col: take(part_out, place(col) * feat, feat, 0))
        own_hidden = take(hidden, place(at_col) * feat, feat, 0)
        output = own_hidden + down_bias[:, None] + out_sum

        grad_proj, qv_sums = attend_back(qkv, attended, grad_att, totals, seg_row, seg_col, heads)
        grads_ff = reduce_dp(after(grads_ff, grad_proj))
        grad_one_part = mm(qkv_rel, grad_proj)

        scaled = grad_one_part * gain_one
        share = put(jnp.zeros((width, count), F32), grad_hidden, own_at, 1) + inv_one * (
            scaled
            - jnp.mean(scaled, axis=0, keepdims=True)
            - hat_one * jnp.mean(scaled * hat_one, axis=0, keepdims=True)
        )
        share_b = share.astype(BF16)
        got = col_exchange(lambda col: take(share_b, place(col) * feat, feat, 0))
        grad_tokens = sum(piece.astype(F32) for piece, _ in got)

        grads_mix = reduce_rest(grads_mix, row_bits[::-1][1:])
        grads_mix = jnp.stack([take(grads_mix, col * feat, feat, 1) for col in range(n_cols)])
        grads_mix = col_halving(lambda col: lax.dynamic_index_in_dim(grads_mix, col, 0, keepdims=False))
        grads_qkv = reduce_core(mm_nt(normed_one, grad_proj))
        grads_qkv = reduce_rest(grads_qkv, row_bits[::-1][1:])
        grads_last = reduce_dp(jnp.concatenate([grads_qkv, grads_mix], axis=1))

        wide_sums = jnp.stack(
            [
                jnp.sum(grad_two * own_hat, axis=1),
                jnp.sum(grad_two, axis=1),
                jnp.sum(grad_hidden, axis=1),
                jnp.sum(grad_one_part * hat_one, axis=1),
                jnp.sum(grad_one_part, axis=1),
            ],
            axis=1,
        )
        wide_sums = whole_sum(to_nat(wide_sums), [("cols", n_cols)])
        wide_sums = take(wide_sums, at_col * feat, feat, 0).T.reshape(-1)
        own_final = jnp.where(live, cotangent.astype(F32), 0.0)
        n_qv = 2 * head_rows
        sums = jnp.concatenate(
            [
                wide_sums,
                jnp.sum(own_final, axis=1),
                jnp.sum(grad_pre.astype(F32), axis=1),
                qv_sums.reshape(-1),
            ]
        )
        sums = whole_sum(sums, [("rows", n_rows), ("dp", n_dp)])
        cuts = [0]
        for length in (feat, feat, feat, feat, feat, feat, n_hid, n_qv):
            cuts.append(cuts[-1] + length)
        sums = [sums[at:end] for at, end in zip(cuts[:-1], cuts[1:])]
        return (
            output.astype(BF16),
            grad_tokens,
            sums[3],
            sums[4],
            grads_last[:, :n_qkv],
            sums[7],
            grads_last[:, n_qkv:].T,
            sums[2],
            sums[0],
            sums[1],
            grads_ff[:, n_hid:],
            sums[6],
            grads_ff[:, :n_hid],
            sums[5],
        )

    return body


def solution(mesh):
    sizes = mesh.shape
    return jax.shard_map(
        make_body(sizes["dp"], sizes["rows"], sizes["cols"]),
        mesh=mesh,
        in_specs=(
            P("cols", ("dp", "rows")),
            P(("dp", "rows")),
            P("cols"),
            P("cols"),
            P("rows", "cols"),
            P("cols"),
            P("cols", "rows"),
            P("cols"),
            P("cols"),
            P("cols"),
            P("rows", "cols"),
            P("cols"),
            P("rows", "cols"),
            P("cols"),
            P("cols", ("dp", "rows")),
        ),
        out_specs=(
            P("cols", ("dp", "rows")),
            P("cols", ("dp", "rows")),
            P("cols"),
            P("cols"),
            P("rows", "cols"),
            P("cols"),
            P("cols", "rows"),
            P("cols"),
            P("cols"),
            P("cols"),
            P("rows", "cols"),
            P("cols"),
            P("rows", "cols"),
            P("cols"),
        ),
        check_vma=False,
    )
```

```python
import functools
import math

import jax
import jax.numpy as jnp
from jax import lax
from jax.experimental import pallas as pl
from jax.experimental.pallas import tpu as pltpu
from jax.sharding import PartitionSpec as P

HD = 64
MAXLEN = 256
EPS = 1e-05
NEG = -1e30
ROOT = 0.7978845608028654
CUBIC = 0.044715
F32 = jnp.float32
BF16 = jnp.bfloat16


def dot(left, right, dims):
    return lax.dot_general(left, right, (dims, ((), ())), preferred_element_type=F32)


def mm(left, right):
    return dot(left, right, ((1,), (0,)))


def mm_t(left, right):
    return dot(left, right, ((0,), (0,)))


def mm_nt(left, right):
    return dot(left, right, ((1,), (1,)))


def gelu_both(pre_act):
    inner_arg = ROOT * (pre_act + CUBIC * pre_act * pre_act * pre_act)
    tanh_val = jnp.tanh(inner_arg)
    value = 0.5 * pre_act * (1.0 + tanh_val)
    slope = 0.5 * (1.0 + tanh_val) + 0.5 * pre_act * (1.0 - tanh_val * tanh_val) * ROOT * (
        1.0 + 3.0 * CUBIC * pre_act * pre_act
    )
    return value, slope


def allowed_mask(seg_row, seg_col, width):
    key_pos = lax.broadcasted_iota(jnp.int32, (width, width), 0)
    query_pos = lax.broadcasted_iota(jnp.int32, (width, width), 1)
    same_seg = (seg_col == seg_row) & (seg_row >= 0)
    return (key_pos < query_pos) & same_seg | (key_pos == query_pos)


def block(index, size):
    return pl.ds(pl.multiple_of(index * size, size), size)


def norm_cols(tok_ref, count, which):
    cols = tok_ref[:, count : tok_ref.shape[1]].astype(F32)
    return [cols[:, k : k + 1] + cols[:, k + 5 : k + 6] + cols[:, k + 10 : k + 11] for k in which]


def run(kernel, name, outs, ins, scratch=(), flops=0):
    specs = [pl.BlockSpec(memory_space=pltpu.SMEM)]
    specs += [pl.BlockSpec(memory_space=pltpu.VMEM)] * (len(ins) - 1)
    size = sum(math.prod(value.shape) * value.dtype.itemsize for value in list(ins) + list(outs))
    return pl.pallas_call(
        kernel,
        out_shape=outs,
        in_specs=specs,
        out_specs=[pl.BlockSpec(memory_space=pltpu.VMEM)] * len(outs),
        scratch_shapes=list(scratch),
        name=name,
        cost_estimate=pl.CostEstimate(flops=flops, transcendentals=0, bytes_accessed=size),
    )(*ins)


def shaped(shape, dtype):
    return jax.ShapeDtypeStruct(shape, dtype)


def pack_kernel(here, tok, g1, b1, bm, g2, b2, qv, up, down, seg, packed, qkv_col, up_col, down_col, seg_col):
    feat, count = tok.shape
    rows = jnp.concatenate([ref[...] for ref in (g1, b1, bm, g2, b2)], axis=0)
    high = rows.astype(BF16).astype(F32)
    middle = (rows - high).astype(BF16).astype(F32)
    low = rows - high - middle
    used = 3 * rows.shape[0]
    filler = jnp.zeros((128 - used, feat), F32)
    packed[:, :count] = tok[...]
    packed[:, count:] = jnp.concatenate([high, middle, low, filler], axis=0).T.astype(BF16)

    def column(row):
        return jnp.broadcast_to(row, (128, row.shape[1])).T[:, :1]

    half = qv.shape[1] // 2
    qv_col = column(qv[...])
    qkv_col[:half, :] = qv_col[:half]
    qkv_col[half : 2 * half, :] = jnp.zeros((half, 1), F32)
    qkv_col[2 * half :, :] = qv_col[half:]
    up_col[...] = column(up[...])
    down_col[...] = column(down[...])
    seg_col[...] = column(seg[...].astype(F32)).astype(jnp.int32)


def first_kernel(order, heads, here, tok, w0, w1, w2, w3, bias, row, col, normed, stats, qkv, att, totals, w_all):
    feat = w0.shape[0]
    count = row.shape[1]
    for value, piece in zip(order, (w0, w1, w2, w3)):
        w_all[block(here[0] ^ value, feat), :] = piece[...]
    gain, shift = norm_cols(tok, count, (0, 1))
    values = tok[:, :count].astype(F32)
    mean = jnp.mean(values, axis=0, keepdims=True)
    inv = lax.rsqrt(jnp.mean(values * values, axis=0, keepdims=True) - mean * mean + EPS)
    stats[0:1, :] = mean
    stats[1:2, :] = inv
    normed[...] = ((values - mean) * inv * gain + shift).astype(BF16)
    qkv[...] = (mm_t(w_all[...], normed[...]) + bias[...]).astype(BF16)
    head_rows = heads * HD
    scale = 1.0 / math.sqrt(HD)
    width = min(MAXLEN, count)
    for half in range(count // width):
        cols = pl.ds(half * width, width)
        allowed = allowed_mask(row[:, cols], col[cols, :], width)
        for head in range(heads):
            query = qkv[pl.ds(head * HD, HD), cols]
            keys = qkv[pl.ds(head_rows + head * HD, HD), cols]
            held = qkv[pl.ds(2 * head_rows + head * HD, HD), cols]
            scores = jnp.where(allowed, mm_t(keys, query) * scale, NEG)
            top = jnp.max(scores, axis=0, keepdims=True)
            log_total = top + jnp.log(jnp.sum(jnp.exp(scores - top), axis=0, keepdims=True))
            probs = jnp.exp(scores - log_total).astype(BF16)
            att[pl.ds(head * HD, HD), cols] = mm(held, probs).astype(BF16)
            totals[pl.ds(head, 1), cols] = log_total


def mix_pack_kernel(here, m0, m1, m2, m3, out):
    for step, piece in enumerate((m0, m1, m2, m3)):
        out[block(here[1] ^ step, m0.shape[0]), :] = piece[...]


def middle_kernel(
    order, here, tok, att, m0, m1, m2, m3, u0, u1, u2, u3, d0, d1, d2, d3, c0, c1, c2, c3, row, up_col,
    normed, grad_pre, active, grad_final, p1, p2, p3, own_two, own_hat, own_inv, own_hidden, up_sum, down_all,
    up_all, hidden,
):
    feat, count = c0.shape
    part = own_two.shape[1]
    live = row[...] >= 0
    bias_mix, gain, shift = norm_cols(tok, count, (2, 3, 4))
    for value, piece in zip(order, (u0, u1, u2, u3)):
        up_all[block(here[0] ^ value, feat), :] = piece[...]
    for value, piece in zip(order, (d0, d1, d2, d3)):
        down_all[block(here[0] ^ value, feat), :] = piece[...]
    for step, piece in enumerate((c0, c1, c2, c3)):
        masked = jnp.where(live, piece[...].astype(F32), 0.0)
        grad_final[block(here[1] ^ step, feat), :] = masked.astype(BF16)
    for value, piece in zip(order, (m0, m1, m2, m3)):
        hidden[block(here[0] ^ value, feat), :] = mm_t(piece[...], att[...])
    hidden[...] = hidden[...] + tok[:, :count].astype(F32) + bias_mix
    values = hidden[...]
    mean = jnp.mean(values, axis=0, keepdims=True)
    inv = lax.rsqrt(jnp.mean(values * values, axis=0, keepdims=True) - mean * mean + EPS)
    own_hidden[...] = hidden[block(here[1], feat), :]
    hat = (values - mean) * inv
    normed[...] = (hat * gain + shift).astype(BF16)
    hidden[...] = hat
    own_inv[...] = jnp.broadcast_to(inv, (8, count))
    own_hat[...] = hidden[:, block(here[1], part)]
    value, slope = gelu_both(mm_t(up_all[...], normed[...]) + up_col[...])
    active[...] = value.astype(BF16)
    grad = mm_t(down_all[...], grad_final[...]) * slope
    grad_pre[...] = grad.astype(BF16)
    up_sum[...] = jnp.sum(grad_pre[...].astype(F32), axis=1, keepdims=True)
    hidden[...] = mm(up_all[...], grad_pre[...])
    own_two[...] = hidden[:, block(here[1], part)]
    for step, out in enumerate((p1, p2, p3)):
        out[...] = hidden[:, block(here[1] ^ (step + 1), part)].astype(BF16)


def ff_grads_kernel(order, here, grad_final, active, normed, grad_pre, down_all, send, keep, out_send, out_keep):
    feat = keep.shape[0] // 2
    hid = active.shape[0]
    for at, value in enumerate(order):
        rows = block(here[0] ^ value, feat)
        down = mm_nt(grad_final[rows, :], active[...])
        up = mm_nt(normed[rows, :], grad_pre[...])
        if at < 2:
            keep[pl.ds(at * feat, feat), :hid] = down
            keep[pl.ds(at * feat, feat), hid:] = up
        else:
            send[pl.ds((at - 2) * feat, feat), :hid] = down.astype(BF16)
            send[pl.ds((at - 2) * feat, feat), hid:] = up.astype(BF16)
    for step in range(4):
        out = mm(down_all[block(here[1] ^ step, feat), :], active[...])
        if step % 2:
            out_send[pl.ds(step // 2 * feat, feat), :] = out.astype(BF16)
        else:
            out_keep[pl.ds(step // 2 * feat, feat), :] = out


def second_back_kernel(
    order, here, tok, own_two, r1, r2, r3, own_hat, own_inv, grad_final, m0, m1, m2, m3,
    grad_hidden, grad_hidden_b, a0, a1, a2, a3, sums, all_att,
):
    feat = a0.shape[0]
    part = own_two.shape[1]
    (gain,) = norm_cols(tok, grad_final.shape[1], (3,))
    grad = own_two[...] + r1[...].astype(F32) + r2[...].astype(F32) + r3[...].astype(F32)
    hat = own_hat[...]
    lanes = block(here[1], part)
    inv = own_inv[:, lanes][:1]
    scaled = grad * gain
    out = grad_final[:, lanes].astype(F32) + inv * (
        scaled
        - jnp.mean(scaled, axis=0, keepdims=True)
        - hat * jnp.mean(scaled * hat, axis=0, keepdims=True)
    )
    grad_hidden[...] = out
    grad_hidden_b[...] = out.astype(BF16)
    total = jnp.zeros(all_att.shape, F32)
    for value, piece in zip(order, (m0, m1, m2, m3)):
        total += mm(piece[...], grad_hidden_b[block(here[0] ^ value, feat), :])
    all_att[...] = total.astype(BF16)
    for step, ref in enumerate((a0, a1, a2, a3)):
        ref[...] = all_att[block(here[1] ^ step, feat), :]
    sums[:, 0:1] = jnp.sum(grad * hat, axis=1, keepdims=True)
    sums[:, 1:2] = jnp.sum(grad, axis=1, keepdims=True)
    sums[:, 2:3] = jnp.sum(out, axis=1, keepdims=True)


def mix_grad_kernel(order, here, att, grad_hidden_b, send, keep):
    feat = send.shape[2]
    own = att[:, block(here[1], grad_hidden_b.shape[1])]
    for at, value in enumerate(order):
        grad = mm_nt(own, grad_hidden_b[block(here[0] ^ value, feat), :])
        if at < 2:
            keep[at] = grad
        else:
            send[at - 2] = grad.astype(BF16)


def first_back_kernel(
    order, heads, here, tok, stats, qkv, att, totals, a0, a1, a2, a3, row, col, w0, w1, w2, w3, grad_hidden,
    grad_proj, qv_sum, s0, s1, s2, s3, sums, grad_att, share,
):
    feat, count = att.shape
    part = a0.shape[1]
    head_rows = heads * HD
    scale = 1.0 / math.sqrt(HD)
    for step, piece in enumerate((a0, a1, a2, a3)):
        grad_att[:, block(here[1] ^ step, part)] = piece[...]
    width = min(MAXLEN, count)
    for half in range(count // width):
        cols = pl.ds(half * width, width)
        allowed = allowed_mask(row[:, cols], col[cols, :], width)
        for head in range(heads):
            query = qkv[pl.ds(head * HD, HD), cols]
            keys = qkv[pl.ds(head_rows + head * HD, HD), cols]
            held = qkv[pl.ds(2 * head_rows + head * HD, HD), cols]
            grad = grad_att[pl.ds(head * HD, HD), cols]
            attended = att[pl.ds(head * HD, HD), cols]
            delta = jnp.sum(grad.astype(F32) * attended.astype(F32), axis=0, keepdims=True)
            scores = jnp.where(allowed, mm_t(keys, query) * scale, NEG)
            probs = jnp.exp(scores - totals[pl.ds(head, 1), cols])
            grad_held = mm_nt(grad, probs.astype(BF16))
            grad_probs = mm_t(held, grad)
            grad_scores = (probs * (grad_probs - delta) * scale).astype(BF16)
            grad_query = mm(keys, grad_scores)
            grad_keys = mm_nt(query, grad_scores)
            grad_proj[pl.ds(head * HD, HD), cols] = grad_query.astype(BF16)
            grad_proj[pl.ds(head_rows + head * HD, HD), cols] = grad_keys.astype(BF16)
            grad_proj[pl.ds(2 * head_rows + head * HD, HD), cols] = grad_held.astype(BF16)
            for at, grown in ((head * HD, grad_query), (head_rows + head * HD, grad_held)):
                total = jnp.sum(grown, axis=1, keepdims=True)
                if half:
                    total = total + qv_sum[pl.ds(at, HD), :]
                qv_sum[pl.ds(at, HD), :] = total
    for value, piece in zip(order, (w0, w1, w2, w3)):
        share[block(here[0] ^ value, feat), :] = mm(piece[...], grad_proj[...])
    (gain,) = norm_cols(tok, count, (0,))
    inv = stats[1:2, :]
    hat = (tok[:, :count].astype(F32) - stats[0:1, :]) * inv
    grad = share[...]
    sums[:, 0:1] = jnp.sum(grad * hat, axis=1, keepdims=True)
    sums[:, 1:2] = jnp.sum(grad, axis=1, keepdims=True)
    scaled = grad * gain
    share[...] = inv * (
        scaled
        - jnp.mean(scaled, axis=0, keepdims=True)
        - hat * jnp.mean(scaled * hat, axis=0, keepdims=True)
    )
    share[:, block(here[1], part)] += grad_hidden[...]
    s0[...] = share[block(here[1], feat), :]
    for step, ref in enumerate((s1, s2, s3)):
        ref[...] = share[block(here[1] ^ (step + 1), feat), :].astype(BF16)


def qkv_grads_kernel(order, here, normed, grad_proj, send, keep):
    feat = keep.shape[0] // 2
    for at, value in enumerate(order):
        grad = mm_nt(normed[block(here[0] ^ value, feat), :], grad_proj[...])
        if at < 2:
            keep[pl.ds(at * feat, feat), :] = grad
        else:
            send[pl.ds((at - 2) * feat, feat), :] = grad.astype(BF16)


def sums_kernel(here, second, first, up_sum, qv_sum, cot, row, wide, rest):
    width = second.shape[0]
    feat = cot.shape[0]
    lane = lax.broadcasted_iota(jnp.int32, (width, 128), 1)

    def rows_of(columns):
        total = jnp.zeros((width, 128), F32)
        for at, column in columns:
            total = jnp.where(lane == at, column, total)
        return total.T[:8]

    wide[...] = rows_of([(k, second[:, k : k + 1]) for k in range(3)] + [(3 + k, first[:, k : k + 1]) for k in range(2)])
    down = jnp.sum(jnp.where(row[...] >= 0, cot[...].astype(F32), 0.0), axis=1, keepdims=True)
    down = jnp.concatenate([down, jnp.zeros((width - feat, 1), F32)], axis=0)
    held = jnp.concatenate([qv_sum[...], jnp.zeros((width - qv_sum.shape[0], 1), F32)], axis=0)
    rest[...] = rows_of([(5, up_sum[...]), (6, held), (7, down)])


def halve_kernel(here, keep, got, kept, send):
    half = kept.shape[0]
    kept[...] = keep[:half] + got[:half].astype(F32)
    send[...] = (keep[half:] + got[half:].astype(F32)).astype(BF16)


def bits_of(size):
    bits, bit = [], 1
    while bit < size:
        bits.append(bit)
        bit *= 2
    return bits


def swap(values, axis, size, bit):
    return lax.ppermute(values, axis, [(at, at ^ bit) for at in range(size)])


def after(value, *others):
    return lax.optimization_barrier((value,) + others)[0]


def make_body(n_dp, n_rows, n_cols):
    assert n_rows == 4 and n_cols == 4
    far, near = 2, 1
    order = (0, far, near, far ^ near)

    def over_rows(value, bit):
        return swap(value, "rows", n_rows, bit)

    def over_cols(value, bit):
        return swap(value, "cols", n_cols, bit)

    def over_dp(value):
        value = value.astype(BF16).astype(F32)
        for bit in bits_of(n_dp):
            value = value + swap(value.astype(BF16), "dp", n_dp, bit).astype(F32)
        return value

    def body(
        tokens,
        segment_ids,
        first_gain,
        first_bias,
        qkv_weight,
        qv_bias,
        mix_weight,
        mix_bias,
        second_gain,
        second_bias,
        up_weight,
        up_bias,
        down_weight,
        down_bias,
        cotangent,
    ):
        feat, count = tokens.shape
        width = feat * n_cols
        part = count // n_cols
        n_qkv = qkv_weight.shape[1]
        n_hid = up_weight.shape[1]
        heads = n_qkv // (3 * HD)
        head_rows = heads * HD
        here = jnp.stack([lax.axis_index("rows"), lax.axis_index("cols")]).astype(jnp.int32)
        row = segment_ids.reshape(1, count)

        def halve(keep, got):
            half = (keep.shape[0] // 2,) + keep.shape[1:]
            return run(halve_kernel, "halve", (shaped(half, F32), shaped(half, BF16)), (here, keep, got))

        qkv_y = over_rows(qkv_weight, far)
        qkv_c = over_rows(qkv_weight, near)
        packed, qkv_col, up_col, down_col, seg_col = run(
            pack_kernel,
            "pack",
            (
                shaped((feat, count + 128), BF16),
                shaped((n_qkv, 1), F32),
                shaped((n_hid, 1), F32),
                shaped((feat, 1), F32),
                shaped((count, 1), jnp.int32),
            ),
            (here, tokens)
            + tuple(
                value.reshape(1, -1)
                for value in (
                    first_gain, first_bias, mix_bias, second_gain, second_bias, qv_bias, up_bias, down_bias, segment_ids,
                )
            ),
        )
        tok = lax.all_gather(packed, "cols", axis=0, tiled=True)
        qkv_yc = over_rows(qkv_y, near)
        w_pieces = (qkv_weight, qkv_y, qkv_c, qkv_yc)

        mix_own, up_own, down_own, cot_own = [
            after(value, tok) for value in (mix_weight, up_weight, down_weight, cotangent)
        ]
        mix_z = [over_cols(mix_own, bit) for bit in (1, 2, 3)]
        up_y, down_y = over_rows(up_own, far), over_rows(down_own, far)
        up_c, down_c = over_rows(up_own, near), over_rows(down_own, near)
        cot_z = [over_cols(cot_own, bit) for bit in (1, 2, 3)]

        normed_one, stats, qkv, attended, totals = run(
            functools.partial(first_kernel, order, heads),
            "first",
            (
                shaped((width, count), BF16),
                shaped((2, count), F32),
                shaped((n_qkv, count), BF16),
                shaped((head_rows, count), BF16),
                shaped((heads, count), F32),
            ),
            (here, tok) + w_pieces + (qkv_col, row, seg_col),
            scratch=(pltpu.VMEM((width, n_qkv), BF16),),
            flops=2 * width * n_qkv * count,
        )
        (mix_all,) = run(
            mix_pack_kernel, "mix_pack", (shaped((width, feat), BF16),), (here, mix_weight) + tuple(mix_z)
        )
        mix_y, mix_c = over_rows(mix_all, far), over_rows(mix_all, near)

        att = lax.all_gather(attended, "cols", axis=0, tiled=True)
        up_yc, down_yc, mix_yc = over_rows(up_y, near), over_rows(down_y, near), over_rows(mix_y, near)
        m_pieces = (mix_all, mix_y, mix_c, mix_yc)

        wide_b = shaped((width, count), BF16)
        piece_b = shaped((width, part), BF16)
        piece_f = shaped((width, part), F32)
        (
            normed_two, grad_pre, active, grad_final, p1, p2, p3, own_two, own_hat, own_inv, own_hidden, up_sum, down_all,
        ) = run(
            functools.partial(middle_kernel, order),
            "middle",
            (
                wide_b, shaped((n_hid, count), BF16), shaped((n_hid, count), BF16), wide_b,
                piece_b, piece_b, piece_b, piece_f, piece_f,
                shaped((8, count), F32), shaped((feat, count), F32), shaped((n_hid, 1), F32), shaped((width, n_hid), BF16),
            ),
            (here, tok, att)
            + m_pieces
            + (up_weight, up_y, up_c, up_yc)
            + (down_weight, down_y, down_c, down_yc)
            + (cotangent,)
            + tuple(cot_z)
            + (row, up_col),
            scratch=(pltpu.VMEM((width, n_hid), BF16), pltpu.VMEM((width, count), F32)),
            flops=2 * width * count * (width + 3 * n_hid),
        )
        got = [over_cols(value, bit) for value, bit in zip((p1, p2, p3), (1, 2, 3))]

        ff_send, ff_keep, out_send, out_keep = run(
            functools.partial(ff_grads_kernel, order),
            "ff_grads",
            (
                shaped((2 * feat, 2 * n_hid), BF16), shaped((2 * feat, 2 * n_hid), F32),
                shaped((2 * feat, count), BF16), shaped((2 * feat, count), F32),
            ),
            (here, grad_final, active, normed_two, grad_pre, down_all),
            flops=2 * width * count * 3 * n_hid,
        )
        ff_keep, ff_send = halve(ff_keep, over_rows(ff_send, near))
        ff_got = over_rows(ff_send, far)

        grad_hidden, grad_hidden_b, a0, a1, a2, a3, second = run(
            functools.partial(second_back_kernel, order),
            "second_back",
            (
                piece_f, piece_b,
                shaped((feat, part), BF16), shaped((feat, part), BF16), shaped((feat, part), BF16), shaped((feat, part), BF16),
                shaped((width, 8), F32),
            ),
            (here, tok, own_two) + tuple(got) + (own_hat, own_inv, grad_final) + m_pieces,
            scratch=(pltpu.VMEM((width, part), BF16),),
            flops=2 * width * part * width,
        )
        b1, b2, b3 = [over_cols(value, bit) for value, bit in zip((a1, a2, a3), (1, 2, 3))]
        mix_send, mix_keep = run(
            functools.partial(mix_grad_kernel, order),
            "mix_grad",
            (shaped((2, width, feat), BF16), shaped((2, width, feat), F32)),
            (here, att, grad_hidden_b),
            flops=2 * width * part * width,
        )
        mix_keep, mix_send = halve(mix_keep, over_rows(mix_send, near))
        mix_got = over_rows(mix_send, far)

        grad_proj, qv_sum, s0, s1, s2, s3, first = run(
            functools.partial(first_back_kernel, order, heads),
            "first_back",
            (
                shaped((n_qkv, count), BF16), shaped((2 * head_rows, 1), F32),
                shaped((feat, count), F32), shaped((feat, count), BF16), shaped((feat, count), BF16), shaped((feat, count), BF16),
                shaped((width, 8), F32),
            ),
            (here, tok, stats, qkv, attended, totals, a0, b1, b2, b3, row, seg_col) + w_pieces + (grad_hidden,),
            scratch=(pltpu.VMEM((head_rows, count), BF16), pltpu.VMEM((width, count), F32)),
            flops=2 * width * n_qkv * count,
        )
        got = [over_cols(value, bit) for value, bit in zip((s1, s2, s3), (1, 2, 3))]

        qkv_send, qkv_keep = run(
            functools.partial(qkv_grads_kernel, order),
            "qkv_grads",
            (shaped((2 * feat, n_qkv), BF16), shaped((2 * feat, n_qkv), F32)),
            (here, normed_one, grad_proj),
            flops=2 * width * count * n_qkv,
        )
        qkv_keep, qkv_send = halve(qkv_keep, over_rows(qkv_send, near))
        grad_qkv = over_dp(qkv_keep + over_rows(qkv_send, far).astype(F32))
        grad_ff = over_dp(ff_keep + ff_got.astype(F32))

        wide, rest = run(
            sums_kernel, "sums", (shaped((8, width), F32), shaped((8, width), F32)),
            (here, second, first, up_sum, qv_sum, cotangent, row),
        )
        for bit in bits_of(n_cols):
            wide = wide + over_cols(wide, bit)
        sums = wide + rest
        for axis, size in (("rows", n_rows), ("dp", n_dp)):
            for bit in bits_of(size):
                sums = sums + swap(sums, axis, size, bit)

        at_col = lax.axis_index("cols")
        grad_mix = (mix_keep[0] + mix_got[0].astype(F32)).reshape(n_cols, feat, feat)

        def mix_block(step):
            return lax.dynamic_index_in_dim(grad_mix, at_col ^ step, 0, keepdims=False)

        mix_got = over_cols(jnp.stack([mix_block(1), mix_block(3)]).astype(BF16), 1).astype(F32)
        mix_low, mix_high = mix_block(0) + mix_got[0], mix_block(2) + mix_got[1]
        grad_mix = over_dp(mix_low + over_cols(mix_high.astype(BF16), 2).astype(F32))

        out_send = after(out_send, a1)
        out_keep, out_send = halve(out_keep, over_cols(out_send, 1))
        output = own_hidden + down_col + out_keep + over_cols(out_send, 2).astype(F32)

        grad_tokens = s0 + got[0].astype(F32) + got[1].astype(F32) + got[2].astype(F32)

        own = lax.dynamic_slice_in_dim(sums, at_col * feat, feat, 1)
        return (
            output.astype(BF16),
            grad_tokens,
            own[3],
            own[4],
            grad_qkv,
            sums[6, : 2 * head_rows],
            grad_mix,
            own[2],
            own[0],
            own[1],
            grad_ff[:, n_hid:],
            sums[5, :n_hid],
            grad_ff[:, :n_hid],
            sums[7, :feat],
        )

    return body


def solution(mesh):
    sizes = mesh.shape
    return jax.shard_map(
        make_body(sizes["dp"], sizes["rows"], sizes["cols"]),
        mesh=mesh,
        in_specs=(
            P("cols", ("dp", "rows")),
            P(("dp", "rows")),
            P("cols"),
            P("cols"),
            P("rows", "cols"),
            P("cols"),
            P("cols", "rows"),
            P("cols"),
            P("cols"),
            P("cols"),
            P("rows", "cols"),
            P("cols"),
            P("rows", "cols"),
            P("cols"),
            P("cols", ("dp", "rows")),
        ),
        out_specs=(
            P("cols", ("dp", "rows")),
            P("cols", ("dp", "rows")),
            P("cols"),
            P("cols"),
            P("rows", "cols"),
            P("cols"),
            P("cols", "rows"),
            P("cols"),
            P("cols"),
            P("cols"),
            P("rows", "cols"),
            P("cols"),
            P("rows", "cols"),
            P("cols"),
        ),
        check_vma=False,
    )
```

```python
import functools
import math

import jax
import jax.numpy as jnp
from jax import lax
from jax.experimental import pallas as pl
from jax.experimental.pallas import tpu as pltpu
from jax.sharding import PartitionSpec as P


HD = 64
MAXLEN = 256
EPS = 1e-05
NEG = -1e30
ROOT = 0.7978845608028654
CUBIC = 0.044715
F32 = jnp.float32
BF16 = jnp.bfloat16


def dot(left, right, dims):
    return lax.dot_general(left, right, (dims, ((), ())), preferred_element_type=F32)


def mm(left, right):
    return dot(left, right, ((1,), (0,)))


def mm_t(left, right):
    return dot(left, right, ((0,), (0,)))


def mm_nt(left, right):
    return dot(left, right, ((1,), (1,)))


def gelu_both(pre_act):
    inner_arg = ROOT * (pre_act + CUBIC * pre_act * pre_act * pre_act)
    tanh_val = jnp.tanh(inner_arg)
    value = 0.5 * pre_act * (1.0 + tanh_val)
    slope = 0.5 * (1.0 + tanh_val) + 0.5 * pre_act * (1.0 - tanh_val * tanh_val) * ROOT * (
        1.0 + 3.0 * CUBIC * pre_act * pre_act
    )
    return value, slope


def allowed_mask(seg_row, seg_col, width):
    key_pos = lax.broadcasted_iota(jnp.int32, (width, width), 0)
    query_pos = lax.broadcasted_iota(jnp.int32, (width, width), 1)
    same_seg = (seg_col == seg_row) & (seg_row >= 0)
    return (key_pos < query_pos) & same_seg | (key_pos == query_pos)


def block(index, size):
    return pl.ds(pl.multiple_of(index * size, size), size)


def norm_cols(tok_ref, count, which):
    start = tok_ref.shape[0] // 4 - 128
    cols = tok_ref[:, count : tok_ref.shape[1]].astype(F32)[:, start:]
    return [cols[:, k : k + 1] + cols[:, k + 5 : k + 6] + cols[:, k + 10 : k + 11] for k in which]


def run(kernel, outs, ins, scratch=(), flops=0):
    specs = [pl.BlockSpec(memory_space=pltpu.SMEM)]
    specs += [pl.BlockSpec(memory_space=pltpu.VMEM)] * (len(ins) - 1)
    size = sum(math.prod(value.shape) * value.dtype.itemsize for value in list(ins) + list(outs))
    return pl.pallas_call(
        kernel,
        out_shape=outs,
        in_specs=specs,
        out_specs=[pl.BlockSpec(memory_space=pltpu.VMEM)] * len(outs),
        scratch_shapes=list(scratch),
        cost_estimate=pl.CostEstimate(flops=flops, transcendentals=0, bytes_accessed=size),
    )(*ins)


def shaped(shape, dtype):
    return jax.ShapeDtypeStruct(shape, dtype)


def column(row):
    return jnp.broadcast_to(row, (128, row.shape[1])).T[:, :1]


def pack_kernel(here, tok, mix, cot, g1, b1, bm, g2, b2, down, seg, packed, packed_two, down_col, seg_col):
    feat, count = tok.shape
    rows = jnp.concatenate([ref[...] for ref in (g1, b1, bm, g2, b2)], axis=0)
    high = rows.astype(BF16).astype(F32)
    middle = (rows - high).astype(BF16).astype(F32)
    low = rows - high - middle
    used = 3 * rows.shape[0]
    norms = jnp.concatenate([high, middle, low, jnp.zeros((128 - used, feat), F32)], axis=0).T
    packed[:, :count] = tok[...]
    packed[:, count : count + 128] = jnp.concatenate(
        [mix[:, 128:].astype(F32), norms[:, : 128 - (feat - 128)]], axis=1
    ).astype(BF16)
    packed_two[:, :count] = cot[...]
    packed_two[:, count:] = mix[:, :128]
    down_col[...] = column(down[...])
    seg_col[...] = column(seg[...].astype(F32)).astype(jnp.int32)


def first_kernel(order, heads, here, tok, w0, w1, w2, w3, qv, row, col, normed, stats, qkv, att, totals, w_all):
    feat = w0.shape[0]
    count = row.shape[1]
    for value, piece in zip(order, (w0, w1, w2, w3)):
        w_all[block(here[0] ^ value, feat), :] = piece[...]
    gain, shift = norm_cols(tok, count, (0, 1))
    values = tok[:, :count].astype(F32)
    mean = jnp.mean(values, axis=0, keepdims=True)
    inv = lax.rsqrt(jnp.mean(values * values, axis=0, keepdims=True) - mean * mean + EPS)
    stats[0:1, :] = mean
    stats[1:2, :] = inv
    normed[...] = ((values - mean) * inv * gain + shift).astype(BF16)
    head_rows = heads * HD
    qv_col = column(qv[...].reshape(1, 2 * head_rows))
    bias = jnp.concatenate([qv_col[:head_rows], jnp.zeros((head_rows, 1), F32), qv_col[head_rows:]], axis=0)
    qkv[...] = (mm_t(w_all[...], normed[...]) + bias).astype(BF16)
    scale = 1.0 / math.sqrt(HD)
    width = min(MAXLEN, count)
    for half in range(count // width):
        cols = pl.ds(half * width, width)
        allowed = allowed_mask(row[:, cols], col[cols, :], width)
        for head in range(heads):
            query = qkv[pl.ds(head * HD, HD), cols]
            keys = qkv[pl.ds(head_rows + head * HD, HD), cols]
            held = qkv[pl.ds(2 * head_rows + head * HD, HD), cols]
            scores = jnp.where(allowed, mm_t(keys, query) * scale, NEG)
            top = jnp.max(scores, axis=0, keepdims=True)
            log_total = top + jnp.log(jnp.sum(jnp.exp(scores - top), axis=0, keepdims=True))
            probs = jnp.exp(scores - log_total).astype(BF16)
            att[pl.ds(head * HD, HD), cols] = mm(held, probs).astype(BF16)
            totals[pl.ds(head, 1), cols] = log_total


def mix_pack_kernel(tok, cot, out):
    out[:, :128] = cot[...]
    out[:, 128:] = tok[:, : out.shape[1] - 128]


def mix_pack(tok, cot, feat):
    width, lanes = tok.shape
    last = pl.BlockSpec((width, 128), lambda step: (0, lanes // 128 - 1))
    return pl.pallas_call(
        mix_pack_kernel,
        grid=(1,),
        out_shape=shaped((width, feat), BF16),
        in_specs=[last, last],
        out_specs=pl.BlockSpec((width, feat), lambda step: (0, 0)),
        name="mix_pack",
    )(tok, cot)


def middle_kernel(
    order, here, tok, att, m0, m1, m2, m3, u0, u1, u2, u3, d0, d1, d2, d3, cot, row, up,
    normed, grad_pre, active, grad_final, p1, p2, p3, own_two, own_hat, own_inv, own_hidden, up_sum, down_all,
    up_all, hidden,
):
    feat, count = own_hidden.shape
    part = own_two.shape[1]
    live = row[...] >= 0
    bias_mix, gain, shift = norm_cols(tok, count, (2, 3, 4))
    for value, piece in zip(order, (u0, u1, u2, u3)):
        up_all[block(here[0] ^ value, feat), :] = piece[...]
    for value, piece in zip(order, (d0, d1, d2, d3)):
        down_all[block(here[0] ^ value, feat), :] = piece[...]
    grad_final[...] = jnp.where(live, cot[:, :count].astype(F32), 0.0).astype(BF16)
    for value, piece in zip(order, (m0, m1, m2, m3)):
        hidden[block(here[0] ^ value, feat), :] = mm_t(piece[...], att[...])
    hidden[...] = hidden[...] + tok[:, :count].astype(F32) + bias_mix
    values = hidden[...]
    mean = jnp.mean(values, axis=0, keepdims=True)
    inv = lax.rsqrt(jnp.mean(values * values, axis=0, keepdims=True) - mean * mean + EPS)
    own_hidden[...] = hidden[block(here[1], feat), :]
    hat = (values - mean) * inv
    normed[...] = (hat * gain + shift).astype(BF16)
    hidden[...] = hat
    own_inv[...] = jnp.broadcast_to(inv, (8, count))
    own_hat[...] = hidden[:, block(here[1], part)]
    value, slope = gelu_both(mm_t(up_all[...], normed[...]) + column(up[...].reshape(1, up.shape[0])))
    active[...] = value.astype(BF16)
    grad = mm_t(down_all[...], grad_final[...]) * slope
    grad_pre[...] = grad.astype(BF16)
    up_sum[...] = jnp.sum(grad_pre[...].astype(F32), axis=1, keepdims=True)
    hidden[...] = mm(up_all[...], grad_pre[...])
    own_two[...] = hidden[:, block(here[1], part)]
    for step, out in enumerate((p1, p2, p3)):
        out[...] = hidden[:, block(here[1] ^ (step + 1), part)].astype(BF16)


def in_order(order, here, target, source):
    feat = target.shape[0] // len(order)
    for at, value in enumerate(order):
        target[pl.ds(at * feat, feat), :] = source[block(here[0] ^ value, feat), :]


def ff_grads_kernel(
    order, here, grad_final, active, normed, grad_pre, down_all, send, keep, out_send, out_keep, rows
):
    half = keep.shape[0]
    feat = half // 2
    hid = active.shape[0]
    in_order(order, here, rows, grad_final)
    down = mm_nt(rows[...], active[...])
    keep[:, :hid] = down[:half]
    send[:, :hid] = down[half:].astype(BF16)
    in_order(order, here, rows, normed)
    up = mm_nt(rows[...], grad_pre[...])
    keep[:, hid:] = up[:half]
    send[:, hid:] = up[half:].astype(BF16)
    for step in (0, 2):
        out_keep[pl.ds(step // 2 * feat, feat), :] = mm(down_all[block(here[1] ^ step, feat), :], active[...])
        out = mm(down_all[block(here[1] ^ (step + 1), feat), :], active[...])
        out_send[pl.ds(step // 2 * feat, feat), :] = out.astype(BF16)


def second_back_kernel(
    order, here, tok, own_two, r1, r2, r3, own_hat, own_inv, grad_final, m0, m1, m2, m3,
    grad_hidden, grad_hidden_b, sums, a0, a1, a2, a3, all_att,
):
    feat = a0.shape[0]
    part = own_two.shape[1]
    (gain,) = norm_cols(tok, grad_final.shape[1], (3,))
    grad = own_two[...] + r1[...].astype(F32) + r2[...].astype(F32) + r3[...].astype(F32)
    sums[:, 1:2] = jnp.sum(grad, axis=1, keepdims=True)
    hat = own_hat[...]
    lanes = block(here[1], part)
    inv = own_inv[:, lanes][:1]
    scaled = grad * gain
    out = grad_final[:, lanes].astype(F32) + inv * (
        scaled
        - jnp.mean(scaled, axis=0, keepdims=True)
        - hat * jnp.mean(scaled * hat, axis=0, keepdims=True)
    )
    grad_hidden[...] = out
    grad_hidden_b[...] = out.astype(BF16)
    sums[:, 0:1] = jnp.sum(grad * hat, axis=1, keepdims=True)
    sums[:, 2:3] = jnp.sum(out, axis=1, keepdims=True)
    total = jnp.zeros(all_att.shape, F32)
    for value, piece in zip(order, (m0, m1, m2, m3)):
        total += mm(piece[...], grad_hidden_b[block(here[0] ^ value, feat), :])
    all_att[...] = total.astype(BF16)
    for step, ref in enumerate((a0, a1, a2, a3)):
        ref[...] = all_att[block(here[1] ^ step, feat), :]


def first_back_kernel(
    order, heads, here, tok, stats, qkv, att, totals, a0, a1, a2, a3, row, col, w0, w1, w2, w3, grad_hidden, second,
    grad_proj, qv_sum, s0, s1, s2, s3, grad_att, share, sums,
):
    feat, count = att.shape
    part = a0.shape[1]
    head_rows = heads * HD
    scale = 1.0 / math.sqrt(HD)
    for step, piece in enumerate((a0, a1, a2, a3)):
        grad_att[:, block(here[1] ^ step, part)] = piece[...]
    width = min(MAXLEN, count)
    for half in range(count // width):
        cols = pl.ds(half * width, width)
        allowed = allowed_mask(row[:, cols], col[cols, :], width)
        for head in range(heads):
            query = qkv[pl.ds(head * HD, HD), cols]
            keys = qkv[pl.ds(head_rows + head * HD, HD), cols]
            held = qkv[pl.ds(2 * head_rows + head * HD, HD), cols]
            grad = grad_att[pl.ds(head * HD, HD), cols]
            attended = att[pl.ds(head * HD, HD), cols]
            delta = jnp.sum(grad.astype(F32) * attended.astype(F32), axis=0, keepdims=True)
            scores = jnp.where(allowed, mm_t(keys, query) * scale, NEG)
            probs = jnp.exp(scores - totals[pl.ds(head, 1), cols])
            grad_held = mm_nt(grad, probs.astype(BF16))
            grad_probs = mm_t(held, grad)
            grad_scores = (probs * (grad_probs - delta) * scale).astype(BF16)
            grad_query = mm(keys, grad_scores)
            grad_keys = mm_nt(query, grad_scores)
            grad_proj[pl.ds(head * HD, HD), cols] = grad_query.astype(BF16)
            grad_proj[pl.ds(head_rows + head * HD, HD), cols] = grad_keys.astype(BF16)
            grad_proj[pl.ds(2 * head_rows + head * HD, HD), cols] = grad_held.astype(BF16)
            for at, grown in ((head * HD, grad_query), (head_rows + head * HD, grad_held)):
                total = jnp.sum(grown, axis=1, keepdims=True)
                if half:
                    total = total + qv_sum[pl.ds(at, HD), :]
                qv_sum[pl.ds(at, HD), :] = total
    for value, piece in zip(order, (w0, w1, w2, w3)):
        share[block(here[0] ^ value, feat), :] = mm(piece[...], grad_proj[...])
    (gain,) = norm_cols(tok, count, (0,))
    inv = stats[1:2, :]
    hat = (tok[:, :count].astype(F32) - stats[0:1, :]) * inv
    grad = share[...]
    lane = lax.broadcasted_iota(jnp.int32, sums.shape, 1)
    columns = [second[:, k : k + 1] for k in range(3)]
    columns += [jnp.sum(grad * hat, axis=1, keepdims=True), jnp.sum(grad, axis=1, keepdims=True)]
    total = jnp.zeros(sums.shape, F32)
    for at, values in enumerate(columns):
        total = jnp.where(lane == at, values, total)
    sums[...] = total
    scaled = grad * gain
    share[...] = inv * (
        scaled
        - jnp.mean(scaled, axis=0, keepdims=True)
        - hat * jnp.mean(scaled * hat, axis=0, keepdims=True)
    )
    share[:, block(here[1], part)] += grad_hidden[...]
    for step, ref in enumerate((s0, s1, s2, s3)):
        rows = block(here[1] ^ step, feat)
        extra = ref.shape[0] - feat
        ref[:feat, :] = share[rows, :].astype(ref.dtype)
        ref[feat:, :feat] = sums[rows, :].T[:extra].astype(ref.dtype)


def last_grads(pair, here, normed, grad_proj, att, pieces, rows, hidden):
    feat, count = att.shape
    part = count // len(pieces)
    for at, value in enumerate(pair):
        source = block(here[0] ^ value, feat)
        target = pl.ds(at * feat, feat)
        rows[target, :] = normed[source, :]
        for step, ref in enumerate(pieces):
            hidden[target, block(here[1] ^ step, part)] = ref[source, :]
    return mm_nt(rows[...], grad_proj[...]), mm_nt(hidden[...], att[...])


def last_send_kernel(order, here, normed, grad_proj, att, h0, h1, h2, h3, send, rows, hidden):
    split = grad_proj.shape[0]
    qkv, mix = last_grads(order[2:], here, normed, grad_proj, att, (h0, h1, h2, h3), rows, hidden)
    send[:, :split] = qkv.astype(BF16)
    send[:, split:] = mix.astype(BF16)


def last_keep_kernel(order, here, normed, grad_proj, att, h0, h1, h2, h3, got, own, own_b, send, rows, hidden):
    feat = att.shape[0]
    split = grad_proj.shape[0]
    qkv, mix = last_grads(order[:2], here, normed, grad_proj, att, (h0, h1, h2, h3), rows, hidden)
    qkv += got[:, :split].astype(F32)
    mix += got[:, split:].astype(F32)
    own[:, :split] = qkv[:feat]
    own[:, split:] = mix[:feat]
    own_b[:, :split] = qkv[:feat].astype(BF16)
    own_b[:, split:] = mix[:feat].astype(BF16)
    send[:, :split] = qkv[feat:].astype(BF16)
    send[:, split:] = mix[feat:].astype(BF16)


def rest_kernel(here, up_sum, qv_sum, cot, row, rest):
    width = up_sum.shape[0]
    feat = cot.shape[0]
    down = jnp.sum(jnp.where(row[...] >= 0, cot[...].astype(F32), 0.0), axis=1, keepdims=True)
    down = jnp.concatenate([down, jnp.zeros((width - feat, 1), F32)], axis=0)
    held = jnp.concatenate([qv_sum[...], jnp.zeros((width - qv_sum.shape[0], 1), F32)], axis=0)
    lane = lax.broadcasted_iota(jnp.int32, (width, 128), 1)
    total = jnp.zeros((width, 128), F32)
    for at, values in ((5, up_sum[...]), (6, held), (7, down)):
        total = jnp.where(lane == at, values, total)
    rest[...] = total.T[:8]


def token_sum_kernel(here, s0, g1, g2, g3, rest, out, sums):
    feat = out.shape[0]
    total = s0[...]
    for ref in (g1, g2, g3):
        total += ref[...].astype(F32)
    out[...] = total[:feat]
    sums[...] = rest[...]
    sums[:5, :feat] = total[feat : feat + 5, :feat]


def last_sum_kernel(here, own, got_y, got_x, got_xy, qkv, mix):
    split = qkv.shape[1]
    total = own[...] + got_y[...].astype(F32) + got_x[...].astype(F32) + got_xy[...].astype(F32)
    qkv[...] = total[:, :split]
    mix[...] = total[:, split:].T


def halve_kernel(here, keep, got, kept, send):
    half = kept.shape[0]
    kept[...] = keep[:half] + got[:half].astype(F32)
    send[...] = (keep[half:] + got[half:].astype(F32)).astype(BF16)


def bits_of(size):
    bits, bit = [], 1
    while bit < size:
        bits.append(bit)
        bit *= 2
    return bits


def swap(values, axis, size, bit):
    return lax.ppermute(values, axis, [(at, at ^ bit) for at in range(size)])


def after(value, *others):
    return lax.optimization_barrier((value,) + others)[0]


def together(*values):
    return lax.optimization_barrier(values)


def make_body(n_dp, n_rows, n_cols):
    assert n_rows == 4 and n_cols == 4
    far, near = 2, 1
    order = (0, far, near, far ^ near)

    def over_rows(value, bit):
        return swap(value, "rows", n_rows, bit)

    def over_cols(value, bit):
        return swap(value, "cols", n_cols, bit)

    def all_over_cols(values):
        return [over_cols(value, bit) for value, bit in zip(values, (1, 2, 3))]

    def over_dp(value):
        value = value.astype(BF16).astype(F32)
        for bit in bits_of(n_dp):
            value = value + swap(value.astype(BF16), "dp", n_dp, bit).astype(F32)
        return value

    def body(
        tokens,
        segment_ids,
        first_gain,
        first_bias,
        qkv_weight,
        qv_bias,
        mix_weight,
        mix_bias,
        second_gain,
        second_bias,
        up_weight,
        up_bias,
        down_weight,
        down_bias,
        cotangent,
    ):
        feat, count = tokens.shape
        width = feat * n_cols
        part = count // n_cols
        n_qkv = qkv_weight.shape[1]
        n_hid = up_weight.shape[1]
        heads = n_qkv // (3 * HD)
        head_rows = heads * HD
        here = jnp.stack([lax.axis_index("rows"), lax.axis_index("cols")]).astype(jnp.int32)
        row = segment_ids.reshape(1, count)

        def halve(keep, got):
            half = (keep.shape[0] // 2,) + keep.shape[1:]
            return run(halve_kernel, (shaped(half, F32), shaped(half, BF16)), (here, keep, got))

        qkv_y = over_rows(qkv_weight, far)
        up_y, down_y = over_rows(up_weight, far), over_rows(down_weight, far)
        qkv_c, up_c, down_c = [over_rows(value, near) for value in (qkv_weight, up_weight, down_weight)]
        lanes = shaped((feat, count + 128), BF16)
        packed, packed_two, down_col, seg_col = run(
            pack_kernel,
            (lanes, lanes, shaped((feat, 1), F32), shaped((count, 1), jnp.int32)),
            (here, tokens, mix_weight, cotangent)
            + tuple(
                value.reshape(1, -1)
                for value in (first_gain, first_bias, mix_bias, second_gain, second_bias, down_bias, segment_ids)
            ),
        )
        tok = lax.all_gather(packed, "cols", axis=0, tiled=True)
        qkv_yc = over_rows(qkv_y, near)
        w_pieces = (qkv_weight, qkv_y, qkv_c, qkv_yc)
        cot = lax.all_gather(after(packed_two, tok), "cols", axis=0, tiled=True)
        mix_all = mix_pack(tok, cot, feat)
        mix_y, mix_c = over_rows(mix_all, far), over_rows(mix_all, near)
        up_yc, down_yc = over_rows(up_y, near), over_rows(down_y, near)

        normed_one, stats, qkv, attended, totals = run(
            functools.partial(first_kernel, order, heads),
            (
                shaped((width, count), BF16),
                shaped((2, count), F32),
                shaped((n_qkv, count), BF16),
                shaped((head_rows, count), BF16),
                shaped((heads, count), F32),
            ),
            (here, after(tok, mix_all)) + w_pieces + (qv_bias, row, seg_col),
            scratch=(pltpu.VMEM((width, n_qkv), BF16),),
            flops=2 * width * n_qkv * count,
        )
        att = lax.all_gather(attended, "cols", axis=0, tiled=True)
        mix_yc = over_rows(mix_y, near)
        m_pieces = (mix_all, mix_y, mix_c, mix_yc)

        wide_b = shaped((width, count), BF16)
        piece_b = shaped((width, part), BF16)
        piece_f = shaped((width, part), F32)
        (
            normed_two, grad_pre, active, grad_final, p1, p2, p3, own_two, own_hat, own_inv, own_hidden, up_sum, down_all,
        ) = run(
            functools.partial(middle_kernel, order),
            (
                wide_b, shaped((n_hid, count), BF16), shaped((n_hid, count), BF16), wide_b,
                piece_b, piece_b, piece_b, piece_f, piece_f,
                shaped((8, count), F32), shaped((feat, count), F32), shaped((n_hid, 1), F32), shaped((width, n_hid), BF16),
            ),
            (here, tok, att)
            + m_pieces
            + (up_weight, up_y, up_c, up_yc)
            + (down_weight, down_y, down_c, down_yc)
            + (cot, row, up_bias),
            scratch=(pltpu.VMEM((width, n_hid), BF16), pltpu.VMEM((width, count), F32)),
            flops=2 * width * count * (width + 3 * n_hid),
        )
        got = all_over_cols((p1, p2, p3))

        ff_send, ff_keep, out_send, out_keep = run(
            functools.partial(ff_grads_kernel, order),
            (
                shaped((2 * feat, 2 * n_hid), BF16), shaped((2 * feat, 2 * n_hid), F32),
                shaped((2 * feat, count), BF16), shaped((2 * feat, count), F32),
            ),
            (here, grad_final, active, normed_two, grad_pre, down_all),
            scratch=(pltpu.VMEM((width, count), BF16),),
            flops=2 * width * count * 3 * n_hid,
        )
        ff_keep, ff_send = halve(ff_keep, over_rows(ff_send, near))
        got[0], got[1], got[2], ff_keep, ff_send, out_send = together(*got, ff_keep, ff_send, out_send)
        ff_got = over_rows(ff_send, far)

        grad_hidden, grad_hidden_b, second, a0, a1, a2, a3 = run(
            functools.partial(second_back_kernel, order),
            (
                piece_f, piece_b, shaped((width, 8), F32),
                shaped((feat, part), BF16), shaped((feat, part), BF16), shaped((feat, part), BF16), shaped((feat, part), BF16),
            ),
            (here, tok, own_two) + tuple(got) + (own_hat, own_inv, grad_final) + m_pieces,
            scratch=(pltpu.VMEM((width, part), BF16),),
            flops=2 * width * part * width,
        )
        b1, b2, b3 = all_over_cols((a1, a2, a3))
        h_pieces = [grad_hidden_b] + all_over_cols((grad_hidden_b,) * 3)
        out_got = over_cols(after(out_send, grad_hidden_b), 1)
        ff_sum = ff_keep + ff_got.astype(F32)
        b1, b2, b3, ff_sum = together(b1, b2, b3, ff_sum)
        grad_ff = over_dp(ff_sum)

        grad_proj, qv_sum, s0, s1, s2, s3 = run(
            functools.partial(first_back_kernel, order, heads),
            (
                shaped((n_qkv, count), BF16), shaped((2 * head_rows, 1), F32),
                shaped((feat + 16, count), F32),
                shaped((feat + 16, count), BF16), shaped((feat + 16, count), BF16), shaped((feat + 16, count), BF16),
            ),
            (here, tok, stats, qkv, attended, totals, a0, b1, b2, b3, row, seg_col) + w_pieces + (grad_hidden, second),
            scratch=(pltpu.VMEM((head_rows, count), BF16), pltpu.VMEM((width, count), F32), pltpu.VMEM((width, 128), F32)),
            flops=2 * width * n_qkv * count,
        )
        got = all_over_cols((s1, s2, s3))

        last_ins = (here, normed_one, grad_proj, attended) + tuple(h_pieces)
        n_last = n_qkv + feat
        (last_send,) = run(
            functools.partial(last_send_kernel, order), (shaped((2 * feat, n_last), BF16),), last_ins,
            scratch=(pltpu.VMEM((2 * feat, count), BF16), pltpu.VMEM((2 * feat, count), BF16)),
            flops=width * count * n_last,
        )
        own, own_b, last_send = run(
            functools.partial(last_keep_kernel, order),
            (shaped((feat, n_last), F32), shaped((feat, n_last), BF16), shaped((feat, n_last), BF16)),
            last_ins + (over_rows(last_send, near),),
            scratch=(pltpu.VMEM((2 * feat, count), BF16), pltpu.VMEM((2 * feat, count), BF16)),
            flops=width * count * n_last,
        )
        pairs = [(at, at ^ 1) for at in range(n_dp)]
        far_dp = [(d * n_rows + r, (d ^ 1) * n_rows + (r ^ far)) for d in range(n_dp) for r in range(n_rows)]
        got_y = over_rows(last_send, far)
        if n_dp > 1:
            got_x = lax.ppermute(own_b, "dp", pairs)
            got_xy = lax.ppermute(last_send, ("dp", "rows"), far_dp)
        else:
            got_x = got_xy = jnp.zeros_like(got_y)
        grad_qkv, grad_mix = run(
            last_sum_kernel, (shaped((feat, n_qkv), F32), shaped((feat, feat), F32)), (here, own, got_y, got_x, got_xy)
        )
        for bit in bits_of(n_dp)[1:]:
            grad_qkv = grad_qkv + swap(grad_qkv.astype(BF16), "dp", n_dp, bit).astype(F32)
            grad_mix = grad_mix + swap(grad_mix.astype(BF16), "dp", n_dp, bit).astype(F32)

        (rest,) = run(rest_kernel, (shaped((8, width), F32),), (here, up_sum, qv_sum, cotangent, row))
        grad_tokens, sums = run(
            token_sum_kernel, (shaped((feat, count), F32), shaped((8, width), F32)), (here, s0) + tuple(got) + (rest,)
        )
        for axis, size in (("rows", n_rows), ("dp", n_dp)):
            for bit in bits_of(size):
                sums = sums + swap(sums, axis, size, bit)

        out_keep, out_send = halve(out_keep, out_got)
        output = own_hidden + down_col + out_keep + over_cols(out_send, 2).astype(F32)
        return (
            output.astype(BF16),
            grad_tokens,
            sums[3, :feat],
            sums[4, :feat],
            grad_qkv,
            sums[6, : 2 * head_rows],
            grad_mix,
            sums[2, :feat],
            sums[0, :feat],
            sums[1, :feat],
            grad_ff[:, n_hid:],
            sums[5, :n_hid],
            grad_ff[:, :n_hid],
            sums[7, :feat],
        )

    return body


def solution(mesh):
    sizes = mesh.shape
    body = make_body(sizes["dp"], sizes["rows"], sizes["cols"])

    return jax.shard_map(
        body,
        mesh=mesh,
        in_specs=(
            P("cols", ("dp", "rows")),
            P(("dp", "rows")),
            P("cols"),
            P("cols"),
            P("rows", "cols"),
            P("cols"),
            P("cols", "rows"),
            P("cols"),
            P("cols"),
            P("cols"),
            P("rows", "cols"),
            P("cols"),
            P("rows", "cols"),
            P("cols"),
            P("cols", ("dp", "rows")),
        ),
        out_specs=(
            P("cols", ("dp", "rows")),
            P("cols", ("dp", "rows")),
            P("cols"),
            P("cols"),
            P("rows", "cols"),
            P("cols"),
            P("cols", "rows"),
            P("cols"),
            P("cols"),
            P("cols"),
            P("rows", "cols"),
            P("cols"),
            P("rows", "cols"),
            P("cols"),
        ),
        check_vma=False,
    )
```

```python
import functools
import math

import jax
import jax.numpy as jnp
from jax import lax
from jax.experimental import pallas as pl
from jax.experimental.pallas import tpu as pltpu
from jax.sharding import PartitionSpec as P


HD = 64
MAXLEN = 256
EPS = 1e-05
NEG = -1e30
ROOT = 0.7978845608028654
CUBIC = 0.044715
F32 = jnp.float32
BF16 = jnp.bfloat16


def dot(left, right, dims):
    return lax.dot_general(left, right, (dims, ((), ())), preferred_element_type=F32)


def mm(left, right):
    return dot(left, right, ((1,), (0,)))


def mm_t(left, right):
    return dot(left, right, ((0,), (0,)))


def mm_nt(left, right):
    return dot(left, right, ((1,), (1,)))


def gelu_both(pre_act):
    inner_arg = ROOT * (pre_act + CUBIC * pre_act * pre_act * pre_act)
    tanh_val = jnp.tanh(inner_arg)
    value = 0.5 * pre_act * (1.0 + tanh_val)
    slope = 0.5 * (1.0 + tanh_val) + 0.5 * pre_act * (1.0 - tanh_val * tanh_val) * ROOT * (
        1.0 + 3.0 * CUBIC * pre_act * pre_act
    )
    return value, slope


def allowed_mask(seg_row, seg_col, width):
    key_pos = lax.broadcasted_iota(jnp.int32, (width, width), 0)
    query_pos = lax.broadcasted_iota(jnp.int32, (width, width), 1)
    same_seg = (seg_col == seg_row) & (seg_row >= 0)
    return (key_pos < query_pos) & same_seg | (key_pos == query_pos)


def block(index, size):
    return pl.ds(pl.multiple_of(index * size, size), size)


def norm_cols(tok_ref, count, which):
    start = tok_ref.shape[0] // 8
    cols = tok_ref[:, count : tok_ref.shape[1]].astype(F32)[:, start:]
    return [cols[:, k : k + 1] + cols[:, k + 5 : k + 6] + cols[:, k + 10 : k + 11] for k in which]


def run(kernel, outs, ins, scratch=(), flops=0, hold=True):
    specs = [pl.BlockSpec(memory_space=pltpu.SMEM)]
    specs += [pl.BlockSpec(memory_space=pltpu.VMEM)] * (len(ins) - 1)
    size = sum(math.prod(value.shape) * value.dtype.itemsize for value in list(ins) + list(outs))
    held = [pltpu.with_memory_space_constraint(value, pltpu.VMEM) if hold else value for value in ins[1:]]
    return pl.pallas_call(
        kernel,
        out_shape=[pltpu.VMEM(value.shape, value.dtype) for value in outs],
        in_specs=specs,
        out_specs=[pl.BlockSpec(memory_space=pltpu.VMEM)] * len(outs),
        scratch_shapes=list(scratch),
        cost_estimate=pl.CostEstimate(flops=flops, transcendentals=0, bytes_accessed=size),
        compiler_params=pltpu.CompilerParams(vmem_limit_bytes=24 * 1024 * 1024),
    )(ins[0], *held)


def shaped(shape, dtype):
    return jax.ShapeDtypeStruct(shape, dtype)


def column(row):
    return jnp.broadcast_to(row, (128, row.shape[1])).T[:, :1]


def pack_kernel(here, tok, mix, g1, b1, bm, g2, b2, down, seg, packed, down_col, seg_col):
    feat, count = tok.shape
    rows = jnp.concatenate([ref[...] for ref in (g1, b1, bm, g2, b2)], axis=0)
    high = rows.astype(BF16).astype(F32)
    middle = (rows - high).astype(BF16).astype(F32)
    low = rows - high - middle
    used = 3 * rows.shape[0]
    norms = jnp.concatenate([high, middle, low, jnp.zeros((128 - used, feat), F32)], axis=0).T
    half = feat // 2
    values = mix[...].astype(F32)
    values = jnp.where(here[2] == 0, values[:, :half], values[:, half:])
    packed[:, :count] = tok[...]
    packed[:, count:] = jnp.concatenate([values, norms[:, : 128 - half]], axis=1).astype(BF16)
    down_col[...] = column(down[...])
    seg_col[...] = column(seg[...].astype(F32)).astype(jnp.int32)


def first_kernel(order, heads, here, tok, w0, w1, w2, w3, qv, row, col, normed, stats, qkv, att, totals, w_all):
    feat = w0.shape[0]
    count = row.shape[1]
    for value, piece in zip(order, (w0, w1, w2, w3)):
        w_all[block(here[0] ^ value, feat), :] = piece[...]
    gain, shift = norm_cols(tok, count, (0, 1))
    values = tok[:, :count].astype(F32)
    mean = jnp.mean(values, axis=0, keepdims=True)
    inv = lax.rsqrt(jnp.mean(values * values, axis=0, keepdims=True) - mean * mean + EPS)
    stats[0:1, :] = mean
    stats[1:2, :] = inv
    normed[...] = ((values - mean) * inv * gain + shift).astype(BF16)
    head_rows = heads * HD
    qv_col = column(qv[...].reshape(1, 2 * head_rows))
    bias = jnp.concatenate([qv_col[:head_rows], jnp.zeros((head_rows, 1), F32), qv_col[head_rows:]], axis=0)
    qkv[...] = (mm_t(w_all[...], normed[...]) + bias).astype(BF16)
    scale = 1.0 / math.sqrt(HD)
    width = min(MAXLEN, count)
    for half in range(count // width):
        cols = pl.ds(half * width, width)
        allowed = allowed_mask(row[:, cols], col[cols, :], width)
        for head in range(heads):
            query = qkv[pl.ds(head * HD, HD), cols]
            keys = qkv[pl.ds(head_rows + head * HD, HD), cols]
            held = qkv[pl.ds(2 * head_rows + head * HD, HD), cols]
            scores = jnp.where(allowed, mm_t(keys, query) * scale, NEG)
            top = jnp.max(scores, axis=0, keepdims=True)
            log_total = top + jnp.log(jnp.sum(jnp.exp(scores - top), axis=0, keepdims=True))
            probs = jnp.exp(scores - log_total).astype(BF16)
            att[pl.ds(head * HD, HD), cols] = mm(held, probs).astype(BF16)
            totals[pl.ds(head, 1), cols] = log_total


def mix_pack_kernel(here, own, got, out):
    half = out.shape[1] // 2
    mine, other = own[...].astype(F32)[:, :half], got[...].astype(F32)[:, :half]
    first = jnp.where(here[2] == 0, mine, other)
    second = jnp.where(here[2] == 0, other, mine)
    out[...] = jnp.concatenate([first, second], axis=1).astype(BF16)


def middle_kernel(
    order, here, tok, att, m0, m1, m2, m3, u0, u1, u2, u3, d0, d1, d2, d3, c0, c1, c2, c3, row, up,
    normed, grad_pre, active, grad_final, p1, p2, p3, own_two, own_hat, own_inv, own_hidden, up_sum, down_all,
    up_all, hidden,
):
    feat, count = own_hidden.shape
    part = own_two.shape[1]
    live = row[...] >= 0
    bias_mix, gain, shift = norm_cols(tok, count, (2, 3, 4))
    for value, piece in zip(order, (u0, u1, u2, u3)):
        up_all[block(here[0] ^ value, feat), :] = piece[...]
    for value, piece in zip(order, (d0, d1, d2, d3)):
        down_all[block(here[0] ^ value, feat), :] = piece[...]
    for step, piece in enumerate((c0, c1, c2, c3)):
        masked = jnp.where(live, piece[...].astype(F32), 0.0)
        grad_final[block(here[1] ^ step, feat), :] = masked.astype(BF16)
    for value, piece in zip(order, (m0, m1, m2, m3)):
        hidden[block(here[0] ^ value, feat), :] = mm_t(piece[...], att[...])
    hidden[...] = hidden[...] + tok[:, :count].astype(F32) + bias_mix
    values = hidden[...]
    mean = jnp.mean(values, axis=0, keepdims=True)
    inv = lax.rsqrt(jnp.mean(values * values, axis=0, keepdims=True) - mean * mean + EPS)
    own_hidden[...] = hidden[block(here[1], feat), :]
    hat = (values - mean) * inv
    normed[...] = (hat * gain + shift).astype(BF16)
    hidden[...] = hat
    own_inv[...] = jnp.broadcast_to(inv, (8, count))
    own_hat[...] = hidden[:, block(here[1], part)]
    value, slope = gelu_both(mm_t(up_all[...], normed[...]) + column(up[...].reshape(1, up.shape[0])))
    active[...] = value.astype(BF16)
    grad = mm_t(down_all[...], grad_final[...]) * slope
    grad_pre[...] = grad.astype(BF16)
    up_sum[...] = jnp.sum(grad_pre[...].astype(F32), axis=1, keepdims=True)
    hidden[...] = mm(up_all[...], grad_pre[...])
    own_two[...] = hidden[:, block(here[1], part)]
    for step, out in enumerate((p1, p2, p3)):
        out[...] = hidden[:, block(here[1] ^ (step + 1), part)].astype(BF16)


def in_order(order, here, target, source):
    feat = target.shape[0] // len(order)
    for at, value in enumerate(order):
        target[pl.ds(at * feat, feat), :] = source[block(here[0] ^ value, feat), :]


def ff_grads_kernel(
    order, here, grad_final, active, normed, grad_pre, down_all, send, keep, out_send, out_keep, rows
):
    half = keep.shape[0]
    feat = half // 2
    hid = active.shape[0]
    in_order(order, here, rows, grad_final)
    down = mm_nt(rows[...], active[...])
    keep[:, :hid] = down[:half]
    send[:, :hid] = down[half:].astype(BF16)
    in_order(order, here, rows, normed)
    up = mm_nt(rows[...], grad_pre[...])
    keep[:, hid:] = up[:half]
    send[:, hid:] = up[half:].astype(BF16)
    for step in (0, 2):
        out_keep[pl.ds(step // 2 * feat, feat), :] = mm(down_all[block(here[1] ^ step, feat), :], active[...])
        out = mm(down_all[block(here[1] ^ (step + 1), feat), :], active[...])
        out_send[pl.ds(step // 2 * feat, feat), :] = out.astype(BF16)


def second_back_kernel(
    order, here, tok, own_two, r1, r2, r3, own_hat, own_inv, grad_final, m0, m1, m2, m3,
    grad_hidden, grad_hidden_b, sums, a0, a1, a2, a3, all_att,
):
    feat = a0.shape[0]
    part = own_two.shape[1]
    (gain,) = norm_cols(tok, grad_final.shape[1], (3,))
    grad = own_two[...] + r1[...].astype(F32) + r2[...].astype(F32) + r3[...].astype(F32)
    sums[:, 1:2] = jnp.sum(grad, axis=1, keepdims=True)
    hat = own_hat[...]
    lanes = block(here[1], part)
    inv = own_inv[:, lanes][:1]
    scaled = grad * gain
    out = grad_final[:, lanes].astype(F32) + inv * (
        scaled
        - jnp.mean(scaled, axis=0, keepdims=True)
        - hat * jnp.mean(scaled * hat, axis=0, keepdims=True)
    )
    grad_hidden[...] = out
    grad_hidden_b[...] = out.astype(BF16)
    sums[:, 0:1] = jnp.sum(grad * hat, axis=1, keepdims=True)
    sums[:, 2:3] = jnp.sum(out, axis=1, keepdims=True)
    total = jnp.zeros(all_att.shape, F32)
    for value, piece in zip(order, (m0, m1, m2, m3)):
        total += mm(piece[...], grad_hidden_b[block(here[0] ^ value, feat), :])
    all_att[...] = total.astype(BF16)
    for step, ref in enumerate((a0, a1, a2, a3)):
        ref[...] = all_att[block(here[1] ^ step, feat), :]


def first_back_kernel(
    order, heads, here, tok, stats, qkv, att, totals, a0, a1, a2, a3, row, col, w0, w1, w2, w3, grad_hidden, second,
    grad_proj, qv_sum, s0, s1, s2, s3, grad_att, share, sums,
):
    feat, count = att.shape
    part = a0.shape[1]
    head_rows = heads * HD
    scale = 1.0 / math.sqrt(HD)
    for step, piece in enumerate((a0, a1, a2, a3)):
        grad_att[:, block(here[1] ^ step, part)] = piece[...]
    width = min(MAXLEN, count)
    for half in range(count // width):
        cols = pl.ds(half * width, width)
        allowed = allowed_mask(row[:, cols], col[cols, :], width)
        for head in range(heads):
            query = qkv[pl.ds(head * HD, HD), cols]
            keys = qkv[pl.ds(head_rows + head * HD, HD), cols]
            held = qkv[pl.ds(2 * head_rows + head * HD, HD), cols]
            grad = grad_att[pl.ds(head * HD, HD), cols]
            attended = att[pl.ds(head * HD, HD), cols]
            delta = jnp.sum(grad.astype(F32) * attended.astype(F32), axis=0, keepdims=True)
            scores = jnp.where(allowed, mm_t(keys, query) * scale, NEG)
            probs = jnp.exp(scores - totals[pl.ds(head, 1), cols])
            grad_held = mm_nt(grad, probs.astype(BF16))
            grad_probs = mm_t(held, grad)
            grad_scores = (probs * (grad_probs - delta) * scale).astype(BF16)
            grad_query = mm(keys, grad_scores)
            grad_keys = mm_nt(query, grad_scores)
            grad_proj[pl.ds(head * HD, HD), cols] = grad_query.astype(BF16)
            grad_proj[pl.ds(head_rows + head * HD, HD), cols] = grad_keys.astype(BF16)
            grad_proj[pl.ds(2 * head_rows + head * HD, HD), cols] = grad_held.astype(BF16)
            for at, grown in ((head * HD, grad_query), (head_rows + head * HD, grad_held)):
                total = jnp.sum(grown, axis=1, keepdims=True)
                if half:
                    total = total + qv_sum[pl.ds(at, HD), :]
                qv_sum[pl.ds(at, HD), :] = total
    for value, piece in zip(order, (w0, w1, w2, w3)):
        share[block(here[0] ^ value, feat), :] = mm(piece[...], grad_proj[...])
    (gain,) = norm_cols(tok, count, (0,))
    inv = stats[1:2, :]
    hat = (tok[:, :count].astype(F32) - stats[0:1, :]) * inv
    grad = share[...]
    lane = lax.broadcasted_iota(jnp.int32, sums.shape, 1)
    columns = [second[:, k : k + 1] for k in range(3)]
    columns += [jnp.sum(grad * hat, axis=1, keepdims=True), jnp.sum(grad, axis=1, keepdims=True)]
    total = jnp.zeros(sums.shape, F32)
    for at, values in enumerate(columns):
        total = jnp.where(lane == at, values, total)
    sums[...] = total
    scaled = grad * gain
    share[...] = inv * (
        scaled
        - jnp.mean(scaled, axis=0, keepdims=True)
        - hat * jnp.mean(scaled * hat, axis=0, keepdims=True)
    )
    share[:, block(here[1], part)] += grad_hidden[...]
    for step, ref in enumerate((s0, s1, s2, s3)):
        rows = block(here[1] ^ step, feat)
        extra = ref.shape[0] - feat
        ref[:feat, :] = share[rows, :].astype(ref.dtype)
        ref[feat:, :feat] = sums[rows, :].T[:extra].astype(ref.dtype)


def last_grads(pair, here, normed, grad_proj, att, pieces, rows, hidden):
    feat, count = att.shape
    part = count // len(pieces)
    for at, value in enumerate(pair):
        source = block(here[0] ^ value, feat)
        target = pl.ds(at * feat, feat)
        rows[target, :] = normed[source, :]
        for step, ref in enumerate(pieces):
            hidden[target, block(here[1] ^ step, part)] = ref[source, :]
    return mm_nt(rows[...], grad_proj[...]), mm_nt(hidden[...], att[...])


def last_send_kernel(order, here, normed, grad_proj, att, h0, h1, h2, h3, send, rows, hidden):
    split = grad_proj.shape[0]
    qkv, mix = last_grads(order[2:], here, normed, grad_proj, att, (h0, h1, h2, h3), rows, hidden)
    send[:, :split] = qkv.astype(BF16)
    send[:, split:] = mix.astype(BF16)


def last_keep_kernel(order, here, normed, grad_proj, att, h0, h1, h2, h3, got, own, own_b, send, rows, hidden):
    feat = att.shape[0]
    split = grad_proj.shape[0]
    qkv, mix = last_grads(order[:2], here, normed, grad_proj, att, (h0, h1, h2, h3), rows, hidden)
    qkv += got[:, :split].astype(F32)
    mix += got[:, split:].astype(F32)
    own[:, :split] = qkv[:feat]
    own[:, split:] = mix[:feat]
    own_b[:, :split] = qkv[:feat].astype(BF16)
    own_b[:, split:] = mix[:feat].astype(BF16)
    send[:, :split] = qkv[feat:].astype(BF16)
    send[:, split:] = mix[feat:].astype(BF16)


def rest_kernel(here, up_sum, qv_sum, cot, row, rest):
    width = up_sum.shape[0]
    feat = cot.shape[0]
    down = jnp.sum(jnp.where(row[...] >= 0, cot[...].astype(F32), 0.0), axis=1, keepdims=True)
    down = jnp.concatenate([down, jnp.zeros((width - feat, 1), F32)], axis=0)
    held = jnp.concatenate([qv_sum[...], jnp.zeros((width - qv_sum.shape[0], 1), F32)], axis=0)
    lane = lax.broadcasted_iota(jnp.int32, (width, 128), 1)
    total = jnp.zeros((width, 128), F32)
    for at, values in ((5, up_sum[...]), (6, held), (7, down)):
        total = jnp.where(lane == at, values, total)
    rest[...] = total.T[:8]


def token_sum_kernel(here, s0, g1, g2, g3, rest, out, sums):
    feat = out.shape[0]
    total = s0[...]
    for ref in (g1, g2, g3):
        total += ref[...].astype(F32)
    out[...] = total[:feat]
    sums[...] = rest[...]
    sums[:5, :feat] = total[feat : feat + 5, :feat]


def last_sum_kernel(here, own, got_y, got_x, got_xy, qkv, mix):
    split = qkv.shape[1]
    total = own[...] + got_y[...].astype(F32) + got_x[...].astype(F32) + got_xy[...].astype(F32)
    qkv[...] = total[:, :split]
    mix[...] = total[:, split:].T


def halve_kernel(here, keep, got, kept, send):
    half = kept.shape[0]
    kept[...] = keep[:half] + got[:half].astype(F32)
    send[...] = (keep[half:] + got[half:].astype(F32)).astype(BF16)


def bits_of(size):
    bits, bit = [], 1
    while bit < size:
        bits.append(bit)
        bit *= 2
    return bits


def swap(values, axis, size, bit):
    return lax.ppermute(values, axis, [(at, at ^ bit) for at in range(size)])


def after(value, *others):
    return lax.optimization_barrier((value,) + others)[0]


def together(*values):
    return lax.optimization_barrier(values)


def make_body(n_dp, n_rows, n_cols):
    assert n_rows == 4 and n_cols == 4 and n_dp % 2 == 0
    far, near = 2, 1
    order = (0, far, near, far ^ near)

    def over_rows(value, bit):
        return swap(value, "rows", n_rows, bit)

    def over_cols(value, bit):
        return swap(value, "cols", n_cols, bit)

    def all_over_cols(values):
        return [over_cols(value, bit) for value, bit in zip(values, (1, 2, 3))]

    def over_dp(value):
        value = value.astype(BF16).astype(F32)
        for bit in bits_of(n_dp):
            value = value + swap(value.astype(BF16), "dp", n_dp, bit).astype(F32)
        return value

    def body(
        tokens,
        segment_ids,
        first_gain,
        first_bias,
        qkv_weight,
        qv_bias,
        mix_weight,
        mix_bias,
        second_gain,
        second_bias,
        up_weight,
        up_bias,
        down_weight,
        down_bias,
        cotangent,
    ):
        feat, count = tokens.shape
        width = feat * n_cols
        part = count // n_cols
        n_qkv = qkv_weight.shape[1]
        n_hid = up_weight.shape[1]
        heads = n_qkv // (3 * HD)
        head_rows = heads * HD
        here = [lax.axis_index("rows"), lax.axis_index("cols"), lax.axis_index("dp") & 1]
        here = jnp.stack(here).astype(jnp.int32)
        row = segment_ids.reshape(1, count)

        def halve(keep, got):
            half = (keep.shape[0] // 2,) + keep.shape[1:]
            return run(halve_kernel, (shaped(half, F32), shaped(half, BF16)), (here, keep, got))

        qkv_y = over_rows(qkv_weight, far)
        up_y, down_y = over_rows(up_weight, far), over_rows(down_weight, far)
        qkv_c, up_c, down_c = [over_rows(value, near) for value in (qkv_weight, up_weight, down_weight)]
        packed, down_col, seg_col = run(
            pack_kernel,
            (shaped((feat, count + 128), BF16), shaped((feat, 1), F32), shaped((count, 1), jnp.int32)),
            (here, tokens, mix_weight)
            + tuple(
                value.reshape(1, -1)
                for value in (first_gain, first_bias, mix_bias, second_gain, second_bias, down_bias, segment_ids)
            ),
            hold=False,
        )
        tok = lax.all_gather(packed, "cols", axis=0, tiled=True)
        qkv_yc = over_rows(qkv_y, near)
        w_pieces = (qkv_weight, qkv_y, qkv_c, qkv_yc)
        cot_own = after(cotangent, tok)
        cot_z = all_over_cols((cot_own,) * 3)
        mix_half = tok[:, count:]
        pairs = [(at, at ^ 1) for at in range(n_dp)]
        mix_got = lax.ppermute(mix_half, "dp", pairs)
        (mix_all,) = run(mix_pack_kernel, (shaped((width, feat), BF16),), (here, mix_half, mix_got))
        mix_y, mix_c = over_rows(mix_all, far), over_rows(mix_all, near)
        up_yc, down_yc = over_rows(up_y, near), over_rows(down_y, near)

        normed_one, stats, qkv, attended, totals = run(
            functools.partial(first_kernel, order, heads),
            (
                shaped((width, count), BF16),
                shaped((2, count), F32),
                shaped((n_qkv, count), BF16),
                shaped((head_rows, count), BF16),
                shaped((heads, count), F32),
            ),
            (here, tok) + w_pieces + (qv_bias, row, seg_col),
            scratch=(pltpu.VMEM((width, n_qkv), BF16),),
            flops=2 * width * n_qkv * count,
        )
        att = lax.all_gather(attended, "cols", axis=0, tiled=True)
        mix_yc = over_rows(mix_y, near)
        m_pieces = (mix_all, mix_y, mix_c, mix_yc)

        wide_b = shaped((width, count), BF16)
        piece_b = shaped((width, part), BF16)
        piece_f = shaped((width, part), F32)
        (
            normed_two, grad_pre, active, grad_final, p1, p2, p3, own_two, own_hat, own_inv, own_hidden, up_sum, down_all,
        ) = run(
            functools.partial(middle_kernel, order),
            (
                wide_b, shaped((n_hid, count), BF16), shaped((n_hid, count), BF16), wide_b,
                piece_b, piece_b, piece_b, piece_f, piece_f,
                shaped((8, count), F32), shaped((feat, count), F32), shaped((n_hid, 1), F32), shaped((width, n_hid), BF16),
            ),
            (here, tok, att)
            + m_pieces
            + (up_weight, up_y, up_c, up_yc)
            + (down_weight, down_y, down_c, down_yc)
            + (cotangent,)
            + tuple(cot_z)
            + (row, up_bias),
            scratch=(pltpu.VMEM((width, n_hid), BF16), pltpu.VMEM((width, count), F32)),
            flops=2 * width * count * (width + 3 * n_hid),
        )
        got = all_over_cols((p1, p2, p3))

        ff_send, ff_keep, out_send, out_keep = run(
            functools.partial(ff_grads_kernel, order),
            (
                shaped((2 * feat, 2 * n_hid), BF16), shaped((2 * feat, 2 * n_hid), F32),
                shaped((2 * feat, count), BF16), shaped((2 * feat, count), F32),
            ),
            (here, grad_final, active, normed_two, grad_pre, down_all),
            scratch=(pltpu.VMEM((width, count), BF16),),
            flops=2 * width * count * 3 * n_hid,
        )
        ff_keep, ff_send = halve(ff_keep, over_rows(ff_send, near))
        got[0], got[1], got[2], ff_keep, ff_send, out_send = together(*got, ff_keep, ff_send, out_send)
        ff_got = over_rows(ff_send, far)

        grad_hidden, grad_hidden_b, second, a0, a1, a2, a3 = run(
            functools.partial(second_back_kernel, order),
            (
                piece_f, piece_b, shaped((width, 8), F32),
                shaped((feat, part), BF16), shaped((feat, part), BF16), shaped((feat, part), BF16), shaped((feat, part), BF16),
            ),
            (here, tok, own_two) + tuple(got) + (own_hat, own_inv, grad_final) + m_pieces,
            scratch=(pltpu.VMEM((width, part), BF16),),
            flops=2 * width * part * width,
        )
        b1, b2, b3 = all_over_cols((a1, a2, a3))
        h_pieces = [grad_hidden_b] + all_over_cols((grad_hidden_b,) * 3)
        out_got = over_cols(after(out_send, grad_hidden_b), 1)
        ff_sum = ff_keep + ff_got.astype(F32)
        b1, b2, b3, ff_sum = together(b1, b2, b3, ff_sum)
        grad_ff = over_dp(ff_sum)

        grad_proj, qv_sum, s0, s1, s2, s3 = run(
            functools.partial(first_back_kernel, order, heads),
            (
                shaped((n_qkv, count), BF16), shaped((2 * head_rows, 1), F32),
                shaped((feat + 16, count), F32),
                shaped((feat + 16, count), BF16), shaped((feat + 16, count), BF16), shaped((feat + 16, count), BF16),
            ),
            (here, tok, stats, qkv, attended, totals, a0, b1, b2, b3, row, seg_col) + w_pieces + (grad_hidden, second),
            scratch=(pltpu.VMEM((head_rows, count), BF16), pltpu.VMEM((width, count), F32), pltpu.VMEM((width, 128), F32)),
            flops=2 * width * n_qkv * count,
        )
        got = all_over_cols((s1, s2, s3))

        last_ins = (here, normed_one, grad_proj, attended) + tuple(h_pieces)
        n_last = n_qkv + feat
        (last_send,) = run(
            functools.partial(last_send_kernel, order), (shaped((2 * feat, n_last), BF16),), last_ins,
            scratch=(pltpu.VMEM((2 * feat, count), BF16), pltpu.VMEM((2 * feat, count), BF16)),
            flops=width * count * n_last,
        )
        own, own_b, last_send = run(
            functools.partial(last_keep_kernel, order),
            (shaped((feat, n_last), F32), shaped((feat, n_last), BF16), shaped((feat, n_last), BF16)),
            last_ins + (over_rows(last_send, near),),
            scratch=(pltpu.VMEM((2 * feat, count), BF16), pltpu.VMEM((2 * feat, count), BF16)),
            flops=width * count * n_last,
        )
        far_dp = [(d * n_rows + r, (d ^ 1) * n_rows + (r ^ far)) for d in range(n_dp) for r in range(n_rows)]
        got_y = over_rows(last_send, far)
        if n_dp > 1:
            got_x = lax.ppermute(own_b, "dp", pairs)
            got_xy = lax.ppermute(last_send, ("dp", "rows"), far_dp)
        else:
            got_x = got_xy = jnp.zeros_like(got_y)
        grad_qkv, grad_mix = run(
            last_sum_kernel, (shaped((feat, n_qkv), F32), shaped((feat, feat), F32)), (here, own, got_y, got_x, got_xy)
        )
        for bit in bits_of(n_dp)[1:]:
            grad_qkv = grad_qkv + swap(grad_qkv.astype(BF16), "dp", n_dp, bit).astype(F32)
            grad_mix = grad_mix + swap(grad_mix.astype(BF16), "dp", n_dp, bit).astype(F32)

        (rest,) = run(rest_kernel, (shaped((8, width), F32),), (here, up_sum, qv_sum, cotangent, row))
        grad_tokens, sums = run(
            token_sum_kernel, (shaped((feat, count), F32), shaped((8, width), F32)), (here, s0) + tuple(got) + (rest,)
        )
        for axis, size in (("rows", n_rows), ("dp", n_dp)):
            for bit in bits_of(size):
                sums = sums + swap(sums, axis, size, bit)

        out_keep, out_send = halve(out_keep, out_got)
        output = own_hidden + down_col + out_keep + over_cols(out_send, 2).astype(F32)
        return (
            output.astype(BF16),
            grad_tokens,
            sums[3, :feat],
            sums[4, :feat],
            grad_qkv,
            sums[6, : 2 * head_rows],
            grad_mix,
            sums[2, :feat],
            sums[0, :feat],
            sums[1, :feat],
            grad_ff[:, n_hid:],
            sums[5, :n_hid],
            grad_ff[:, :n_hid],
            sums[7, :feat],
        )

    return body


def solution(mesh):
    sizes = mesh.shape
    body = make_body(sizes["dp"], sizes["rows"], sizes["cols"])

    return jax.shard_map(
        body,
        mesh=mesh,
        in_specs=(
            P("cols", ("dp", "rows")),
            P(("dp", "rows")),
            P("cols"),
            P("cols"),
            P("rows", "cols"),
            P("cols"),
            P("cols", "rows"),
            P("cols"),
            P("cols"),
            P("cols"),
            P("rows", "cols"),
            P("cols"),
            P("rows", "cols"),
            P("cols"),
            P("cols", ("dp", "rows")),
        ),
        out_specs=(
            P("cols", ("dp", "rows")),
            P("cols", ("dp", "rows")),
            P("cols"),
            P("cols"),
            P("rows", "cols"),
            P("cols"),
            P("cols", "rows"),
            P("cols"),
            P("cols"),
            P("cols"),
            P("rows", "cols"),
            P("cols"),
            P("rows", "cols"),
            P("cols"),
        ),
        check_vma=False,
    )
```

```python
import functools
import math

import jax
import jax.numpy as jnp
from jax import lax
from jax.experimental import pallas as pl
from jax.experimental.pallas import tpu as pltpu
from jax.sharding import PartitionSpec as P


HD = 64
MAXLEN = 256
EPS = 1e-05
NEG = -1e30
ROOT = 0.7978845608028654
CUBIC = 0.044715
F32 = jnp.float32
BF16 = jnp.bfloat16


def dot(left, right, dims):
    return lax.dot_general(left, right, (dims, ((), ())), preferred_element_type=F32)


def mm(left, right):
    return dot(left, right, ((1,), (0,)))


def mm_t(left, right):
    return dot(left, right, ((0,), (0,)))


def mm_nt(left, right):
    return dot(left, right, ((1,), (1,)))


def gelu_both(pre_act):
    inner_arg = ROOT * (pre_act + CUBIC * pre_act * pre_act * pre_act)
    tanh_val = jnp.tanh(inner_arg)
    value = 0.5 * pre_act * (1.0 + tanh_val)
    slope = 0.5 * (1.0 + tanh_val) + 0.5 * pre_act * (1.0 - tanh_val * tanh_val) * ROOT * (
        1.0 + 3.0 * CUBIC * pre_act * pre_act
    )
    return value, slope


def allowed_mask(seg_row, seg_col, width):
    key_pos = lax.broadcasted_iota(jnp.int32, (width, width), 0)
    query_pos = lax.broadcasted_iota(jnp.int32, (width, width), 1)
    same_seg = (seg_col == seg_row) & (seg_row >= 0)
    return (key_pos < query_pos) & same_seg | (key_pos == query_pos)


def block(index, size):
    return pl.ds(pl.multiple_of(index * size, size), size)


def norm_cols(tok_ref, count, which):
    start = tok_ref.shape[0] // 8
    cols = tok_ref[:, count : tok_ref.shape[1]].astype(F32)[:, start:]
    return [cols[:, k : k + 1] + cols[:, k + 5 : k + 6] + cols[:, k + 10 : k + 11] for k in which]


def run(kernel, outs, ins, scratch=(), flops=0, hold=True, limit=24):
    specs = [pl.BlockSpec(memory_space=pltpu.SMEM)]
    specs += [pl.BlockSpec(memory_space=pltpu.VMEM)] * (len(ins) - 1)
    size = sum(math.prod(value.shape) * value.dtype.itemsize for value in list(ins) + list(outs))
    held = [pltpu.with_memory_space_constraint(value, pltpu.VMEM) if hold else value for value in ins[1:]]
    return pl.pallas_call(
        kernel,
        out_shape=[pltpu.VMEM(value.shape, value.dtype) for value in outs],
        in_specs=specs,
        out_specs=[pl.BlockSpec(memory_space=pltpu.VMEM)] * len(outs),
        scratch_shapes=list(scratch),
        cost_estimate=pl.CostEstimate(flops=flops, transcendentals=0, bytes_accessed=size),
        compiler_params=pltpu.CompilerParams(vmem_limit_bytes=limit * 1024 * 1024),
    )(ins[0], *held)


def shaped(shape, dtype):
    return jax.ShapeDtypeStruct(shape, dtype)


def column(row):
    return jnp.broadcast_to(row, (128, row.shape[1])).T[:, :1]


def pack_kernel(here, tok, mix, g1, b1, bm, g2, b2, down, seg, packed, down_col, seg_col):
    feat, count = tok.shape
    rows = jnp.concatenate([ref[...] for ref in (g1, b1, bm, g2, b2)], axis=0)
    high = rows.astype(BF16).astype(F32)
    middle = (rows - high).astype(BF16).astype(F32)
    low = rows - high - middle
    used = 3 * rows.shape[0]
    norms = jnp.concatenate([high, middle, low, jnp.zeros((128 - used, feat), F32)], axis=0).T
    half = feat // 2
    values = mix[...].astype(F32)
    values = jnp.where(here[2] == 0, values[:, :half], values[:, half:])
    packed[:, :count] = tok[...]
    packed[:, count:] = jnp.concatenate([values, norms[:, : 128 - half]], axis=1).astype(BF16)
    down_col[...] = column(down[...])
    seg_col[...] = column(seg[...].astype(F32)).astype(jnp.int32)


def first_kernel(order, heads, here, tok, w0, w1, w2, w3, qv, row, col, normed, stats, qkv, att, totals, w_all):
    feat = w0.shape[0]
    count = row.shape[1]
    for value, piece in zip(order, (w0, w1, w2, w3)):
        w_all[block(here[0] ^ value, feat), :] = piece[...]
    gain, shift = norm_cols(tok, count, (0, 1))
    values = tok[:, :count].astype(F32)
    mean = jnp.mean(values, axis=0, keepdims=True)
    inv = lax.rsqrt(jnp.mean(values * values, axis=0, keepdims=True) - mean * mean + EPS)
    stats[0:1, :] = mean
    stats[1:2, :] = inv
    normed[...] = ((values - mean) * inv * gain + shift).astype(BF16)
    head_rows = heads * HD
    qv_col = column(qv[...].reshape(1, 2 * head_rows))
    bias = jnp.concatenate([qv_col[:head_rows], jnp.zeros((head_rows, 1), F32), qv_col[head_rows:]], axis=0)
    qkv[...] = (mm_t(w_all[...], normed[...]) + bias).astype(BF16)
    scale = 1.0 / math.sqrt(HD)
    width = min(MAXLEN, count)
    for half in range(count // width):
        cols = pl.ds(half * width, width)
        allowed = allowed_mask(row[:, cols], col[cols, :], width)
        for head in range(heads):
            query = qkv[pl.ds(head * HD, HD), cols]
            keys = qkv[pl.ds(head_rows + head * HD, HD), cols]
            held = qkv[pl.ds(2 * head_rows + head * HD, HD), cols]
            scores = jnp.where(allowed, mm_t(keys, query) * scale, NEG)
            top = jnp.max(scores, axis=0, keepdims=True)
            log_total = top + jnp.log(jnp.sum(jnp.exp(scores - top), axis=0, keepdims=True))
            probs = jnp.exp(scores - log_total).astype(BF16)
            att[pl.ds(head * HD, HD), cols] = mm(held, probs).astype(BF16)
            totals[pl.ds(head, 1), cols] = log_total


def mix_pack_kernel(here, own, got, out):
    half = out.shape[1] // 2
    mine, other = own[...].astype(F32)[:, :half], got[...].astype(F32)[:, :half]
    first = jnp.where(here[2] == 0, mine, other)
    second = jnp.where(here[2] == 0, other, mine)
    out[...] = jnp.concatenate([first, second], axis=1).astype(BF16)


def middle_kernel(
    order, here, tok, att, m0, m1, m2, m3, u0, u1, u2, u3, d0, d1, d2, d3, c0, c1, c2, c3, row, up,
    normed, grad_pre, active, grad_final, p1, p2, p3, own_two, own_hat, own_inv, own_hidden, up_sum, down_all,
    up_all, hidden,
):
    feat, count = own_hidden.shape
    part = own_two.shape[1]
    live = row[...] >= 0
    bias_mix, gain, shift = norm_cols(tok, count, (2, 3, 4))
    for value, piece in zip(order, (u0, u1, u2, u3)):
        up_all[block(here[0] ^ value, feat), :] = piece[...]
    for value, piece in zip(order, (d0, d1, d2, d3)):
        down_all[block(here[0] ^ value, feat), :] = piece[...]
    for step, piece in enumerate((c0, c1, c2, c3)):
        masked = jnp.where(live, piece[...].astype(F32), 0.0)
        grad_final[block(here[1] ^ step, feat), :] = masked.astype(BF16)
    for value, piece in zip(order, (m0, m1, m2, m3)):
        hidden[block(here[0] ^ value, feat), :] = mm_t(piece[...], att[...])
    hidden[...] = hidden[...] + tok[:, :count].astype(F32) + bias_mix
    values = hidden[...]
    mean = jnp.mean(values, axis=0, keepdims=True)
    inv = lax.rsqrt(jnp.mean(values * values, axis=0, keepdims=True) - mean * mean + EPS)
    own_hidden[...] = hidden[block(here[1], feat), :]
    hat = (values - mean) * inv
    normed[...] = (hat * gain + shift).astype(BF16)
    hidden[...] = hat
    own_inv[...] = jnp.broadcast_to(inv, (8, count))
    own_hat[...] = hidden[:, block(here[1], part)]
    value, slope = gelu_both(mm_t(up_all[...], normed[...]) + column(up[...].reshape(1, up.shape[0])))
    active[...] = value.astype(BF16)
    grad = mm_t(down_all[...], grad_final[...]) * slope
    grad_pre[...] = grad.astype(BF16)
    up_sum[...] = jnp.sum(grad_pre[...].astype(F32), axis=1, keepdims=True)
    hidden[...] = mm(up_all[...], grad_pre[...])
    own_two[...] = hidden[:, block(here[1], part)]
    for step, out in enumerate((p1, p2, p3)):
        out[...] = hidden[:, block(here[1] ^ (step + 1), part)].astype(BF16)


def in_order(order, here, target, source):
    feat = target.shape[0] // len(order)
    for at, value in enumerate(order):
        target[pl.ds(at * feat, feat), :] = source[block(here[0] ^ value, feat), :]


def ff_grads_kernel(
    order, here, grad_final, active, normed, grad_pre, send, keep, rows
):
    half = keep.shape[0]
    hid = active.shape[0]
    in_order(order, here, rows, grad_final)
    down = mm_nt(rows[...], active[...])
    keep[:, :hid] = down[:half]
    send[:, :hid] = down[half:].astype(BF16)
    in_order(order, here, rows, normed)
    up = mm_nt(rows[...], grad_pre[...])
    keep[:, hid:] = up[:half]
    send[:, hid:] = up[half:].astype(BF16)


def out_parts_kernel(here, down_all, active, out_send, out_keep):
    feat = out_keep.shape[0] // 2
    for step in (0, 2):
        out_keep[pl.ds(step // 2 * feat, feat), :] = mm(down_all[block(here[1] ^ step, feat), :], active[...])
        out = mm(down_all[block(here[1] ^ (step + 1), feat), :], active[...])
        out_send[pl.ds(step // 2 * feat, feat), :] = out.astype(BF16)


def second_back_kernel(
    order, here, tok, own_two, r1, r2, r3, own_hat, own_inv, grad_final, m0, m1, m2, m3,
    grad_hidden, grad_hidden_b, sums, a0, a1, a2, a3, all_att,
):
    feat = a0.shape[0]
    part = own_two.shape[1]
    (gain,) = norm_cols(tok, grad_final.shape[1], (3,))
    grad = own_two[...] + r1[...].astype(F32) + r2[...].astype(F32) + r3[...].astype(F32)
    sums[:, 1:2] = jnp.sum(grad, axis=1, keepdims=True)
    hat = own_hat[...]
    lanes = block(here[1], part)
    inv = own_inv[:, lanes][:1]
    scaled = grad * gain
    out = grad_final[:, lanes].astype(F32) + inv * (
        scaled
        - jnp.mean(scaled, axis=0, keepdims=True)
        - hat * jnp.mean(scaled * hat, axis=0, keepdims=True)
    )
    grad_hidden[...] = out
    grad_hidden_b[...] = out.astype(BF16)
    sums[:, 0:1] = jnp.sum(grad * hat, axis=1, keepdims=True)
    sums[:, 2:3] = jnp.sum(out, axis=1, keepdims=True)
    total = jnp.zeros(all_att.shape, F32)
    for value, piece in zip(order, (m0, m1, m2, m3)):
        total += mm(piece[...], grad_hidden_b[block(here[0] ^ value, feat), :])
    all_att[...] = total.astype(BF16)
    for step, ref in enumerate((a0, a1, a2, a3)):
        ref[...] = all_att[block(here[1] ^ step, feat), :]


def first_back_kernel(
    order, heads, here, tok, stats, qkv, att, totals, a0, a1, a2, a3, row, col, w0, w1, w2, w3, grad_hidden, second,
    grad_proj, qv_sum, s0, s1, s2, s3, grad_att, share, sums,
):
    feat, count = att.shape
    part = a0.shape[1]
    head_rows = heads * HD
    scale = 1.0 / math.sqrt(HD)
    for step, piece in enumerate((a0, a1, a2, a3)):
        grad_att[:, block(here[1] ^ step, part)] = piece[...]
    width = min(MAXLEN, count)
    for half in range(count // width):
        cols = pl.ds(half * width, width)
        allowed = allowed_mask(row[:, cols], col[cols, :], width)
        for head in range(heads):
            query = qkv[pl.ds(head * HD, HD), cols]
            keys = qkv[pl.ds(head_rows + head * HD, HD), cols]
            held = qkv[pl.ds(2 * head_rows + head * HD, HD), cols]
            grad = grad_att[pl.ds(head * HD, HD), cols]
            attended = att[pl.ds(head * HD, HD), cols]
            delta = jnp.sum(grad.astype(F32) * attended.astype(F32), axis=0, keepdims=True)
            scores = jnp.where(allowed, mm_t(keys, query) * scale, NEG)
            probs = jnp.exp(scores - totals[pl.ds(head, 1), cols])
            grad_held = mm_nt(grad, probs.astype(BF16))
            grad_probs = mm_t(held, grad)
            grad_scores = (probs * (grad_probs - delta) * scale).astype(BF16)
            grad_query = mm(keys, grad_scores)
            grad_keys = mm_nt(query, grad_scores)
            grad_proj[pl.ds(head * HD, HD), cols] = grad_query.astype(BF16)
            grad_proj[pl.ds(head_rows + head * HD, HD), cols] = grad_keys.astype(BF16)
            grad_proj[pl.ds(2 * head_rows + head * HD, HD), cols] = grad_held.astype(BF16)
            for at, grown in ((head * HD, grad_query), (head_rows + head * HD, grad_held)):
                total = jnp.sum(grown, axis=1, keepdims=True)
                if half:
                    total = total + qv_sum[pl.ds(at, HD), :]
                qv_sum[pl.ds(at, HD), :] = total
    for value, piece in zip(order, (w0, w1, w2, w3)):
        share[block(here[0] ^ value, feat), :] = mm(piece[...], grad_proj[...])
    (gain,) = norm_cols(tok, count, (0,))
    inv = stats[1:2, :]
    hat = (tok[:, :count].astype(F32) - stats[0:1, :]) * inv
    grad = share[...]
    lane = lax.broadcasted_iota(jnp.int32, sums.shape, 1)
    columns = [second[:, k : k + 1] for k in range(3)]
    columns += [jnp.sum(grad * hat, axis=1, keepdims=True), jnp.sum(grad, axis=1, keepdims=True)]
    total = jnp.zeros(sums.shape, F32)
    for at, values in enumerate(columns):
        total = jnp.where(lane == at, values, total)
    sums[...] = total
    scaled = grad * gain
    share[...] = inv * (
        scaled
        - jnp.mean(scaled, axis=0, keepdims=True)
        - hat * jnp.mean(scaled * hat, axis=0, keepdims=True)
    )
    share[:, block(here[1], part)] += grad_hidden[...]
    for step, ref in enumerate((s0, s1, s2, s3)):
        rows = block(here[1] ^ step, feat)
        extra = ref.shape[0] - feat
        ref[:feat, :] = share[rows, :].astype(ref.dtype)
        ref[feat:, :feat] = sums[rows, :].T[:extra].astype(ref.dtype)


def last_grads(pair, here, normed, grad_proj, rows):
    feat = rows.shape[0] // 2
    for at, value in enumerate(pair):
        rows[pl.ds(at * feat, feat), :] = normed[block(here[0] ^ value, feat), :]
    return mm_nt(rows[...], grad_proj[...])


def last_send_kernel(order, here, normed, grad_proj, send, rows):
    send[...] = last_grads(order[2:], here, normed, grad_proj, rows).astype(BF16)


def last_keep_kernel(order, here, normed, grad_proj, got, own, own_b, send, rows):
    feat = own.shape[0]
    grad = last_grads(order[:2], here, normed, grad_proj, rows) + got[...].astype(F32)
    own[...] = grad[:feat]
    own_b[...] = grad[:feat].astype(BF16)
    send[...] = grad[feat:].astype(BF16)


def mix_send_kernel(order, here, att, grad_hidden_b, send):
    feat = send.shape[0] // 2
    own = att[:, block(here[1], grad_hidden_b.shape[1])]
    for at in (0, 1):
        rows = grad_hidden_b[block(here[0] ^ order[2 + at], feat), :]
        send[pl.ds(at * feat, feat), :] = mm_nt(rows, own).astype(BF16)


def mix_keep_kernel(order, here, att, grad_hidden_b, got, keep, send):
    feat = keep.shape[0]
    own = att[:, block(here[1], grad_hidden_b.shape[1])]
    for at, out in enumerate((keep, send)):
        rows = grad_hidden_b[block(here[0] ^ order[at], feat), :]
        out[...] = (mm_nt(rows, own) + got[pl.ds(at * feat, feat), :].astype(F32)).astype(out.dtype)


def mix_turn_kernel(here, grad_mix, own, p1, p2, p3, turned):
    feat = own.shape[0]
    turned[...] = grad_mix[...].T
    own[...] = turned[block(here[1], feat), :]
    for step, out in enumerate((p1, p2, p3)):
        out[...] = turned[block(here[1] ^ (step + 1), feat), :].astype(BF16)


def mix_sum_kernel(here, own, g1, g2, g3, out):
    out[...] = own[...] + g1[...].astype(F32) + g2[...].astype(F32) + g3[...].astype(F32)


def rest_kernel(here, up_sum, qv_sum, cot, row, rest):
    width = up_sum.shape[0]
    feat = cot.shape[0]
    down = jnp.sum(jnp.where(row[...] >= 0, cot[...].astype(F32), 0.0), axis=1, keepdims=True)
    down = jnp.concatenate([down, jnp.zeros((width - feat, 1), F32)], axis=0)
    held = jnp.concatenate([qv_sum[...], jnp.zeros((width - qv_sum.shape[0], 1), F32)], axis=0)
    lane = lax.broadcasted_iota(jnp.int32, (width, 128), 1)
    total = jnp.zeros((width, 128), F32)
    for at, values in ((5, up_sum[...]), (6, held), (7, down)):
        total = jnp.where(lane == at, values, total)
    rest[...] = total.T[:8]


def token_sum_kernel(here, s0, g1, g2, g3, rest, out, sums):
    feat = out.shape[0]
    total = s0[...]
    for ref in (g1, g2, g3):
        total += ref[...].astype(F32)
    out[...] = total[:feat]
    sums[...] = rest[...]
    sums[:5, :feat] = total[feat : feat + 5, :feat]


def last_sum_kernel(here, own, got_y, got_x, got_xy, qkv):
    qkv[...] = own[...] + got_y[...].astype(F32) + got_x[...].astype(F32) + got_xy[...].astype(F32)


def halve_kernel(here, keep, got, kept, send):
    half = kept.shape[0]
    kept[...] = keep[:half] + got[:half].astype(F32)
    send[...] = (keep[half:] + got[half:].astype(F32)).astype(BF16)


def bits_of(size):
    bits, bit = [], 1
    while bit < size:
        bits.append(bit)
        bit *= 2
    return bits


def swap(values, axis, size, bit):
    return lax.ppermute(values, axis, [(at, at ^ bit) for at in range(size)])


def after(value, *others):
    return lax.optimization_barrier((value,) + others)[0]


def together(*values):
    return lax.optimization_barrier(values)


def make_body(n_dp, n_rows, n_cols):
    assert n_rows == 4 and n_cols == 4 and n_dp % 2 == 0
    far, near = 2, 1
    order = (0, far, near, far ^ near)

    def over_rows(value, bit):
        return swap(value, "rows", n_rows, bit)

    def over_cols(value, bit):
        return swap(value, "cols", n_cols, bit)

    def all_over_cols(values):
        return [over_cols(value, bit) for value, bit in zip(values, (1, 2, 3))]

    def over_dp(value):
        value = value.astype(BF16).astype(F32)
        for bit in bits_of(n_dp):
            value = value + swap(value.astype(BF16), "dp", n_dp, bit).astype(F32)
        return value

    def body(
        tokens,
        segment_ids,
        first_gain,
        first_bias,
        qkv_weight,
        qv_bias,
        mix_weight,
        mix_bias,
        second_gain,
        second_bias,
        up_weight,
        up_bias,
        down_weight,
        down_bias,
        cotangent,
    ):
        feat, count = tokens.shape
        width = feat * n_cols
        part = count // n_cols
        n_qkv = qkv_weight.shape[1]
        n_hid = up_weight.shape[1]
        heads = n_qkv // (3 * HD)
        head_rows = heads * HD
        here = [lax.axis_index("rows"), lax.axis_index("cols"), lax.axis_index("dp") & 1]
        here = jnp.stack(here).astype(jnp.int32)
        row = segment_ids.reshape(1, count)

        def halve(keep, got):
            half = (keep.shape[0] // 2,) + keep.shape[1:]
            return run(halve_kernel, (shaped(half, F32), shaped(half, BF16)), (here, keep, got))

        qkv_y = over_rows(qkv_weight, far)
        up_y, down_y = over_rows(up_weight, far), over_rows(down_weight, far)
        qkv_c, up_c, down_c = [over_rows(value, near) for value in (qkv_weight, up_weight, down_weight)]
        packed, down_col, seg_col = run(
            pack_kernel,
            (shaped((feat, count + 128), BF16), shaped((feat, 1), F32), shaped((count, 1), jnp.int32)),
            (here, tokens, mix_weight)
            + tuple(
                value.reshape(1, -1)
                for value in (first_gain, first_bias, mix_bias, second_gain, second_bias, down_bias, segment_ids)
            ),
            hold=False,
            limit=58,
        )
        tok = lax.all_gather(packed, "cols", axis=0, tiled=True)
        qkv_yc = over_rows(qkv_y, near)
        w_pieces = (qkv_weight, qkv_y, qkv_c, qkv_yc)
        cot_own = after(cotangent, tok)
        cot_z = all_over_cols((cot_own,) * 3)
        mix_half = tok[:, count:]
        pairs = [(at, at ^ 1) for at in range(n_dp)]
        mix_got = lax.ppermute(mix_half, "dp", pairs)
        (mix_all,) = run(mix_pack_kernel, (shaped((width, feat), BF16),), (here, mix_half, mix_got))
        mix_y, mix_c = over_rows(mix_all, far), over_rows(mix_all, near)
        up_yc, down_yc = over_rows(up_y, near), over_rows(down_y, near)

        normed_one, stats, qkv, attended, totals = run(
            functools.partial(first_kernel, order, heads),
            (
                shaped((width, count), BF16),
                shaped((2, count), F32),
                shaped((n_qkv, count), BF16),
                shaped((head_rows, count), BF16),
                shaped((heads, count), F32),
            ),
            (here, tok) + w_pieces + (qv_bias, row, seg_col),
            scratch=(pltpu.VMEM((width, n_qkv), BF16),),
            flops=2 * width * n_qkv * count,
        )
        att = lax.all_gather(attended, "cols", axis=0, tiled=True)
        mix_yc = over_rows(mix_y, near)
        m_pieces = (mix_all, mix_y, mix_c, mix_yc)

        wide_b = shaped((width, count), BF16)
        piece_b = shaped((width, part), BF16)
        piece_f = shaped((width, part), F32)
        (
            normed_two, grad_pre, active, grad_final, p1, p2, p3, own_two, own_hat, own_inv, own_hidden, up_sum, down_all,
        ) = run(
            functools.partial(middle_kernel, order),
            (
                wide_b, shaped((n_hid, count), BF16), shaped((n_hid, count), BF16), wide_b,
                piece_b, piece_b, piece_b, piece_f, piece_f,
                shaped((8, count), F32), shaped((feat, count), F32), shaped((n_hid, 1), F32), shaped((width, n_hid), BF16),
            ),
            (here, tok, att)
            + m_pieces
            + (up_weight, up_y, up_c, up_yc)
            + (down_weight, down_y, down_c, down_yc)
            + (cotangent,)
            + tuple(cot_z)
            + (row, up_bias),
            scratch=(pltpu.VMEM((width, n_hid), BF16), pltpu.VMEM((width, count), F32)),
            flops=2 * width * count * (width + 3 * n_hid),
        )
        got = all_over_cols((p1, p2, p3))

        ff_send, ff_keep = run(
            functools.partial(ff_grads_kernel, order),
            (
                shaped((2 * feat, 2 * n_hid), BF16), shaped((2 * feat, 2 * n_hid), F32),
            ),
            (here, grad_final, active, normed_two, grad_pre),
            scratch=(pltpu.VMEM((width, count), BF16),),
            flops=2 * width * count * 2 * n_hid,
        )
        out_send, out_keep = run(
            out_parts_kernel,
            (shaped((2 * feat, count), BF16), shaped((2 * feat, count), F32)),
            (here, down_all, active),
            flops=2 * width * count * n_hid,
        )
        ff_keep, ff_send = halve(ff_keep, over_rows(ff_send, near))
        ff_got = over_rows(ff_send, far)
        got[0], got[1], got[2], ff_keep, out_send = together(*got, ff_keep, out_send)

        grad_hidden, grad_hidden_b, second, a0, a1, a2, a3 = run(
            functools.partial(second_back_kernel, order),
            (
                piece_f, piece_b, shaped((width, 8), F32),
                shaped((feat, part), BF16), shaped((feat, part), BF16), shaped((feat, part), BF16), shaped((feat, part), BF16),
            ),
            (here, tok, own_two) + tuple(got) + (own_hat, own_inv, grad_final) + m_pieces,
            scratch=(pltpu.VMEM((width, part), BF16),),
            flops=2 * width * part * width,
        )
        b1, b2, b3 = all_over_cols((a1, a2, a3))
        (mix_send,) = run(
            functools.partial(mix_send_kernel, order), (shaped((2 * feat, width), BF16),),
            (here, att, grad_hidden_b), flops=width * width * part,
        )
        mix_keep, mix_send = run(
            functools.partial(mix_keep_kernel, order),
            (shaped((feat, width), F32), shaped((feat, width), BF16)),
            (here, att, grad_hidden_b, over_rows(mix_send, near)),
            flops=width * width * part,
        )
        mix_got = over_rows(mix_send, far)
        out_got = over_cols(after(out_send, grad_hidden_b), 1)
        ff_sum = ff_keep + ff_got.astype(F32)
        b1, b2, b3, ff_sum = together(b1, b2, b3, ff_sum)
        grad_ff = over_dp(ff_sum)

        grad_proj, qv_sum, s0, s1, s2, s3 = run(
            functools.partial(first_back_kernel, order, heads),
            (
                shaped((n_qkv, count), BF16), shaped((2 * head_rows, 1), F32),
                shaped((feat + 16, count), F32),
                shaped((feat + 16, count), BF16), shaped((feat + 16, count), BF16), shaped((feat + 16, count), BF16),
            ),
            (here, tok, stats, qkv, attended, totals, a0, b1, b2, b3, row, seg_col) + w_pieces + (grad_hidden, second),
            scratch=(pltpu.VMEM((head_rows, count), BF16), pltpu.VMEM((width, count), F32), pltpu.VMEM((width, 128), F32)),
            flops=2 * width * n_qkv * count,
        )
        got = all_over_cols((s1, s2, s3))

        grad_mix = over_dp(mix_keep + mix_got.astype(F32))
        last_ins = (here, normed_one, grad_proj)
        last_rows = (pltpu.VMEM((2 * feat, count), BF16),)
        (last_send,) = run(
            functools.partial(last_send_kernel, order), (shaped((2 * feat, n_qkv), BF16),), last_ins,
            scratch=last_rows, flops=width * count * n_qkv,
        )
        own, own_b, last_send = run(
            functools.partial(last_keep_kernel, order),
            (shaped((feat, n_qkv), F32), shaped((feat, n_qkv), BF16), shaped((feat, n_qkv), BF16)),
            last_ins + (over_rows(last_send, near),),
            scratch=last_rows,
            flops=width * count * n_qkv,
        )
        far_dp = [(d * n_rows + r, (d ^ 1) * n_rows + (r ^ far)) for d in range(n_dp) for r in range(n_rows)]
        got_y = over_rows(last_send, far)
        if n_dp > 1:
            got_x = lax.ppermute(own_b, "dp", pairs)
            got_xy = lax.ppermute(last_send, ("dp", "rows"), far_dp)
        else:
            got_x = got_xy = jnp.zeros_like(got_y)
        (grad_qkv,) = run(last_sum_kernel, (shaped((feat, n_qkv), F32),), (here, own, got_y, got_x, got_xy))
        for bit in bits_of(n_dp)[1:]:
            grad_qkv = grad_qkv + swap(grad_qkv.astype(BF16), "dp", n_dp, bit).astype(F32)

        (rest,) = run(rest_kernel, (shaped((8, width), F32),), (here, up_sum, qv_sum, cotangent, row))
        grad_tokens, sums = run(
            token_sum_kernel, (shaped((feat, count), F32), shaped((8, width), F32)), (here, s0) + tuple(got) + (rest,)
        )
        for axis, size in (("rows", n_rows), ("dp", n_dp)):
            for bit in bits_of(size):
                sums = sums + swap(sums, axis, size, bit)

        square_b = shaped((feat, feat), BF16)
        mix_own, p1, p2, p3 = run(
            mix_turn_kernel,
            (shaped((feat, feat), F32), square_b, square_b, square_b),
            (here, grad_mix),
            scratch=(pltpu.VMEM((width, feat), F32),),
        )
        got = all_over_cols((p1, p2, p3))
        (grad_mix,) = run(mix_sum_kernel, (shaped((feat, feat), F32),), (here, mix_own) + tuple(got))
        out_keep, out_send = halve(out_keep, out_got)
        output = own_hidden + down_col + out_keep + over_cols(out_send, 2).astype(F32)
        return (
            output.astype(BF16),
            grad_tokens,
            sums[3, :feat],
            sums[4, :feat],
            grad_qkv,
            sums[6, : 2 * head_rows],
            grad_mix,
            sums[2, :feat],
            sums[0, :feat],
            sums[1, :feat],
            grad_ff[:, n_hid:],
            sums[5, :n_hid],
            grad_ff[:, :n_hid],
            sums[7, :feat],
        )

    return body


def solution(mesh):
    sizes = mesh.shape
    body = make_body(sizes["dp"], sizes["rows"], sizes["cols"])

    return jax.shard_map(
        body,
        mesh=mesh,
        in_specs=(
            P("cols", ("dp", "rows")),
            P(("dp", "rows")),
            P("cols"),
            P("cols"),
            P("rows", "cols"),
            P("cols"),
            P("cols", "rows"),
            P("cols"),
            P("cols"),
            P("cols"),
            P("rows", "cols"),
            P("cols"),
            P("rows", "cols"),
            P("cols"),
            P("cols", ("dp", "rows")),
        ),
        out_specs=(
            P("cols", ("dp", "rows")),
            P("cols", ("dp", "rows")),
            P("cols"),
            P("cols"),
            P("rows", "cols"),
            P("cols"),
            P("cols", "rows"),
            P("cols"),
            P("cols"),
            P("cols"),
            P("rows", "cols"),
            P("cols"),
            P("rows", "cols"),
            P("cols"),
        ),
        check_vma=False,
    )
```

```python
import functools
import math

import jax
import jax.numpy as jnp
from jax import lax
from jax.experimental import pallas as pl
from jax.experimental.pallas import tpu as pltpu
from jax.sharding import PartitionSpec as P


COLS = "cols"
ROWS = "rows"
HD = 64
MAXLEN = 256
EPS = 1e-05
NEG = -1e30
ROOT = 0.7978845608028654
CUBIC = 0.044715
F32 = jnp.float32
BF16 = jnp.bfloat16


def dot(left, right, dims):
    return lax.dot_general(left, right, (dims, ((), ())), preferred_element_type=F32)


def mm(left, right):
    return dot(left, right, ((1,), (0,)))


def mm_t(left, right):
    return dot(left, right, ((0,), (0,)))


def mm_nt(left, right):
    return dot(left, right, ((1,), (1,)))


def gelu_both(pre_act):
    inner_arg = ROOT * (pre_act + CUBIC * pre_act * pre_act * pre_act)
    tanh_val = jnp.tanh(inner_arg)
    value = 0.5 * pre_act * (1.0 + tanh_val)
    slope = 0.5 * (1.0 + tanh_val) + 0.5 * pre_act * (1.0 - tanh_val * tanh_val) * ROOT * (
        1.0 + 3.0 * CUBIC * pre_act * pre_act
    )
    return value, slope


def allowed_mask(seg_row, seg_col, width):
    key_pos = lax.broadcasted_iota(jnp.int32, (width, width), 0)
    query_pos = lax.broadcasted_iota(jnp.int32, (width, width), 1)
    same_seg = (seg_col == seg_row) & (seg_row >= 0)
    return (key_pos < query_pos) & same_seg | (key_pos == query_pos)


def block(index, size):
    return pl.ds(pl.multiple_of(index * size, size), size)


def norm_cols(tok_ref, count, which):
    start = tok_ref.shape[0] // 8
    cols = tok_ref[:, count : tok_ref.shape[1]].astype(F32)[:, start:]
    return [cols[:, k : k + 1] + cols[:, k + 5 : k + 6] + cols[:, k + 10 : k + 11] for k in which]


def run(kernel, outs, ins, scratch=(), flops=0, hold=True, limit=24, final=False):
    specs = [pl.BlockSpec(memory_space=pltpu.SMEM)]
    specs += [pl.BlockSpec(memory_space=pltpu.VMEM)] * (len(ins) - 1)
    size = sum(math.prod(value.shape) * value.dtype.itemsize for value in list(ins) + list(outs))
    held = [pltpu.with_memory_space_constraint(value, pltpu.VMEM) if hold else value for value in ins[1:]]
    return pl.pallas_call(
        kernel,
        out_shape=list(outs) if final else [pltpu.VMEM(value.shape, value.dtype) for value in outs],
        in_specs=specs,
        out_specs=[pl.BlockSpec(memory_space=pltpu.VMEM)] * len(outs),
        scratch_shapes=list(scratch),
        cost_estimate=pl.CostEstimate(flops=flops, transcendentals=0, bytes_accessed=size),
        compiler_params=pltpu.CompilerParams(vmem_limit_bytes=limit * 1024 * 1024),
    )(ins[0], *held)


def shaped(shape, dtype):
    return jax.ShapeDtypeStruct(shape, dtype)


def column(row):
    return jnp.broadcast_to(row, (128, row.shape[1])).T[:, :1]


def pack_kernel(here, tok, mix, g1, b1, bm, g2, b2, down, seg, packed, down_col, seg_col):
    feat, count = tok.shape
    rows = jnp.concatenate([ref[...] for ref in (g1, b1, bm, g2, b2)], axis=0)
    high = rows.astype(BF16).astype(F32)
    middle = (rows - high).astype(BF16).astype(F32)
    low = rows - high - middle
    used = 3 * rows.shape[0]
    norms = jnp.concatenate([high, middle, low, jnp.zeros((128 - used, feat), F32)], axis=0).T
    half = feat // 2
    values = mix[...].astype(F32)
    values = jnp.where(here[2] == 0, values[:, :half], values[:, half:])
    packed[:, :count] = tok[...]
    packed[:, count:] = jnp.concatenate([values, norms[:, : 128 - half]], axis=1).astype(BF16)
    down_col[...] = column(down[...])
    seg_col[...] = column(seg[...].astype(F32)).astype(jnp.int32)


def first_kernel(order, heads, here, tok, w0, w1, w2, w3, qv, row, col, normed, stats, qkv, att, totals, w_all):
    feat = w0.shape[0]
    count = row.shape[1]
    for value, piece in zip(order, (w0, w1, w2, w3)):
        w_all[block(here[0] ^ value, feat), :] = piece[...]
    gain, shift = norm_cols(tok, count, (0, 1))
    values = tok[:, :count].astype(F32)
    mean = jnp.mean(values, axis=0, keepdims=True)
    inv = lax.rsqrt(jnp.mean(values * values, axis=0, keepdims=True) - mean * mean + EPS)
    stats[0:1, :] = mean
    stats[1:2, :] = inv
    normed[...] = ((values - mean) * inv * gain + shift).astype(BF16)
    head_rows = heads * HD
    qv_col = column(qv[...].reshape(1, 2 * head_rows))
    bias = jnp.concatenate([qv_col[:head_rows], jnp.zeros((head_rows, 1), F32), qv_col[head_rows:]], axis=0)
    qkv[...] = (mm_t(w_all[...], normed[...]) + bias).astype(BF16)
    scale = 1.0 / math.sqrt(HD)
    width = min(MAXLEN, count)
    for half in range(count // width):
        cols = pl.ds(half * width, width)
        allowed = allowed_mask(row[:, cols], col[cols, :], width)
        for head in range(heads):
            query = qkv[pl.ds(head * HD, HD), cols]
            keys = qkv[pl.ds(head_rows + head * HD, HD), cols]
            held = qkv[pl.ds(2 * head_rows + head * HD, HD), cols]
            scores = jnp.where(allowed, mm_t(keys, query) * scale, NEG)
            top = jnp.max(scores, axis=0, keepdims=True)
            log_total = top + jnp.log(jnp.sum(jnp.exp(scores - top), axis=0, keepdims=True))
            probs = jnp.exp(scores - log_total).astype(BF16)
            att[pl.ds(head * HD, HD), cols] = mm(held, probs).astype(BF16)
            totals[pl.ds(head, 1), cols] = log_total


def mix_pack_kernel(here, own, got, out):
    half = out.shape[1] // 2
    mine, other = own[...].astype(F32)[:, :half], got[...].astype(F32)[:, :half]
    first = jnp.where(here[2] == 0, mine, other)
    second = jnp.where(here[2] == 0, other, mine)
    out[...] = jnp.concatenate([first, second], axis=1).astype(BF16)


def middle_kernel(
    order, here, tok, att, m0, m1, m2, m3, u0, u1, u2, u3, d0, d1, d2, d3, c0, c1, c2, c3, row, up,
    normed, grad_pre, active, grad_final, p1, p2, p3, own_two, own_hat, own_inv, own_hidden, up_sum, down_all,
    up_all, hidden,
):
    feat, count = own_hidden.shape
    part = own_two.shape[1]
    live = row[...] >= 0
    bias_mix, gain, shift = norm_cols(tok, count, (2, 3, 4))
    for value, piece in zip(order, (u0, u1, u2, u3)):
        up_all[block(here[0] ^ value, feat), :] = piece[...]
    for value, piece in zip(order, (d0, d1, d2, d3)):
        down_all[block(here[0] ^ value, feat), :] = piece[...]
    for step, piece in enumerate((c0, c1, c2, c3)):
        masked = jnp.where(live, piece[...].astype(F32), 0.0)
        grad_final[block(here[1] ^ step, feat), :] = masked.astype(BF16)
    for value, piece in zip(order, (m0, m1, m2, m3)):
        hidden[block(here[0] ^ value, feat), :] = mm_t(piece[...], att[...])
    hidden[...] = hidden[...] + tok[:, :count].astype(F32) + bias_mix
    values = hidden[...]
    mean = jnp.mean(values, axis=0, keepdims=True)
    inv = lax.rsqrt(jnp.mean(values * values, axis=0, keepdims=True) - mean * mean + EPS)
    own_hidden[...] = hidden[block(here[1], feat), :]
    hat = (values - mean) * inv
    normed[...] = (hat * gain + shift).astype(BF16)
    hidden[...] = hat
    own_inv[...] = jnp.broadcast_to(inv, (8, count))
    own_hat[...] = hidden[:, block(here[1], part)]
    value, slope = gelu_both(mm_t(up_all[...], normed[...]) + column(up[...].reshape(1, up.shape[0])))
    active[...] = value.astype(BF16)
    grad = mm_t(down_all[...], grad_final[...]) * slope
    grad_pre[...] = grad.astype(BF16)
    up_sum[...] = jnp.sum(grad_pre[...].astype(F32), axis=1, keepdims=True)
    hidden[...] = mm(up_all[...], grad_pre[...])
    own_two[...] = hidden[:, block(here[1], part)]
    for step, out in enumerate((p1, p2, p3)):
        out[...] = hidden[:, block(here[1] ^ (step + 1), part)].astype(BF16)


def in_order(order, here, target, source):
    feat = target.shape[0] // len(order)
    for at, value in enumerate(order):
        target[pl.ds(at * feat, feat), :] = source[block(here[0] ^ value, feat), :]


def ff_grads_kernel(
    order, here, grad_final, active, normed, grad_pre, send, keep, rows
):
    half = keep.shape[0]
    hid = active.shape[0]
    in_order(order, here, rows, grad_final)
    down = mm_nt(rows[...], active[...])
    keep[:, :hid] = down[:half]
    send[:, :hid] = down[half:].astype(BF16)
    in_order(order, here, rows, normed)
    up = mm_nt(rows[...], grad_pre[...])
    keep[:, hid:] = up[:half]
    send[:, hid:] = up[half:].astype(BF16)


def out_parts_kernel(here, down_all, active, out_send, out_keep):
    feat = out_keep.shape[0] // 2
    for step in (0, 2):
        out_keep[pl.ds(step // 2 * feat, feat), :] = mm(down_all[block(here[1] ^ step, feat), :], active[...])
        out = mm(down_all[block(here[1] ^ (step + 1), feat), :], active[...])
        out_send[pl.ds(step // 2 * feat, feat), :] = out.astype(BF16)


def second_back_kernel(
    order, here, tok, own_two, r1, r2, r3, own_hat, own_inv, grad_final, m0, m1, m2, m3,
    grad_hidden, grad_hidden_b, sums, a0, a1, a2, a3, all_att,
):
    feat = a0.shape[0]
    part = own_two.shape[1]
    (gain,) = norm_cols(tok, grad_final.shape[1], (3,))
    grad = own_two[...] + r1[...].astype(F32) + r2[...].astype(F32) + r3[...].astype(F32)
    sums[:, 1:2] = jnp.sum(grad, axis=1, keepdims=True)
    hat = own_hat[...]
    lanes = block(here[1], part)
    inv = own_inv[:, lanes][:1]
    scaled = grad * gain
    out = grad_final[:, lanes].astype(F32) + inv * (
        scaled
        - jnp.mean(scaled, axis=0, keepdims=True)
        - hat * jnp.mean(scaled * hat, axis=0, keepdims=True)
    )
    grad_hidden[...] = out
    grad_hidden_b[...] = out.astype(BF16)
    sums[:, 0:1] = jnp.sum(grad * hat, axis=1, keepdims=True)
    sums[:, 2:3] = jnp.sum(out, axis=1, keepdims=True)
    total = jnp.zeros(all_att.shape, F32)
    for value, piece in zip(order, (m0, m1, m2, m3)):
        total += mm(piece[...], grad_hidden_b[block(here[0] ^ value, feat), :])
    all_att[...] = total.astype(BF16)
    for step, ref in enumerate((a0, a1, a2, a3)):
        ref[...] = all_att[block(here[1] ^ step, feat), :]


def first_back_kernel(
    order, heads, here, tok, stats, qkv, att, totals, a0, a1, a2, a3, row, col, w0, w1, w2, w3, grad_hidden, second,
    grad_proj, qv_sum, s0, s1, s2, s3, grad_att, share, sums,
):
    feat, count = att.shape
    part = a0.shape[1]
    head_rows = heads * HD
    scale = 1.0 / math.sqrt(HD)
    for step, piece in enumerate((a0, a1, a2, a3)):
        grad_att[:, block(here[1] ^ step, part)] = piece[...]
    width = min(MAXLEN, count)
    for half in range(count // width):
        cols = pl.ds(half * width, width)
        allowed = allowed_mask(row[:, cols], col[cols, :], width)
        for head in range(heads):
            query = qkv[pl.ds(head * HD, HD), cols]
            keys = qkv[pl.ds(head_rows + head * HD, HD), cols]
            held = qkv[pl.ds(2 * head_rows + head * HD, HD), cols]
            grad = grad_att[pl.ds(head * HD, HD), cols]
            attended = att[pl.ds(head * HD, HD), cols]
            delta = jnp.sum(grad.astype(F32) * attended.astype(F32), axis=0, keepdims=True)
            scores = jnp.where(allowed, mm_t(keys, query) * scale, NEG)
            probs = jnp.exp(scores - totals[pl.ds(head, 1), cols])
            grad_held = mm_nt(grad, probs.astype(BF16))
            grad_probs = mm_t(held, grad)
            grad_scores = (probs * (grad_probs - delta) * scale).astype(BF16)
            grad_query = mm(keys, grad_scores)
            grad_keys = mm_nt(query, grad_scores)
            grad_proj[pl.ds(head * HD, HD), cols] = grad_query.astype(BF16)
            grad_proj[pl.ds(head_rows + head * HD, HD), cols] = grad_keys.astype(BF16)
            grad_proj[pl.ds(2 * head_rows + head * HD, HD), cols] = grad_held.astype(BF16)
            for at, grown in ((head * HD, grad_query), (head_rows + head * HD, grad_held)):
                total = jnp.sum(grown, axis=1, keepdims=True)
                if half:
                    total = total + qv_sum[pl.ds(at, HD), :]
                qv_sum[pl.ds(at, HD), :] = total
    for value, piece in zip(order, (w0, w1, w2, w3)):
        share[block(here[0] ^ value, feat), :] = mm(piece[...], grad_proj[...])
    (gain,) = norm_cols(tok, count, (0,))
    inv = stats[1:2, :]
    hat = (tok[:, :count].astype(F32) - stats[0:1, :]) * inv
    grad = share[...]
    lane = lax.broadcasted_iota(jnp.int32, sums.shape, 1)
    columns = [second[:, k : k + 1] for k in range(3)]
    columns += [jnp.sum(grad * hat, axis=1, keepdims=True), jnp.sum(grad, axis=1, keepdims=True)]
    total = jnp.zeros(sums.shape, F32)
    for at, values in enumerate(columns):
        total = jnp.where(lane == at, values, total)
    sums[...] = total
    scaled = grad * gain
    share[...] = inv * (
        scaled
        - jnp.mean(scaled, axis=0, keepdims=True)
        - hat * jnp.mean(scaled * hat, axis=0, keepdims=True)
    )
    share[:, block(here[1], part)] += grad_hidden[...]
    for step, ref in enumerate((s0, s1, s2, s3)):
        rows = block(here[1] ^ step, feat)
        extra = ref.shape[0] - feat
        ref[:feat, :] = share[rows, :].astype(ref.dtype)
        ref[feat:, :feat] = sums[rows, :].T[:extra].astype(ref.dtype)


def last_grads(pair, here, normed, grad_proj, rows):
    feat = rows.shape[0] // 2
    for at, value in enumerate(pair):
        rows[pl.ds(at * feat, feat), :] = normed[block(here[0] ^ value, feat), :]
    return mm_nt(rows[...], grad_proj[...])


def last_send_kernel(order, here, normed, grad_proj, send, rows):
    send[...] = last_grads(order[2:], here, normed, grad_proj, rows).astype(BF16)


def last_keep_kernel(order, here, normed, grad_proj, got, own, own_b, send, rows):
    feat = own.shape[0]
    grad = last_grads(order[:2], here, normed, grad_proj, rows) + got[...].astype(F32)
    own[...] = grad[:feat]
    own_b[...] = grad[:feat].astype(BF16)
    send[...] = grad[feat:].astype(BF16)


def mix_send_kernel(order, here, att, grad_hidden_b, send):
    feat = send.shape[0] // 2
    own = att[:, block(here[1], grad_hidden_b.shape[1])]
    for at in (0, 1):
        rows = grad_hidden_b[block(here[0] ^ order[2 + at], feat), :]
        send[pl.ds(at * feat, feat), :] = mm_nt(rows, own).astype(BF16)


def mix_keep_kernel(order, here, att, grad_hidden_b, got, keep, send):
    feat = keep.shape[0]
    own = att[:, block(here[1], grad_hidden_b.shape[1])]
    for at, out in enumerate((keep, send)):
        rows = grad_hidden_b[block(here[0] ^ order[at], feat), :]
        out[...] = (mm_nt(rows, own) + got[pl.ds(at * feat, feat), :].astype(F32)).astype(out.dtype)


def mix_turn_kernel(here, grad_mix, own, p1, p2, p3, turned):
    feat = own.shape[0]
    turned[...] = grad_mix[...].T
    own[...] = turned[block(here[1], feat), :]
    for step, out in enumerate((p1, p2, p3)):
        out[...] = turned[block(here[1] ^ (step + 1), feat), :].astype(BF16)


def mix_sum_kernel(here, own, g1, g2, g3, out):
    out[...] = own[...] + g1[...].astype(F32) + g2[...].astype(F32) + g3[...].astype(F32)


def rest_kernel(here, up_sum, qv_sum, cot, row, rest):
    width = up_sum.shape[0]
    feat = cot.shape[0]
    down = jnp.sum(jnp.where(row[...] >= 0, cot[...].astype(F32), 0.0), axis=1, keepdims=True)
    down = jnp.concatenate([down, jnp.zeros((width - feat, 1), F32)], axis=0)
    held = jnp.concatenate([qv_sum[...], jnp.zeros((width - qv_sum.shape[0], 1), F32)], axis=0)
    lane = lax.broadcasted_iota(jnp.int32, (width, 128), 1)
    total = jnp.zeros((width, 128), F32)
    for at, values in ((5, up_sum[...]), (6, held), (7, down)):
        total = jnp.where(lane == at, values, total)
    rest[...] = total.T[:8]


def sums_out_kernel(here, sums, got, *outs):
    total = sums[...] + got[...]
    for row, out in enumerate(outs):
        out[...] = total[row : row + 1, : out.shape[1]]


def token_sum_kernel(here, s0, g1, g2, g3, rest, out, sums):
    feat = out.shape[0]
    total = s0[...]
    for ref in (g1, g2, g3):
        total += ref[...].astype(F32)
    out[...] = total[:feat]
    sums[...] = rest[...]
    sums[:5, :feat] = total[feat : feat + 5, :feat]


def last_sum_kernel(here, own, got_y, got_x, got_xy, qkv):
    qkv[...] = own[...] + got_y[...].astype(F32) + got_x[...].astype(F32) + got_xy[...].astype(F32)


def output_kernel(here, own_hidden, down_col, keep, got, out):
    out[...] = (own_hidden[...] + down_col[...] + keep[...] + got[...].astype(F32)).astype(BF16)


def halve_kernel(here, keep, got, kept, send):
    half = kept.shape[0]
    kept[...] = keep[:half] + got[:half].astype(F32)
    send[...] = (keep[half:] + got[half:].astype(F32)).astype(BF16)


def bits_of(size):
    bits, bit = [], 1
    while bit < size:
        bits.append(bit)
        bit *= 2
    return bits


def swap(values, axis, size, bit):
    return lax.ppermute(values, axis, [(at, at ^ bit) for at in range(size)])


def after(value, *others):
    return lax.optimization_barrier((value,) + others)[0]


def together(*values):
    return lax.optimization_barrier(values)


def make_body(n_dp, n_rows, n_cols):
    assert n_rows == 4 and n_cols == 4 and n_dp % 2 == 0
    far, near = 2, 1
    order = (0, far, near, far ^ near)

    def over_rows(value, bit):
        return swap(value, ROWS, n_rows, bit)

    def over_cols(value, bit):
        return swap(value, COLS, n_cols, bit)

    def all_over_cols(values):
        return [over_cols(value, bit) for value, bit in zip(values, (1, 2, 3))]

    def over_dp(value):
        value = value.astype(BF16).astype(F32)
        for bit in bits_of(n_dp):
            value = value + swap(value.astype(BF16), "dp", n_dp, bit).astype(F32)
        return value

    def body(
        tokens,
        segment_ids,
        first_gain,
        first_bias,
        qkv_weight,
        qv_bias,
        mix_weight,
        mix_bias,
        second_gain,
        second_bias,
        up_weight,
        up_bias,
        down_weight,
        down_bias,
        cotangent,
    ):
        feat, count = tokens.shape
        width = feat * n_cols
        part = count // n_cols
        n_qkv = qkv_weight.shape[1]
        n_hid = up_weight.shape[1]
        heads = n_qkv // (3 * HD)
        head_rows = heads * HD
        here = [lax.axis_index(ROWS), lax.axis_index(COLS), lax.axis_index("dp") & 1]
        here = jnp.stack(here).astype(jnp.int32)
        row = segment_ids.reshape(1, count)

        def halve(keep, got):
            half = (keep.shape[0] // 2,) + keep.shape[1:]
            return run(halve_kernel, (shaped(half, F32), shaped(half, BF16)), (here, keep, got))

        qkv_y = over_rows(qkv_weight, far)
        up_y, down_y = over_rows(up_weight, far), over_rows(down_weight, far)
        qkv_c, up_c, down_c = [over_rows(value, near) for value in (qkv_weight, up_weight, down_weight)]
        packed, down_col, seg_col = run(
            pack_kernel,
            (shaped((feat, count + 128), BF16), shaped((feat, 1), F32), shaped((count, 1), jnp.int32)),
            (here, tokens, mix_weight)
            + tuple(
                value.reshape(1, -1)
                for value in (first_gain, first_bias, mix_bias, second_gain, second_bias, down_bias, segment_ids)
            ),
            hold=False,
            limit=58,
        )
        tok = lax.all_gather(packed, COLS, axis=0, tiled=True)
        qkv_yc = over_rows(qkv_y, near)
        w_pieces = (qkv_weight, qkv_y, qkv_c, qkv_yc)
        cot_own = after(cotangent, tok)
        cot_z = all_over_cols((cot_own,) * 3)
        mix_half = tok[:, count:]
        pairs = [(at, at ^ 1) for at in range(n_dp)]
        mix_got = lax.ppermute(mix_half, "dp", pairs)
        (mix_all,) = run(mix_pack_kernel, (shaped((width, feat), BF16),), (here, mix_half, mix_got))
        mix_y, mix_c = over_rows(mix_all, far), over_rows(mix_all, near)
        up_yc, down_yc = over_rows(up_y, near), over_rows(down_y, near)

        normed_one, stats, qkv, attended, totals = run(
            functools.partial(first_kernel, order, heads),
            (
                shaped((width, count), BF16),
                shaped((2, count), F32),
                shaped((n_qkv, count), BF16),
                shaped((head_rows, count), BF16),
                shaped((heads, count), F32),
            ),
            (here, tok) + w_pieces + (qv_bias, row, seg_col),
            scratch=(pltpu.VMEM((width, n_qkv), BF16),),
            flops=2 * width * n_qkv * count,
        )
        att = lax.all_gather(attended, COLS, axis=0, tiled=True)
        mix_yc = over_rows(mix_y, near)
        m_pieces = (mix_all, mix_y, mix_c, mix_yc)

        wide_b = shaped((width, count), BF16)
        piece_b = shaped((width, part), BF16)
        piece_f = shaped((width, part), F32)
        (
            normed_two, grad_pre, active, grad_final, p1, p2, p3, own_two, own_hat, own_inv, own_hidden, up_sum, down_all,
        ) = run(
            functools.partial(middle_kernel, order),
            (
                wide_b, shaped((n_hid, count), BF16), shaped((n_hid, count), BF16), wide_b,
                piece_b, piece_b, piece_b, piece_f, piece_f,
                shaped((8, count), F32), shaped((feat, count), F32), shaped((n_hid, 1), F32), shaped((width, n_hid), BF16),
            ),
            (here, tok, att)
            + m_pieces
            + (up_weight, up_y, up_c, up_yc)
            + (down_weight, down_y, down_c, down_yc)
            + (cotangent,)
            + tuple(cot_z)
            + (row, up_bias),
            scratch=(pltpu.VMEM((width, n_hid), BF16), pltpu.VMEM((width, count), F32)),
            flops=2 * width * count * (width + 3 * n_hid),
        )
        got = all_over_cols((p1, p2, p3))

        ff_send, ff_keep = run(
            functools.partial(ff_grads_kernel, order),
            (
                shaped((2 * feat, 2 * n_hid), BF16), shaped((2 * feat, 2 * n_hid), F32),
            ),
            (here, grad_final, active, normed_two, grad_pre),
            scratch=(pltpu.VMEM((width, count), BF16),),
            flops=2 * width * count * 2 * n_hid,
        )
        out_send, out_keep = run(
            out_parts_kernel,
            (shaped((2 * feat, count), BF16), shaped((2 * feat, count), F32)),
            (here, down_all, active),
            flops=2 * width * count * n_hid,
        )
        ff_keep, ff_send = halve(ff_keep, over_rows(ff_send, near))
        ff_got = over_rows(ff_send, far)
        got[0], got[1], got[2], ff_keep = together(*got, ff_keep)

        grad_hidden, grad_hidden_b, second, a0, a1, a2, a3 = run(
            functools.partial(second_back_kernel, order),
            (
                piece_f, piece_b, shaped((width, 8), F32),
                shaped((feat, part), BF16), shaped((feat, part), BF16), shaped((feat, part), BF16), shaped((feat, part), BF16),
            ),
            (here, tok, own_two) + tuple(got) + (own_hat, own_inv, grad_final) + m_pieces,
            scratch=(pltpu.VMEM((width, part), BF16),),
            flops=2 * width * part * width,
        )
        b1, b2, b3 = all_over_cols((a1, a2, a3))
        (mix_send,) = run(
            functools.partial(mix_send_kernel, order), (shaped((2 * feat, width), BF16),),
            (here, att, grad_hidden_b), flops=width * width * part,
        )
        mix_keep, mix_send = run(
            functools.partial(mix_keep_kernel, order),
            (shaped((feat, width), F32), shaped((feat, width), BF16)),
            (here, att, grad_hidden_b, over_rows(mix_send, near)),
            flops=width * width * part,
        )
        mix_got = over_rows(mix_send, far)
        out_got = over_cols(out_send, 1)
        ff_sum = ff_keep + ff_got.astype(F32)
        b1, b2, b3, ff_sum = together(b1, b2, b3, ff_sum)
        grad_ff = over_dp(ff_sum)

        grad_proj, qv_sum, s0, s1, s2, s3 = run(
            functools.partial(first_back_kernel, order, heads),
            (
                shaped((n_qkv, count), BF16), shaped((2 * head_rows, 1), F32),
                shaped((feat + 16, count), F32),
                shaped((feat + 16, count), BF16), shaped((feat + 16, count), BF16), shaped((feat + 16, count), BF16),
            ),
            (here, tok, stats, qkv, attended, totals, a0, b1, b2, b3, row, seg_col) + w_pieces + (grad_hidden, second),
            scratch=(pltpu.VMEM((head_rows, count), BF16), pltpu.VMEM((width, count), F32), pltpu.VMEM((width, 128), F32)),
            flops=2 * width * n_qkv * count,
        )
        got = all_over_cols((s1, s2, s3))

        grad_mix = over_dp(mix_keep + mix_got.astype(F32))
        last_ins = (here, normed_one, grad_proj)
        last_rows = (pltpu.VMEM((2 * feat, count), BF16),)
        (last_send,) = run(
            functools.partial(last_send_kernel, order), (shaped((2 * feat, n_qkv), BF16),), last_ins,
            scratch=last_rows, flops=width * count * n_qkv,
        )
        own, own_b, last_send = run(
            functools.partial(last_keep_kernel, order),
            (shaped((feat, n_qkv), F32), shaped((feat, n_qkv), BF16), shaped((feat, n_qkv), BF16)),
            last_ins + (over_rows(last_send, near),),
            scratch=last_rows,
            flops=width * count * n_qkv,
        )
        far_dp = [(d * n_rows + r, (d ^ 1) * n_rows + (r ^ far)) for d in range(n_dp) for r in range(n_rows)]
        got_y = over_rows(last_send, far)
        if n_dp > 1:
            got_x = lax.ppermute(own_b, "dp", pairs)
            got_xy = lax.ppermute(last_send, ("dp", ROWS), far_dp)
        else:
            got_x = got_xy = jnp.zeros_like(got_y)
        (grad_qkv,) = run(last_sum_kernel, (shaped((feat, n_qkv), F32),), (here, own, got_y, got_x, got_xy), final=True)
        for bit in bits_of(n_dp)[1:]:
            grad_qkv = grad_qkv + swap(grad_qkv.astype(BF16), "dp", n_dp, bit).astype(F32)

        (rest,) = run(rest_kernel, (shaped((8, width), F32),), (here, up_sum, qv_sum, cotangent, row), hold=False)
        grad_tokens, sums = run(
            token_sum_kernel, (shaped((feat, count), F32), shaped((8, width), F32)), (here, s0) + tuple(got) + (rest,)
        )
        steps = [(ROWS, n_rows, bit) for bit in bits_of(n_rows)] + [("dp", n_dp, bit) for bit in bits_of(n_dp)]
        for axis, size, bit in steps:
            sums_got = swap(sums, axis, size, bit)
            if (axis, size, bit) != steps[-1]:
                sums = sums + sums_got
        lengths = (feat, feat, feat, feat, feat, n_hid, 2 * head_rows, feat)
        sums = run(
            sums_out_kernel, tuple(shaped((1, length), F32) for length in lengths), (here, sums, sums_got),
            final=True,
        )
        sums = [value.reshape(-1) for value in sums]

        square_b = shaped((feat, feat), BF16)
        mix_own, p1, p2, p3 = run(
            mix_turn_kernel,
            (shaped((feat, feat), F32), square_b, square_b, square_b),
            (here, grad_mix),
            scratch=(pltpu.VMEM((width, feat), F32),),
        )
        got = all_over_cols((p1, p2, p3))
        (grad_mix,) = run(mix_sum_kernel, (shaped((feat, feat), F32),), (here, mix_own) + tuple(got), final=True)
        out_keep, out_send = halve(out_keep, out_got)
        (output,) = run(
            output_kernel, (shaped((feat, count), BF16),),
            (here, own_hidden, down_col, out_keep, over_cols(out_send, 2)),
            final=True,
        )
        return (
            output,
            grad_tokens,
            sums[3],
            sums[4],
            grad_qkv,
            sums[6],
            grad_mix,
            sums[2],
            sums[0],
            sums[1],
            grad_ff[:, n_hid:],
            sums[5],
            grad_ff[:, :n_hid],
            sums[7],
        )

    return body


def solution(mesh):
    sizes = mesh.shape
    body = make_body(sizes["dp"], sizes[ROWS], sizes[COLS])

    return jax.shard_map(
        body,
        mesh=mesh,
        in_specs=(
            P(COLS, ("dp", ROWS)),
            P(("dp", ROWS)),
            P(COLS),
            P(COLS),
            P(ROWS, COLS),
            P(COLS),
            P(COLS, ROWS),
            P(COLS),
            P(COLS),
            P(COLS),
            P(ROWS, COLS),
            P(COLS),
            P(ROWS, COLS),
            P(COLS),
            P(COLS, ("dp", ROWS)),
        ),
        out_specs=(
            P(COLS, ("dp", ROWS)),
            P(COLS, ("dp", ROWS)),
            P(COLS),
            P(COLS),
            P(ROWS, COLS),
            P(COLS),
            P(COLS, ROWS),
            P(COLS),
            P(COLS),
            P(COLS),
            P(ROWS, COLS),
            P(COLS),
            P(ROWS, COLS),
            P(COLS),
        ),
        check_vma=False,
    )
```
